32 devices in a mesh: seq: 8 (over z, y), head: 4 (over x, core).
Axes of the slice: x: 2, y: 2, z: 4, core: 2. Of those that a mesh axis runs over, the one named last changes fastest.
Arguments:
- inputs: bfloat16 [4, 4096, 768], P(None, 'seq'), may hold values from -6 to 6
- w_qkv: bfloat16 [3, 768, 768], P(None, None, 'head'), may hold values from -0.21875 to 0.21875
- b_qv: bfloat16 [2, 768], P(None, 'head'), may hold values from -4 to 4
- w_out: bfloat16 [768, 768], P('head'), may hold values from -1 to 1
- out_bias: bfloat16 [2, 768], replicated, may hold values from -4 to 4
- w_up: bfloat16 [768, 3072], P(None, 'head'), may hold values from -0.21875 to 0.21875
- b_up: bfloat16 [3072], P('head'), may hold values from -4 to 4
- w_down: bfloat16 [3072, 768], P('head'), may hold values from -0.109375 to 0.109375
- norm_gain: float32 [2, 768], replicated, may hold values from 0.5 to 1.5
- norm_shift: float32 [2, 768], replicated, may hold values from -3 to 3
- d_out: bfloat16 [4, 4096, 768], P(None, ('seq', 'head')), may hold values from -6 to 6
- q_perm: int32 [4, 12, 4096], P(None, 'head'), may hold values from 0 to 4095, as said below
- k_perm: int32 [4, 12, 4096], P(None, 'head'), may hold values from 0 to 4095, as said below
- masked: int32 [4, 1024], replicated, may hold values from 0 to 4095, as said below
Outputs:
- result: float32 [4, 4096, 768], P(None, ('seq', 'head'))
- d_inputs: float32 [4, 4096, 768], P(None, ('seq', 'head'))
- grad_qkv: float32 [3, 768, 768], P(None, 'seq', 'head')
- grad_bqv: float32 [2, 768], replicated
- grad_wout: float32 [768, 768], P('head', 'seq')
- grad_obias: float32 [2, 768], replicated
- grad_wup: float32 [768, 3072], P('seq', 'head')
- grad_bup: float32 [3072], replicated
- grad_wdown: float32 [3072, 768], P('head', 'seq')
- grad_gain: float32 [2, 768], replicated
- grad_shift: float32 [2, 768], replicated
- entropy: float32 [12, 128], P('head', 'seq')
- occupancy: int32 [12, 128], P('head', 'seq')
The draws below stay inside these ranges and needn't reach their ends.
Inputs may be any that keep to these rules, and one draw needn't show every extreme that they name: `q_perm`: for each sequence and head a permutation of the 4096 positions. Cut the positions into aligned blocks of 512 and the slots into aligned runs of 2048: one block puts between 171 and 341 of its positions into one run, and 341 is reached for every sequence and head. `k_perm`: same law as q_perm, drawn independently. `masked`: each row lists 1024 distinct positions in increasing order.
All inputs are finite; a program needn't handle non-finite values.
Results may differ from the reference program's by a relative error of at most 0.015.
Values may be sent and summed in bfloat16 or wider, within the bound.
No kernel may reach another device: no remote copies, remote signals or barrier semaphores. Data moves between devices by JAX's collectives and lax.ppermute only.
A program may use at most 192 MiB of HBM per device.

```python
import jax
import jax.numpy as jnp
from jax import lax

D = 768
HEADS = 12
DH = 64
FF = 3072
CLUSTER = 128
LENGTH = 4096
NSEQS = 4
BLOCK = 512
OWNERS = 2
SPREAD = 85
MASKED = 1024
CLUSTERS = 128


def one_order(seed_key):
    block_total = LENGTH // BLOCK
    pair_count = block_total // 2
    mean_rows = BLOCK // OWNERS
    sub_keys = jax.random.split(seed_key, 5)
    rotation = jax.random.randint(sub_keys[0], (pair_count,), 0, OWNERS)
    shifts = jax.random.randint(sub_keys[1], (pair_count,), 0, SPREAD + 1)
    chosen = jax.random.randint(sub_keys[2], (), 0, pair_count)
    shifts = jnp.where(jnp.arange(pair_count) == chosen, SPREAD, shifts)
    owner_ids = jnp.arange(OWNERS, dtype=jnp.int32)
    pattern = (owner_ids[None, :] == rotation[:, None]).astype(jnp.int32) - (owner_ids[None, :] == ((rotation + 1) % OWNERS)[:, None]).astype(jnp.int32)
    sign_pair = jnp.array([1, -1], dtype=jnp.int32)
    counts = mean_rows + sign_pair[None, :, None] * shifts[:, None, None] * pattern[:, None, :]
    bounds = jnp.cumsum(counts.reshape(block_total, OWNERS), 1)
    within = jax.vmap(lambda sub_key: jax.random.permutation(sub_key, BLOCK))(jax.random.split(sub_keys[3], block_total))
    owner_of = jnp.sum((within[:, :, None] >= bounds[:, None, :]).astype(jnp.int32), -1).reshape(LENGTH)
    ordering = jax.random.permutation(sub_keys[4], LENGTH)
    return jnp.argsort(owner_of * LENGTH + ordering).astype(jnp.int32)


def cluster_orders(seed_key):
    sub_keys = jax.random.split(seed_key, NSEQS * HEADS)
    return jax.vmap(one_order)(sub_keys).reshape(NSEQS, HEADS, LENGTH)


def draw_q_perm(key, part):
    return cluster_orders(jax.random.fold_in(key, 11))


def draw_k_perm(key, part):
    return cluster_orders(jax.random.fold_in(key, 23))


def draw_masked(key, part):
    sub_keys = jax.random.split(jax.random.fold_in(key, 37), 2)
    block_total = LENGTH // BLOCK
    levels = jax.random.randint(sub_keys[0], (block_total,), 0, 5)
    block_weight = jnp.left_shift(jnp.ones((block_total,), jnp.int32), levels)
    base_score = jax.random.randint(sub_keys[1], (NSEQS, LENGTH), 0, 4096)
    position_ids = jnp.arange(LENGTH, dtype=jnp.int32)[None, :]
    scores = base_score * jnp.repeat(block_weight, BLOCK)[None, :] * LENGTH + position_ids
    at_ends = (position_ids == 0) | (position_ids == LENGTH - 1)
    scores = jnp.where(at_ends, 1073741824 + position_ids, scores)
    chosen = lax.top_k(scores, MASKED)[1]
    return jnp.sort(chosen, -1).astype(jnp.int32)


def level_of(key, shape, shards, smallest, largest):
    factor_of = 1.0
    for dim, blocks in shards:
        heights = jax.random.uniform(jax.random.fold_in(jax.random.fold_in(key, 6), dim), (blocks,), jnp.float32, smallest / len(shards), largest / len(shards))
        factor_of = factor_of * jnp.repeat(jnp.exp(heights), shape[dim] // blocks).reshape((-1,) + (1,) * (len(shape) - 1 - dim))
    return factor_of


def scatter_about(own_key, dims, width, bound, shards=(), kind=jnp.bfloat16):
    values = jax.random.normal(own_key, dims, jnp.float32) * width
    if len(shards) > 0:
        values = level_of(own_key, dims, shards, -0.22, 0.18) * values
    return jnp.clip(values, min=-bound, max=bound).astype(kind)


def setup_inputs(seed: int = 0) -> dict:
    keys = jax.random.split(jax.random.key(seed), 15)
    return {
        "inputs": scatter_about(keys[0], (NSEQS, LENGTH, D), 1.0, 6.0, ((1, 8),)),
        "w_qkv": scatter_about(keys[1], (3, D, D), D ** -0.5, 0.21875, ((2, 4),)),
        "b_qv": scatter_about(keys[2], (2, D), 0.3, 4.0, ((1, 4),)),
        "w_out": scatter_about(keys[3], (D, D), (D // 24) ** -0.5, 1.0, ((0, 4),)),
        "out_bias": scatter_about(keys[4], (2, D), 0.3, 4.0),
        "w_up": scatter_about(keys[5], (D, FF), D ** -0.5, 0.21875, ((1, 4),)),
        "b_up": scatter_about(keys[6], (FF,), 0.3, 4.0, ((0, 4),)),
        "w_down": scatter_about(keys[7], (FF, D), FF ** -0.5, 0.109375, ((0, 4),)),
        "norm_gain": jnp.clip(1.0 + 0.1 * jax.random.normal(keys[8], (2, D), jnp.float32), 0.5, 1.5),
        "norm_shift": scatter_about(keys[9], (2, D), 0.2, 3.0, (), jnp.float32),
        "d_out": scatter_about(keys[10], (NSEQS, LENGTH, D), 1.0, 6.0, ((1, 32),)),
        "q_perm": draw_q_perm(jax.random.fold_in(keys[14], 71), 0),
        "k_perm": draw_k_perm(jax.random.fold_in(keys[14], 71), 0),
        "masked": draw_masked(jax.random.fold_in(keys[14], 71), 0),
    }


@jax.custom_vjp
def low(v):
    return lax.optimization_barrier(v.astype(jnp.bfloat16)).astype(jnp.float32)

@jax.custom_vjp
def low_back(v):
    return v

def low_keep(v):
    return (low(v), None)

def low_pass(kept, grad):
    return (grad,)

def back_keep(v):
    return (v, None)

def back_low(kept, grad):
    return (low(grad),)
low.defvjp(low_keep, low_pass)
low_back.defvjp(back_keep, back_low)
EPS = 1e-06
HIGH = lax.Precision.HIGHEST

def layer_norm(values, gain_row, shift_row):
    row_mean = lax.optimization_barrier(jnp.mean(values, -1, keepdims=True))
    centred = values - row_mean
    variance = lax.optimization_barrier(jnp.mean(centred * centred, -1, keepdims=True))
    return centred * lax.rsqrt(variance + EPS) * gain_row + shift_row

def invert(slot_order):
    slot_ids = jnp.broadcast_to(jnp.arange(slot_order.shape[1], dtype=jnp.int32), slot_order.shape)
    row_ids = jnp.arange(slot_order.shape[0], dtype=jnp.int32)[:, None]
    return jnp.zeros_like(slot_order).at[row_ids, slot_order].set(slot_ids)

def clustered(row_data, slot_order):
    head_major = row_data.reshape(LENGTH, HEADS, DH).transpose(1, 0, 2)
    picked = jnp.take_along_axis(head_major, slot_order[:, :, None], axis=1)
    return picked.reshape(HEADS, LENGTH // CLUSTER, CLUSTER, DH)

def one_sequence(params, tokens, q_order, k_order):
    w_qkv, b_qv, w_out, out_bias, w_up, b_up, w_down, norm_gain, norm_shift = params
    queries = low_back(low(jnp.dot(tokens, w_qkv[0], precision=HIGH) + b_qv[0]))
    keys_all = low_back(low(jnp.dot(tokens, w_qkv[1], precision=HIGH)))
    values_all = low_back(low(jnp.dot(tokens, w_qkv[2], precision=HIGH) + b_qv[1]))
    q_heads = clustered(queries, q_order)
    k_heads = clustered(keys_all, k_order)
    v_heads = clustered(values_all, k_order)
    raw_scores = low_back(jnp.einsum('hgqe,hgke->hgqk', q_heads, k_heads, precision=HIGH))
    scores = raw_scores * DH ** (-0.5)
    log_total = jax.nn.logsumexp(scores, -1)
    soft_weights = jnp.exp(scores - log_total[..., None])
    entropy = lax.optimization_barrier(jnp.mean(log_total - lax.optimization_barrier(jnp.sum(soft_weights * scores, -1)), -1))
    attended = low_back(low(jnp.einsum('hgqk,hgke->hgqe', low(soft_weights), v_heads, precision=HIGH)))
    attended = attended.reshape(HEADS, LENGTH, DH)
    restored = jnp.take_along_axis(attended, invert(q_order)[:, :, None], axis=1)
    merged = restored.transpose(1, 0, 2).reshape(LENGTH, HEADS * DH)
    attn_out = low_back(jnp.dot(merged, w_out, precision=HIGH))
    first_out = layer_norm(tokens + attn_out + out_bias[0], norm_gain[0], norm_shift[0])
    upper_in = low_back(jnp.dot(low(first_out), w_up, precision=HIGH)) + b_up
    hidden = low(jax.nn.gelu(upper_in, approximate=False))
    ffn_out = low_back(jnp.dot(hidden, w_down, precision=HIGH)) + out_bias[1]
    return (layer_norm(first_out + ffn_out, norm_gain[1], norm_shift[1]), entropy)

def reference(inputs, w_qkv, b_qv, w_out, out_bias, w_up, b_up, w_down, norm_gain, norm_shift, d_out, q_perm, k_perm, masked):
    params = tuple((array_in.astype(jnp.float32) for array_in in (w_qkv, b_qv, w_out, out_bias, w_up, b_up, w_down, norm_gain, norm_shift)))

    def forward(weights_all, tokens_all):

        def scan_step(carried, seq_item):
            tokens, q_order, k_order = seq_item
            layer_out, entropy = jax.checkpoint(one_sequence)(weights_all, tokens, q_order, k_order)
            return (carried, (layer_out, entropy))
        carried, (results, entropies) = lax.scan(scan_step, jnp.zeros((), jnp.float32), (tokens_all, q_perm, k_perm))
        return (results, entropies)
    outputs, pullback, entropies = jax.vjp(forward, params, inputs.astype(jnp.float32), has_aux=True)
    seq_ids = jnp.arange(NSEQS, dtype=jnp.int32)[:, None]
    mask_full = jnp.zeros((NSEQS, LENGTH), jnp.int32).at[seq_ids, masked].set(1)
    cotangent = d_out.astype(jnp.float32) * mask_full[..., None].astype(jnp.float32)
    gradients, d_inputs = pullback(cotangent)
    at_slots = jnp.take_along_axis(mask_full[:, None, :], q_perm, axis=2)
    occupancy = lax.optimization_barrier(jnp.sum(at_slots.reshape(NSEQS, HEADS, LENGTH // CLUSTER, CLUSTER), -1))
    occupancy = occupancy.transpose(1, 0, 2).reshape(HEADS, CLUSTERS).astype(jnp.int32)
    entropy_out = entropies.transpose(1, 0, 2).reshape(HEADS, CLUSTERS)
    return (outputs, d_inputs, gradients[0], gradients[1], gradients[2], gradients[3], gradients[4], gradients[5], gradients[6], gradients[7], gradients[8], entropy_out, occupancy)
```

```python
import functools

import jax
import jax.numpy as jnp
from jax import lax
from jax.experimental import pallas as pl
from jax.experimental.pallas import tpu as pltpu
from jax.sharding import Mesh
from jax.sharding import PartitionSpec as P

DH = 64
FF = 3072
CLUSTER = 128
LENGTH = 4096
TOK_DEV = 2048
OWN = LENGTH // TOK_DEV
EPS = 1e-06
PLANE = ("own", "hx", "hc")
HEAD = ("hx", "hc")
SEQ = ("sq", "own")
CHUNK = 512
STEPS = 3 * TOK_DEV // CHUNK
FULL_STEPS = 2 * TOK_DEV // CHUNK
GROUPS = CHUNK // CLUSTER
BF = jnp.bfloat16
F32 = jnp.float32
VMEM = 56 * 1024 * 1024


def nn(a, b):
    return lax.dot_general(a, b, (((1,), (0,)), ((), ())), preferred_element_type=F32)


def nt(a, b):
    return lax.dot_general(a, b, (((1,), (1,)), ((), ())), preferred_element_type=F32)


def tn(a, b):
    return lax.dot_general(a, b, (((0,), (0,)), ((), ())), preferred_element_type=F32)


def project_body(x_ref, w_ref, b_ref, tq_ref, tkv_ref):
    y = (nn(x_ref[...], w_ref[...]) + b_ref[...]).astype(BF)
    for t in range(2):
        for lo in range(4):
            tq_ref[t, :, lo * DH : (lo + 1) * DH] = y[
                lo * 128 : (lo + 1) * 128, t * DH : (t + 1) * DH
            ]
        for lo in range(2):
            tkv_ref[t, :, lo * 128 : (lo + 1) * 128] = y[
                lo * 256 : (lo + 1) * 256, (t + 1) * 128 : (t + 2) * 128
            ]


def project(x_all, w_sel, b_sel):
    blocks = x_all.shape[0] // 512
    width = x_all.shape[1]
    return pl.pallas_call(
        project_body,
        grid=(blocks,),
        in_specs=[
            pl.BlockSpec((512, width), lambda j: (j, 0)),
            pl.BlockSpec((width, 384), lambda j: (0, 0)),
            pl.BlockSpec((1, 384), lambda j: (0, 0)),
        ],
        out_specs=[
            pl.BlockSpec((2, 128, 256), lambda j: (0, j, 0)),
            pl.BlockSpec((2, 256, 256), lambda j: (0, j, 0)),
        ],
        out_shape=[
            jax.ShapeDtypeStruct((2, 1024, 256), BF),
            jax.ShapeDtypeStruct((2, 2048, 256), BF),
        ],
        compiler_params=pltpu.CompilerParams(vmem_limit_bytes=VMEM),
        name="project",
    )(x_all, w_sel, b_sel)


def hot_rows(col, count):
    return (lax.broadcasted_iota(jnp.int32, (col.shape[0], count), 1) == col).astype(BF)


def hot_cols(row, count):
    return (lax.broadcasted_iota(jnp.int32, (count, row.shape[1]), 0) == row).astype(BF)


def take_quarter(table, place):
    wide = nn(hot_rows(place & 1023, 1024), table)
    lane = lax.broadcasted_iota(jnp.int32, wide.shape, 1)
    wide = jnp.where((lane >> 6) == (place >> 10), wide, 0.0)
    half = wide[:, :128] + wide[:, 128:]
    return half + pltpu.roll(half, 64, 1)


def take_half(table, place):
    wide = nn(hot_rows(place & 2047, 2048), table)
    return jnp.where((place >> 11) == 1, wide[:, 128:], wide[:, :128])


def spread_quarter(twice, place):
    wide = jnp.concatenate([twice, twice], 1)
    lane = lax.broadcasted_iota(jnp.int32, wide.shape, 1)
    return jnp.where((lane >> 6) == (place >> 10), wide, 0.0).astype(BF)


def spread_half(rows, place):
    upper = (place >> 11) == 1
    return jnp.concatenate(
        [jnp.where(upper, 0.0, rows), jnp.where(upper, rows, 0.0)], 1
    ).astype(BF)


def low_lanes(shape):
    return lax.broadcasted_iota(jnp.int32, shape, 1) < DH


def attend_body(
    pq_ref, pk_ref, pqr_ref, tq_ref, tkv_ref, q_ref, kv_ref, lt_ref, ent_ref, out_ref, acc_ref
):
    step = pl.program_id(0)
    place_q = pq_ref[0]
    twice = take_quarter(tq_ref[0], place_q)
    q_all = jnp.where(low_lanes(twice.shape), twice, 0.0).astype(BF)
    kv_all = take_half(tkv_ref[0], pk_ref[0]).astype(BF)
    q_ref[0] = q_all
    kv_ref[0] = kv_all
    outs = []
    ents = []
    for c in range(GROUPS):
        rows = slice(c * CLUSTER, (c + 1) * CLUSTER)
        q = q_all[rows]
        kv = kv_all[rows]
        scores = nt(q, kv) * (DH**-0.5)
        top = jnp.max(scores, 1, keepdims=True)
        total = jnp.sum(jnp.exp(scores - top), 1, keepdims=True)
        log_total = top + jnp.log(total)
        soft = jnp.exp(scores - log_total)
        inner = jnp.sum(soft * scores, 1, keepdims=True)
        ents.append(
            jnp.broadcast_to(jnp.sum(log_total - inner, 0, keepdims=True) / CLUSTER, (1, 128))
        )
        lt_ref[0, rows, :] = log_total
        got = nn(soft.astype(BF), kv)
        outs.append(jnp.where(low_lanes(got.shape), pltpu.roll(got, 64, 1), got))
    ent_ref[0] = jnp.concatenate(ents + ents, 0)
    spread = spread_quarter(jnp.concatenate(outs, 0), place_q)
    part = nn(hot_cols(pqr_ref[0] & 1023, 1024), spread)
    first = (step == 0) | (step == FULL_STEPS)

    @pl.when(first)
    def _():
        acc_ref[...] = part

    @pl.when(jnp.logical_not(first))
    def _():
        acc_ref[...] += part

    out_ref[0] = acc_ref[...].astype(BF)


def table_of(g):
    return g // FULL_STEPS


def attend(pq_col, pk_col, pq_row, tq, tkv):
    chunk = lambda width: pl.BlockSpec((1, CHUNK, width), lambda g: (g, 0, 0))
    return pl.pallas_call(
        attend_body,
        grid=(STEPS,),
        in_specs=[
            chunk(1),
            chunk(1),
            pl.BlockSpec((1, 1, CHUNK), lambda g: (g, 0, 0)),
            pl.BlockSpec((1, 1024, 256), lambda g: (table_of(g), 0, 0)),
            pl.BlockSpec((1, 2048, 256), lambda g: (table_of(g), 0, 0)),
        ],
        out_specs=[
            chunk(128),
            chunk(128),
            chunk(1),
            pl.BlockSpec((1, 8, 128), lambda g: (g, 0, 0)),
            pl.BlockSpec((1, 1024, 256), lambda g: (table_of(g), 0, 0)),
        ],
        out_shape=[
            jax.ShapeDtypeStruct((STEPS, CHUNK, 128), BF),
            jax.ShapeDtypeStruct((STEPS, CHUNK, 128), BF),
            jax.ShapeDtypeStruct((STEPS, CHUNK, 1), F32),
            jax.ShapeDtypeStruct((STEPS, 8, 128), F32),
            jax.ShapeDtypeStruct((2, 1024, 256), BF),
        ],
        scratch_shapes=[pltpu.VMEM((1024, 256), F32)],
        compiler_params=pltpu.CompilerParams(vmem_limit_bytes=VMEM),
        name="attend",
    )(pq_col, pk_col, pq_row, tq, tkv)


def attend_back_body(
    pq_ref, pk_ref, pqr_ref, pkr_ref, td_ref, q_ref, kv_ref, lt_ref, dq_ref, dkv_ref, accq, acckv
):
    step = pl.program_id(0)
    place_q = pq_ref[0]
    twice = take_quarter(td_ref[0], place_q)
    d_all = jnp.where(low_lanes(twice.shape), 0.0, twice).astype(BF)
    gq = []
    gkv = []
    for c in range(GROUPS):
        rows = slice(c * CLUSTER, (c + 1) * CLUSTER)
        q = q_ref[0, rows, :]
        kv = kv_ref[0, rows, :]
        d = d_all[rows]
        scores = nt(q, kv) * (DH**-0.5)
        soft = jnp.exp(scores - lt_ref[0, rows, :])
        d_soft = nt(d, kv)
        d_scores = soft * (d_soft - jnp.sum(soft * d_soft, 1, keepdims=True))
        d_raw = (d_scores * (DH**-0.5)).astype(BF)
        got = nn(d_raw, kv)
        gq.append(jnp.where(low_lanes(got.shape), got, pltpu.roll(got, 64, 1)))
        gkv.append(tn(d_raw, q) + tn(soft.astype(BF), d))
    part_q = nn(
        hot_cols(pqr_ref[0] & 1023, 1024), spread_quarter(jnp.concatenate(gq, 0), place_q)
    )
    part_kv = nn(
        hot_cols(pkr_ref[0] & 2047, 2048), spread_half(jnp.concatenate(gkv, 0), pk_ref[0])
    )
    first = (step == 0) | (step == FULL_STEPS)

    @pl.when(first)
    def _():
        accq[...] = part_q
        acckv[...] = part_kv

    @pl.when(jnp.logical_not(first))
    def _():
        accq[...] += part_q
        acckv[...] += part_kv

    @pl.when((step == FULL_STEPS - 1) | (step == STEPS - 1))
    def _():
        dq_ref[0] = accq[...].astype(BF)
        dkv_ref[0] = acckv[...].astype(BF)


def attend_back(pq_col, pk_col, pq_row, pk_row, td, q_all, kv_all, log_total):
    chunk = lambda width: pl.BlockSpec((1, CHUNK, width), lambda g: (g, 0, 0))
    line = pl.BlockSpec((1, 1, CHUNK), lambda g: (g, 0, 0))
    return pl.pallas_call(
        attend_back_body,
        grid=(STEPS,),
        in_specs=[
            chunk(1),
            chunk(1),
            line,
            line,
            pl.BlockSpec((1, 1024, 256), lambda g: (table_of(g), 0, 0)),
            chunk(128),
            chunk(128),
            chunk(1),
        ],
        out_specs=[
            pl.BlockSpec((1, 1024, 256), lambda g: (table_of(g), 0, 0)),
            pl.BlockSpec((1, 2048, 256), lambda g: (table_of(g), 0, 0)),
        ],
        out_shape=[
            jax.ShapeDtypeStruct((2, 1024, 256), BF),
            jax.ShapeDtypeStruct((2, 2048, 256), BF),
        ],
        scratch_shapes=[pltpu.VMEM((1024, 256), F32), pltpu.VMEM((2048, 256), F32)],
        compiler_params=pltpu.CompilerParams(vmem_limit_bytes=VMEM),
        name="attend_back",
    )(pq_col, pk_col, pq_row, pk_row, td, q_all, kv_all, log_total)


def project_back_body(x_ref, dq_ref, dkv_ref, w_ref, dx_ref, grad_ref, sum_ref):
    j = pl.program_id(0)
    quarters = []
    for lo in range(4):
        cols = slice(lo * DH, (lo + 1) * DH)
        quarters.append(jnp.concatenate([dq_ref[0, :, cols], dq_ref[1, :, cols]], 1))
    parts = [jnp.concatenate(quarters, 0)]
    for t in range(2):
        parts.append(jnp.concatenate([dkv_ref[t, :, :128], dkv_ref[t, :, 128:]], 0))
    rows = jnp.concatenate(parts, 1)
    dx_ref[...] = nt(rows, w_ref[...]).astype(BF)
    part = tn(x_ref[...], rows)
    sums = jnp.sum(rows.astype(F32), 0, keepdims=True)

    @pl.when(j == 0)
    def _():
        grad_ref[...] = part
        sum_ref[...] = sums

    @pl.when(j > 0)
    def _():
        grad_ref[...] += part
        sum_ref[...] += sums


def project_back(x_all, dq, dkv, w_sel):
    tokens, width = x_all.shape
    return pl.pallas_call(
        project_back_body,
        grid=(tokens // 512,),
        in_specs=[
            pl.BlockSpec((512, width), lambda j: (j, 0)),
            pl.BlockSpec((2, 128, 256), lambda j: (0, j, 0)),
            pl.BlockSpec((2, 256, 256), lambda j: (0, j, 0)),
            pl.BlockSpec((width, 384), lambda j: (0, 0)),
        ],
        out_specs=[
            pl.BlockSpec((512, width), lambda j: (j, 0)),
            pl.BlockSpec((width, 384), lambda j: (0, 0)),
            pl.BlockSpec((1, 384), lambda j: (0, 0)),
        ],
        out_shape=[
            jax.ShapeDtypeStruct((tokens, width), BF),
            jax.ShapeDtypeStruct((width, 384), F32),
            jax.ShapeDtypeStruct((1, 384), F32),
        ],
        compiler_params=pltpu.CompilerParams(vmem_limit_bytes=VMEM),
        name="project_back",
    )(x_all, dq, dkv, w_sel)


def swap(x, axis, bit=1):
    size = lax.axis_size(axis)
    return lax.ppermute(x, axis, [(i, i ^ bit) for i in range(size)])


def sum_everywhere(x):
    for axis in ("hc", "hx", "own", "sq"):
        bit = 1
        while bit < lax.axis_size(axis):
            x = x + swap(x, axis, bit)
            bit *= 2
    return x


def pick(x, index):
    return lax.dynamic_index_in_dim(x, index, 0, keepdims=False)


def sum_over_head(parts):
    hx = lax.axis_index("hx")
    hc = lax.axis_index("hc")
    by_core = jnp.moveaxis(parts, 1, 0)
    kept = pick(by_core, hc).astype(F32) + swap(pick(by_core, 1 - hc), "hc").astype(F32)
    sent = swap(pick(kept, 1 - hx).astype(BF), "hx").astype(F32)
    return pick(kept, hx) + sent


def sum_over_seq(x):
    length = lax.axis_size("sq") * lax.axis_size("own")
    tiles = lax.all_to_all(
        x.reshape(length, x.shape[0] // length, x.shape[1]), SEQ, 0, 0, tiled=True
    )
    return jnp.sum(tiles.astype(F32), 0)


def layer_norm(values, gain_row, shift_row):
    row_mean = jnp.mean(values, -1, keepdims=True)
    centred = values - row_mean
    variance = jnp.mean(centred * centred, -1, keepdims=True)
    inv_std = lax.rsqrt(variance + EPS)
    normed = centred * inv_std
    return (normed * gain_row + shift_row, normed, inv_std)


def norm_back(grad_in, normed, inv_std, gain_row):
    scaled = grad_in * gain_row
    inner_term = (
        scaled
        - jnp.mean(scaled, -1, keepdims=True)
        - normed * jnp.mean(scaled * normed, -1, keepdims=True)
    )
    return inner_term * inv_std


def per_device(
    inputs,
    w_qkv,
    b_qv,
    w_out,
    out_bias,
    w_up,
    b_up,
    w_down,
    norm_gain,
    norm_shift,
    d_out,
    q_perm,
    k_perm,
    masked,
):
    seqs, block_len, width = inputs.shape
    heads = lax.axis_size("hx") * lax.axis_size("hc")
    plane = OWN * heads
    share = block_len // heads
    tokens = seqs * share
    sq = lax.axis_index("sq")
    own = lax.axis_index("own")
    head = lax.axis_index("hx") * lax.axis_size("hc") + lax.axis_index("hc")
    part = head_cols = q_perm.shape[1] * DH

    mine = lax.dynamic_slice_in_dim(inputs, head * share, share, 1)
    x_own = lax.all_to_all(mine, "sq", 0, 0, tiled=True).reshape(tokens, width)
    x_all = lax.all_gather(x_own, PLANE, axis=0, tiled=True)
    d_own = lax.all_to_all(d_out, "sq", 0, 0, tiled=True).reshape(tokens, width)

    up_all = lax.all_gather(w_up, HEAD, axis=0, tiled=False)
    down_all = lax.all_gather(w_down, HEAD, axis=0, tiled=False)
    out_all = lax.all_gather(w_out, HEAD, axis=0, tiled=True)
    bup_all = lax.all_gather(b_up, HEAD, axis=0, tiled=True).astype(F32)

    def places(perm):
        mine = pick(perm, sq)
        full = pick(mine, 2 * own).reshape(2, TOK_DEV)
        half = lax.dynamic_slice_in_dim(mine[1], own * TOK_DEV, TOK_DEV, 0)
        pos = jnp.concatenate([full, half[None]], 0)
        block = pos // block_len
        rest = pos % block_len
        device = (block % OWN) * heads + rest // share
        return device, (block // OWN) * share + rest % share

    dev_q, tok_q = places(q_perm)
    dev_k, tok_k = places(k_perm)
    place_q = (tok_q // 128) * 1024 + dev_q * 128 + tok_q % 128
    place_k = (tok_k // 256) * 2048 + dev_k * 256 + tok_k % 256
    pq_col = place_q.reshape(STEPS, CHUNK, 1)
    pk_col = place_k.reshape(STEPS, CHUNK, 1)
    pq_row = place_q.reshape(STEPS, 1, CHUNK)
    pk_row = place_k.reshape(STEPS, 1, CHUNK)

    def two_heads(x):
        full = lax.dynamic_slice_in_dim(x, own * 2 * DH, DH, x.ndim - 1)
        return full, x[..., DH : 2 * DH]

    w_full, w_half = two_heads(w_qkv)
    w_sel = jnp.concatenate(
        [w_full[0], w_half[0], w_full[1], w_full[2], w_half[1], w_half[2]], 1
    )
    b_full, b_half = two_heads(b_qv.astype(F32))
    none = jnp.zeros((DH,), F32)
    b_sel = jnp.concatenate([b_full[0], b_half[0], none, b_full[1], none, b_half[1]])[None]
    tq, tkv = project(x_all, w_sel, b_sel)
    q_all, kv_all, log_total, ent, attended = attend(pq_col, pk_col, pq_row, tq, tkv)

    got = lax.all_to_all(
        attended.reshape(2, plane, 128, 256), PLANE, 1, 1, tiled=True
    ).reshape(2, OWN, heads, 128, 4, DH)
    shared = (got[1, 0].astype(F32) + got[1, 1].astype(F32)).astype(BF)
    head_rows = jnp.stack([got[0, 0], shared, got[0, 1]], 1)
    head_rows = head_rows.transpose(3, 2, 0, 1, 4).reshape(tokens, heads * head_cols)

    bias_out = out_bias.astype(F32)
    attn = jnp.dot(head_rows, out_all, preferred_element_type=F32)
    first_out, normed_one, inv_one = layer_norm(
        x_own.astype(F32) + attn + bias_out[0], norm_gain[0], norm_shift[0]
    )
    first_low = first_out.astype(BF)
    upper = jnp.einsum("td,hdf->thf", first_low, up_all, preferred_element_type=F32)
    upper = upper + bup_all.reshape(heads, -1)
    gelu_out, gelu_back = jax.vjp(lambda val: jax.nn.gelu(val, approximate=False), upper)
    hidden = gelu_out.astype(BF)
    ffn = jnp.einsum("thf,hfd->td", hidden, down_all, preferred_element_type=F32)
    result_own, normed_two, inv_two = layer_norm(
        first_out + ffn + bias_out[1], norm_gain[1], norm_shift[1]
    )
    result = lax.all_to_all(
        result_own.astype(BF).reshape(seqs, share, width), "sq", 0, 0, tiled=True
    ).astype(F32)

    masked_row = pick(masked, sq)
    own_pos = (
        (jnp.arange(seqs, dtype=jnp.int32) * OWN + own)[:, None] * block_len
        + head * share
        + jnp.arange(share, dtype=jnp.int32)
    ).reshape(tokens)
    mask_own = jnp.any(masked_row[:, None] == own_pos[None, :], 0).astype(F32)
    seed_grad = d_own.astype(F32) * mask_own[:, None]
    gain_two = jnp.sum(seed_grad * normed_two, 0)
    shift_two = jnp.sum(seed_grad, 0)
    d_second = norm_back(seed_grad, normed_two, inv_two, norm_gain[1])
    bias_two = jnp.sum(d_second, 0)
    d_low2 = d_second.astype(BF)
    d_hidden = jnp.einsum("td,hfd->thf", d_low2, down_all, preferred_element_type=F32)
    d_upper = gelu_back(d_hidden)[0]
    grad_bup = jnp.sum(d_upper, 0).reshape(-1)
    d_upper_low = d_upper.astype(BF)
    d_first = d_second + jnp.einsum(
        "thf,hdf->td", d_upper_low, up_all, preferred_element_type=F32
    )
    gain_one = jnp.sum(d_first * normed_one, 0)
    shift_one = jnp.sum(d_first, 0)
    d_first_in = norm_back(d_first, normed_one, inv_one, norm_gain[0])
    bias_one = jnp.sum(d_first_in, 0)
    d_attn = d_first_in.astype(BF)
    d_heads = jnp.einsum("td,cd->tc", d_attn, out_all, preferred_element_type=F32).astype(BF)
    d_heads = d_heads.reshape(4, 128, heads, 3, DH).transpose(3, 2, 1, 0, 4)
    d_heads = d_heads.reshape(3, heads, 128, 256)
    d_send = jnp.stack([d_heads[0], d_heads[2], d_heads[1], d_heads[1]], 0)
    td = lax.all_to_all(
        d_send.reshape(2, plane, 128, 256), PLANE, 1, 1, tiled=True
    ).reshape(2, plane * 128, 256)
    dq, dkv = attend_back(pq_col, pk_col, pq_row, pk_row, td, q_all, kv_all, log_total)
    dx, grad_sel, sum_sel = project_back(x_all, dq, dkv, w_sel)
    dx_own = lax.psum_scatter(dx, PLANE, scatter_dimension=0, tiled=True)
    d_in_own = d_first_in + dx_own.astype(F32)
    d_inputs = lax.all_to_all(
        d_in_own.astype(BF).reshape(seqs, share, width), "sq", 0, 0, tiled=True
    ).astype(F32)

    split = (lax.axis_size("hx"), lax.axis_size("hc"))
    down_part = jnp.einsum("td,thf->hdf", d_low2, hidden, preferred_element_type=F32).astype(BF)
    up_part = jnp.einsum("td,thf->hdf", first_low, d_upper_low, preferred_element_type=F32).astype(BF)
    out_part = jnp.einsum(
        "td,thc->hdc", d_attn, head_rows.reshape(tokens, heads, head_cols), preferred_element_type=F32
    ).astype(BF)
    down_sum, up_sum, out_sum = (
        sum_over_seq(sum_over_head(p.reshape(*split, *p.shape[1:])).astype(BF))
        for p in (down_part, up_part, out_part)
    )
    length = lax.axis_size("sq") * OWN
    qkv_tiles = lax.all_to_all(
        grad_sel.astype(BF).reshape(length, width // length, 384), SEQ, 0, 0, tiled=True
    ).reshape(length // OWN, OWN, width // length, 6, DH)
    qkv_own = jnp.sum(qkv_tiles.astype(F32), 0)

    def three_heads(full, half):
        return jnp.stack([qkv_own[0, :, full], qkv_own[0, :, half] + qkv_own[1, :, half], qkv_own[1, :, full]], 1)

    qkv_sum = jnp.stack([three_heads(0, 1), three_heads(2, 4), three_heads(3, 5)], 0)
    qkv_sum = qkv_sum.reshape(3, width // length, head_cols)

    small = sum_everywhere(
        jnp.concatenate([bias_one, bias_two, gain_one, gain_two, shift_one, shift_two, grad_bup])
    )
    obias_sum = small[: 2 * width].reshape(2, width)
    gain_sum = small[2 * width : 4 * width].reshape(2, width)
    shift_sum = small[4 * width : 6 * width].reshape(2, width)
    bup_sum = small[6 * width :]
    sums = sum_sel.reshape(6, DH)
    bqv = jnp.zeros((2, heads, 3, DH), F32)
    at_full = (jnp.arange(3) == 2 * own)[:, None]
    at_half = (jnp.arange(3) == 1)[:, None]
    at_head = (jnp.arange(heads) == head)[None, :, None, None]
    pair = jnp.stack(
        [jnp.where(at_full, sums[a], 0.0) + jnp.where(at_half, sums[b], 0.0) for a, b in ((0, 1), (3, 5))]
    )
    bqv = jnp.where(at_head, pair[:, None], 0.0).reshape(2, width)
    bqv_sum = sum_everywhere(bqv)

    ent_seg = ent[:, :GROUPS, 0].reshape(3, TOK_DEV // CLUSTER)
    ent_got = swap(jnp.where(own == 0, ent_seg[1], ent_seg[0]), "own")
    entropy = jnp.stack(
        [
            jnp.where(own == 0, ent_seg[0], ent_got),
            ent_seg[2],
            jnp.where(own == 0, ent_got, ent_seg[1]),
        ]
    )
    slots = lax.dynamic_slice_in_dim(pick(q_perm, sq), own * TOK_DEV, TOK_DEV, 1)
    slot_masked = jnp.any(slots[..., None] == masked_row[None, None, :], -1).astype(jnp.int32)
    occupancy = jnp.sum(slot_masked.reshape(slots.shape[0], TOK_DEV // CLUSTER, CLUSTER), -1)
    return (
        result,
        d_inputs,
        qkv_sum,
        bqv_sum,
        out_sum.T,
        obias_sum,
        up_sum,
        bup_sum,
        down_sum.T,
        gain_sum,
        shift_sum,
        entropy,
        occupancy,
    )


def solution(mesh):
    seq, head = (mesh.shape["seq"], mesh.shape["head"])
    fine = Mesh(
        mesh.devices.reshape(seq // OWN, OWN, 2, head // 2), ("sq", "own", "hx", "hc")
    )
    both = SEQ + HEAD
    placed = (
        P(None, SEQ, None),
        P(None, None, HEAD),
        P(None, HEAD),
        P(HEAD, None),
        P(),
        P(None, HEAD),
        P(HEAD),
        P(HEAD, None),
        P(),
        P(),
        P(None, both, None),
        P(None, HEAD, None),
        P(None, HEAD, None),
        P(),
    )
    return jax.shard_map(
        per_device,
        mesh=fine,
        in_specs=placed,
        out_specs=(
            P(None, both, None),
            P(None, both, None),
            P(None, SEQ, HEAD),
            P(),
            P(HEAD, SEQ),
            P(),
            P(SEQ, HEAD),
            P(),
            P(HEAD, SEQ),
            P(),
            P(),
            P(HEAD, SEQ),
            P(HEAD, SEQ),
        ),
        check_vma=False,
    )
```

```python
import functools

import jax
import jax.numpy as jnp
from jax import lax
from jax.experimental import pallas as pl
from jax.experimental.pallas import tpu as pltpu
from jax.sharding import Mesh
from jax.sharding import PartitionSpec as P

DH = 64
FF = 3072
CLUSTER = 128
LENGTH = 4096
TOK_DEV = 2048
OWN = LENGTH // TOK_DEV
EPS = 1e-06
PLANE = ("own", "hx", "hc")
HEAD = ("hx", "hc")
SEQ = ("sq", "own")
CHUNK = 512
GROUPS = CHUNK // CLUSTER
BF = jnp.bfloat16
F32 = jnp.float32
VMEM = 56 * 1024 * 1024
SIDE = 128


def cost(micros):
    return pl.CostEstimate(flops=micros * 10**9, transcendentals=0, bytes_accessed=micros * 10**6)


def nn(a, b):
    return lax.dot_general(a, b, (((1,), (0,)), ((), ())), preferred_element_type=F32)


def nt(a, b):
    return lax.dot_general(a, b, (((1,), (1,)), ((), ())), preferred_element_type=F32)


def tn(a, b):
    return lax.dot_general(a, b, (((0,), (0,)), ((), ())), preferred_element_type=F32)


def log2(n):
    return n.bit_length() - 1


def prepare_body(
    block_len, heads, here_ref, q_ref, k_ref, masked_ref, pq_ref, pk_ref, pqr_ref, pkr_ref, mask_ref
):
    share = block_len // heads

    def place(pos, size):
        block = pos >> log2(block_len)
        rest = pos & (block_len - 1)
        device = (block & (OWN - 1)) * heads + (rest >> log2(share))
        token = (block >> log2(OWN)) * share + (rest & (share - 1))
        return ((token >> log2(size)) << log2(size * OWN * heads)) + device * size + (token & (size - 1))

    for pos_ref, col_ref, row_ref, size in (
        (q_ref, pq_ref, pqr_ref, 128),
        (k_ref, pk_ref, pkr_ref, 256),
    ):
        for c in range(pos_ref.shape[0]):
            row = place(pos_ref[c], size)
            row_ref[c] = row
            col_ref[c] = jnp.broadcast_to(row, (8, CHUNK)).T[:, :1]
    token = lax.broadcasted_iota(jnp.int32, mask_ref.shape, 0)
    own_pos = (
        (((token >> log2(share)) * OWN + here_ref[0]) << log2(block_len))
        + here_ref[1] * share
        + (token & (share - 1))
    )
    mask_ref[...] = jnp.max((own_pos == masked_ref[...]).astype(F32), 1, keepdims=True)


def prepare(block_len, heads, here, q_pos, k_pos, masked_row, tokens):
    steps = q_pos.shape[0]
    vmem = pl.BlockSpec(memory_space=pltpu.VMEM)
    col = jax.ShapeDtypeStruct((steps, CHUNK, 1), jnp.int32)
    row = jax.ShapeDtypeStruct((steps, 1, CHUNK), jnp.int32)
    return pl.pallas_call(
        functools.partial(prepare_body, block_len, heads),
        in_specs=[pl.BlockSpec(memory_space=pltpu.SMEM), vmem, vmem, vmem],
        out_specs=[vmem] * 5,
        out_shape=[col, col, row, row, jax.ShapeDtypeStruct((tokens, 1), F32)],
        compiler_params=pltpu.CompilerParams(vmem_limit_bytes=VMEM),
        name="prepare",
        cost_estimate=cost(1),
    )(here, q_pos, k_pos, masked_row)


def project_body(x_ref, w_ref, b_ref, tq0_ref, tq1_ref, tkv0_ref, tkv1_ref):
    y = (nn(x_ref[...], w_ref[...]) + b_ref[...]).astype(BF)
    for t, (tq_ref, tkv_ref) in enumerate(((tq0_ref, tkv0_ref), (tq1_ref, tkv1_ref))):
        for lo in range(4):
            tq_ref[:, lo * DH : (lo + 1) * DH] = y[
                lo * 128 : (lo + 1) * 128, t * DH : (t + 1) * DH
            ]
        for lo in range(2):
            tkv_ref[:, lo * 128 : (lo + 1) * 128] = y[
                lo * 256 : (lo + 1) * 256, (t + 1) * 128 : (t + 2) * 128
            ]


def project(x_all, w_sel, b_sel):
    blocks = x_all.shape[0] // 512
    width = x_all.shape[1]
    quarter = pl.BlockSpec((128, 256), lambda j: (j, 0))
    half = pl.BlockSpec((256, 256), lambda j: (j, 0))
    quarter_shape = jax.ShapeDtypeStruct((1024, 256), BF)
    half_shape = jax.ShapeDtypeStruct((2048, 256), BF)
    return pl.pallas_call(
        project_body,
        grid=(blocks,),
        in_specs=[
            pl.BlockSpec((512, width), lambda j: (j, 0)),
            pl.BlockSpec((width, 384), lambda j: (0, 0)),
            pl.BlockSpec((1, 384), lambda j: (0, 0)),
        ],
        out_specs=[quarter, quarter, half, half],
        out_shape=[quarter_shape, quarter_shape, half_shape, half_shape],
        compiler_params=pltpu.CompilerParams(vmem_limit_bytes=VMEM),
        name="project",
        cost_estimate=cost(1),
    )(x_all, w_sel, b_sel)


def hot_rows(col, count):
    return (lax.broadcasted_iota(jnp.int32, (col.shape[0], count), 1) == col).astype(BF)


def hot_cols(row, count):
    return (lax.broadcasted_iota(jnp.int32, (count, row.shape[1]), 0) == row).astype(BF)


def take_quarter(table, place):
    wide = nn(hot_rows(place & 1023, 1024), table)
    lane = lax.broadcasted_iota(jnp.int32, wide.shape, 1)
    wide = jnp.where((lane >> 6) == (place >> 10), wide, 0.0)
    half = wide[:, :128] + wide[:, 128:]
    return half + pltpu.roll(half, 64, 1)


def take_half(table, place):
    wide = nn(hot_rows(place & 2047, 2048), table)
    return jnp.where((place >> 11) == 1, wide[:, 128:], wide[:, :128])


def spread_quarter(twice, place):
    wide = jnp.concatenate([twice, twice], 1)
    lane = lax.broadcasted_iota(jnp.int32, wide.shape, 1)
    return jnp.where((lane >> 6) == (place >> 10), wide, 0.0).astype(BF)


def spread_half(rows, place):
    upper = (place >> 11) == 1
    return jnp.concatenate(
        [jnp.where(upper, 0.0, rows), jnp.where(upper, rows, 0.0)], 1
    ).astype(BF)


def low_lanes(shape):
    return lax.broadcasted_iota(jnp.int32, shape, 1) < DH


def attend_body(
    pq_ref, pk_ref, pqr_ref, tq_ref, tkv_ref, q_ref, kv_ref, lt_ref, ent_ref, out_ref, acc_ref
):
    step = pl.program_id(0)
    place_q = pq_ref[0]
    twice = take_quarter(tq_ref[...], place_q)
    q_all = jnp.where(low_lanes(twice.shape), twice, 0.0).astype(BF)
    kv_all = take_half(tkv_ref[...], pk_ref[0]).astype(BF)
    q_ref[0] = q_all
    kv_ref[0] = kv_all
    outs = []
    ents = []
    for c in range(GROUPS):
        rows = slice(c * CLUSTER, (c + 1) * CLUSTER)
        q = q_all[rows]
        kv = kv_all[rows]
        scores = nt(q, kv) * (DH**-0.5)
        top = jnp.max(scores, 1, keepdims=True)
        total = jnp.sum(jnp.exp(scores - top), 1, keepdims=True)
        log_total = top + jnp.log(total)
        soft = jnp.exp(scores - log_total)
        inner = jnp.sum(soft * scores, 1, keepdims=True)
        ents.append(
            jnp.broadcast_to(jnp.sum(log_total - inner, 0, keepdims=True) / CLUSTER, (1, 128))
        )
        lt_ref[0, rows, :] = log_total
        got = nn(soft.astype(BF), kv)
        outs.append(jnp.where(low_lanes(got.shape), pltpu.roll(got, 64, 1), got))
    ent_ref[0] = jnp.concatenate(ents + ents, 0)
    spread = spread_quarter(jnp.concatenate(outs, 0), place_q)
    part = nn(hot_cols(pqr_ref[0] & 1023, 1024), spread)

    @pl.when(step == 0)
    def _():
        acc_ref[...] = part

    @pl.when(step > 0)
    def _():
        acc_ref[...] += part

    @pl.when(step == pl.num_programs(0) - 1)
    def _():
        for j in range(out_ref.shape[0]):
            out_ref[j] = acc_ref[j * 128 : (j + 1) * 128, :].astype(BF)


def once(*shape):
    return pl.BlockSpec(shape, lambda g: (0,) * len(shape))


def attend(places, start, steps, tq, tkv):
    pq_col, pk_col, pq_row, _ = places
    chunk = lambda width: pl.BlockSpec((1, CHUNK, width), lambda g: (g, 0, 0))
    col = pl.BlockSpec((1, CHUNK, 1), lambda g: (g + start, 0, 0))
    return pl.pallas_call(
        attend_body,
        grid=(steps,),
        in_specs=[
            col,
            col,
            pl.BlockSpec((1, 1, CHUNK), lambda g: (g + start, 0, 0)),
            once(1024, 256),
            once(2048, 256),
        ],
        out_specs=[
            chunk(128),
            chunk(128),
            chunk(1),
            pl.BlockSpec((1, 8, 128), lambda g: (g, 0, 0)),
            once(8, 128, 256),
        ],
        out_shape=[
            jax.ShapeDtypeStruct((steps, CHUNK, 128), BF),
            jax.ShapeDtypeStruct((steps, CHUNK, 128), BF),
            jax.ShapeDtypeStruct((steps, CHUNK, 1), F32),
            jax.ShapeDtypeStruct((steps, 8, 128), F32),
            jax.ShapeDtypeStruct((8, 128, 256), BF),
        ],
        scratch_shapes=[pltpu.VMEM((1024, 256), F32)],
        compiler_params=pltpu.CompilerParams(vmem_limit_bytes=VMEM),
        name="attend",
        cost_estimate=cost(1),
    )(pq_col, pk_col, pq_row, tq, tkv)


def attend_back_body(
    pq_ref, pk_ref, pqr_ref, pkr_ref, td_ref, q_ref, kv_ref, lt_ref, out_ref, accq, acckv
):
    step = pl.program_id(0)
    place_q = pq_ref[0]
    twice = take_quarter(td_ref[...], place_q)
    d_all = jnp.where(low_lanes(twice.shape), 0.0, twice).astype(BF)
    gq = []
    gkv = []
    for c in range(GROUPS):
        rows = slice(c * CLUSTER, (c + 1) * CLUSTER)
        q = q_ref[0, rows, :]
        kv = kv_ref[0, rows, :]
        d = d_all[rows]
        scores = nt(q, kv) * (DH**-0.5)
        soft = jnp.exp(scores - lt_ref[0, rows, :])
        d_soft = nt(d, kv)
        d_scores = soft * (d_soft - jnp.sum(soft * d_soft, 1, keepdims=True))
        d_raw = (d_scores * (DH**-0.5)).astype(BF)
        got = nn(d_raw, kv)
        gq.append(jnp.where(low_lanes(got.shape), got, pltpu.roll(got, 64, 1)))
        gkv.append(tn(d_raw, q) + tn(soft.astype(BF), d))
    part_q = nn(
        hot_cols(pqr_ref[0] & 1023, 1024), spread_quarter(jnp.concatenate(gq, 0), place_q)
    )
    part_kv = nn(
        hot_cols(pkr_ref[0] & 2047, 2048), spread_half(jnp.concatenate(gkv, 0), pk_ref[0])
    )

    @pl.when(step == 0)
    def _():
        accq[...] = part_q
        acckv[...] = part_kv

    @pl.when(step > 0)
    def _():
        accq[...] += part_q
        acckv[...] += part_kv

    @pl.when(step == pl.num_programs(0) - 1)
    def _():
        for j in range(out_ref.shape[0]):
            out_ref[j, :128, :] = accq[j * 128 : (j + 1) * 128, :].astype(BF)
            out_ref[j, 128:, :] = acckv[j * 256 : (j + 1) * 256, :].astype(BF)


def attend_back(places, start, td, q_all, kv_all, log_total):
    pq_col, pk_col, pq_row, pk_row = places
    steps = q_all.shape[0]
    chunk = lambda width: pl.BlockSpec((1, CHUNK, width), lambda g: (g, 0, 0))
    col = pl.BlockSpec((1, CHUNK, 1), lambda g: (g + start, 0, 0))
    line = pl.BlockSpec((1, 1, CHUNK), lambda g: (g + start, 0, 0))
    return pl.pallas_call(
        attend_back_body,
        grid=(steps,),
        in_specs=[
            col,
            col,
            line,
            line,
            once(1024, 256),
            chunk(128),
            chunk(128),
            chunk(1),
        ],
        out_specs=once(8, 384, 256),
        out_shape=jax.ShapeDtypeStruct((8, 384, 256), BF),
        scratch_shapes=[pltpu.VMEM((1024, 256), F32), pltpu.VMEM((2048, 256), F32)],
        compiler_params=pltpu.CompilerParams(vmem_limit_bytes=VMEM),
        name="attend_back",
        cost_estimate=cost(1),
    )(pq_col, pk_col, pq_row, pk_row, td, q_all, kv_all, log_total)


def project_grad_body(x_ref, full_ref, half_ref, grad_ref, sum_ref, acc_ref):
    j = pl.program_id(0)
    quarters = []
    for lo in range(4):
        cols = slice(lo * DH, (lo + 1) * DH)
        quarters.append(jnp.concatenate([full_ref[0, :128, cols], half_ref[0, :128, cols]], 1))
    parts = [jnp.concatenate(quarters, 0)]
    for ref in (full_ref, half_ref):
        parts.append(jnp.concatenate([ref[0, 128:, :128], ref[0, 128:, 128:]], 0))
    rows = jnp.concatenate(parts, 1)
    part = tn(x_ref[...], rows)
    sums = jnp.sum(rows.astype(F32), 0, keepdims=True)

    @pl.when(j == 0)
    def _():
        acc_ref[...] = part
        sum_ref[...] = sums

    @pl.when(j > 0)
    def _():
        acc_ref[...] += part
        sum_ref[...] += sums

    @pl.when(j == pl.num_programs(0) - 1)
    def _():
        grad_ref[...] = acc_ref[...].astype(BF)


def project_grad(x_all, full, half):
    tokens, width = x_all.shape
    rows = pl.BlockSpec((1, 384, 256), lambda j: (j, 0, 0))
    return pl.pallas_call(
        project_grad_body,
        grid=(tokens // 512,),
        in_specs=[pl.BlockSpec((512, width), lambda j: (j, 0)), rows, rows],
        out_specs=[once(width, 384), once(1, 384)],
        out_shape=[
            jax.ShapeDtypeStruct((width, 384), BF),
            jax.ShapeDtypeStruct((1, 384), F32),
        ],
        scratch_shapes=[pltpu.VMEM((width, 384), F32)],
        compiler_params=pltpu.CompilerParams(vmem_limit_bytes=VMEM),
        name="project_grad",
        cost_estimate=cost(1),
    )(x_all, full, half)


def project_back_body(heads, full_ref, half_ref, w_ref, dfi_ref, dx_ref, q_ref, kv_ref):
    for hd in range(heads):
        for h in range(3):
            if h == 1:
                piece = (half_ref[hd].astype(F32) + half_ref[heads + hd].astype(F32)).astype(BF)
            else:
                piece = full_ref[(h // 2) * heads + hd]
            n = hd * 3 + h
            for lo in range(4):
                q_ref[lo * 128 : (lo + 1) * 128, hd * 256 + h * DH : hd * 256 + (h + 1) * DH] = piece[
                    :128, lo * DH : (lo + 1) * DH
                ]
            for lo in range(2):
                kv_ref[lo * 256 : (lo + 1) * 256, n * 128 : (n + 1) * 128] = piece[
                    128:, lo * 128 : (lo + 1) * 128
                ]
    for i in range(4):
        r = slice(i * 128, (i + 1) * 128)
        dx = dfi_ref[r, :]
        for hd in range(heads):
            dx += nn(q_ref[r, hd * 256 : hd * 256 + 3 * DH], w_ref[hd, : 3 * DH, :])
            dx += nn(kv_ref[r, hd * 384 : (hd + 1) * 384], w_ref[hd, 3 * DH :, :])
        dx_ref[r, :] = dx.astype(BF)


def project_back(full, half, w_all, d_first_in):
    tokens, width = d_first_in.shape
    heads = w_all.shape[0]
    return pl.pallas_call(
        functools.partial(project_back_body, heads),
        out_shape=jax.ShapeDtypeStruct((tokens, width), BF),
        scratch_shapes=[
            pltpu.VMEM((tokens, heads * 256), BF),
            pltpu.VMEM((tokens, heads * 384), BF),
        ],
        compiler_params=pltpu.CompilerParams(vmem_limit_bytes=VMEM),
        name="project_back",
        cost_estimate=cost(1),
    )(full, half, w_all, d_first_in)


def erf_parts(u):
    mag = jnp.abs(u) * (0.5**0.5)
    bell = jnp.exp(-(mag * mag))
    t = 1.0 / (1.0 + 0.3275911 * mag)
    poly = t * (
        0.254829592
        + t * (-0.284496736 + t * (1.421413741 + t * (-1.453152027 + t * 1.061405429)))
    )
    tail = 0.5 * poly * bell
    return jnp.where(u < 0, tail, 1.0 - tail), bell * ((2 * jnp.pi) ** -0.5)


def row_mean(x):
    return jnp.mean(x, 1, keepdims=True)


def column_sum(x):
    return jnp.sum(x, 0, keepdims=True)


def middle_body(
    heads,
    hc_ref,
    full_ref,
    half_ref,
    x_ref,
    dout_ref,
    mask_ref,
    wo_ref,
    up_ref,
    bup_ref,
    down_ref,
    bias_ref,
    gain_ref,
    shift_ref,
    res_ref,
    send_full_ref,
    send_half_ref,
    dfi_ref,
    down_sent_ref,
    down_kept_ref,
    up_sent_ref,
    up_kept_ref,
    sums_ref,
    gbup_ref,
    rows_ref,
    first_ref,
    n1_ref,
    inv1_ref,
    low_ref,
    acc_ref,
    hid_ref,
    slope_ref,
    dlow_ref,
):
    step = pl.program_id(0)
    tiles = 4
    tokens = x_ref.shape[0]
    size = tokens // tiles

    @pl.when(step == 0)
    def _():
        for hd in range(heads):
            for h in range(3):
                if h == 1:
                    piece = (half_ref[hd].astype(F32) + half_ref[heads + hd].astype(F32)).astype(BF)
                else:
                    piece = full_ref[hd + (h // 2) * heads]
                col = (hd * 3 + h) * DH
                for lo in range(4):
                    rows_ref[lo * 128 : (lo + 1) * 128, col : col + DH] = piece[
                        :, lo * DH : (lo + 1) * DH
                    ]
        for i in range(tiles):
            r = slice(i * size, (i + 1) * size)
            v = x_ref[r, :].astype(F32) + nn(rows_ref[r, :], wo_ref[...]) + bias_ref[0:1, :]
            centred = v - row_mean(v)
            inv = lax.rsqrt(row_mean(centred * centred) + EPS)
            normed = centred * inv
            first = normed * gain_ref[0:1, :] + shift_ref[0:1, :]
            n1_ref[r, :] = normed
            inv1_ref[r, :] = inv
            first_ref[r, :] = first
            low_ref[r, :] = first.astype(BF)
            acc_ref[r, :] = first + bias_ref[1:2, :]

    @pl.when(step < heads)
    def _():
        for i in range(tiles):
            r = slice(i * size, (i + 1) * size)
            u = nn(low_ref[r, :], up_ref[0]) + bup_ref[0]
            phi, bell = erf_parts(u)
            hid = (u * phi).astype(BF)
            hid_ref[step, r, :] = hid
            slope_ref[step, r, :] = phi + u * bell
            acc_ref[r, :] += nn(hid, down_ref[0])

    @pl.when(step == heads)
    def _():
        zero = jnp.zeros((1, x_ref.shape[1]), F32)
        g_sum, s_sum, b_sum = zero, zero, zero
        for i in range(tiles):
            r = slice(i * size, (i + 1) * size)
            v = acc_ref[r, :]
            centred = v - row_mean(v)
            inv = lax.rsqrt(row_mean(centred * centred) + EPS)
            normed = centred * inv
            res_ref[r, :] = (normed * gain_ref[1:2, :] + shift_ref[1:2, :]).astype(BF)
            seed = dout_ref[r, :].astype(F32) * mask_ref[r, :]
            g_sum += column_sum(seed * normed)
            s_sum += column_sum(seed)
            e = seed * gain_ref[1:2, :]
            d = inv * (e - row_mean(e) - normed * row_mean(e * normed))
            b_sum += column_sum(d)
            acc_ref[r, :] = d
            dlow_ref[r, :] = d.astype(BF)
        sums_ref[1:2, :] = b_sum
        sums_ref[3:4, :] = g_sum
        sums_ref[5:6, :] = s_sum

    @pl.when(step >= heads)
    def _():
        c = step - heads
        total = jnp.zeros((1, up_ref.shape[2]), F32)
        for i in range(tiles):
            r = slice(i * size, (i + 1) * size)
            d_up = nt(dlow_ref[r, :], down_ref[0]) * slope_ref[c, r, :]
            total += column_sum(d_up)
            d_low = d_up.astype(BF)
            slope_ref[c, r, :] = d_up
            acc_ref[r, :] += nt(d_low, up_ref[0])
        gbup_ref[0] = total
        gdown = tn(dlow_ref[...], hid_ref[c]).astype(BF)
        gup = tn(low_ref[...], slope_ref[c].astype(BF)).astype(BF)

        hid = gdown.shape[1]
        for there, k, down_to, up_to in (
            (c < heads // 2, c, down_sent_ref, up_sent_ref),
            (c >= heads // 2, c - heads // 2, down_kept_ref, up_kept_ref),
        ):

            @pl.when(there)
            def _():
                down_to[k, :, :hid] = gdown
                up_to[k, :, :hid] = gup

    @pl.when(step == 2 * heads - 1)
    def _():
        zero = jnp.zeros((1, x_ref.shape[1]), F32)
        g_sum, s_sum, b_sum = zero, zero, zero
        for i in range(tiles):
            r = slice(i * size, (i + 1) * size)
            d_first = acc_ref[r, :]
            normed = n1_ref[r, :]
            g_sum += column_sum(d_first * normed)
            s_sum += column_sum(d_first)
            e = d_first * gain_ref[0:1, :]
            d = inv1_ref[r, :] * (e - row_mean(e) - normed * row_mean(e * normed))
            b_sum += column_sum(d)
            dfi_ref[r, :] = d
            dlow_ref[r, :] = d.astype(BF)
        sums_ref[0:1, :] = b_sum
        sums_ref[2:3, :] = g_sum
        sums_ref[4:5, :] = s_sum
        for lo in range(4):
            r = slice(lo * 128, (lo + 1) * 128)
            back = nt(dlow_ref[r, :], wo_ref[...]).astype(BF)
            for hd in range(heads):
                for h in range(3):
                    piece = back[:, (hd * 3 + h) * DH : (hd * 3 + h + 1) * DH]
                    lanes = slice(lo * DH, (lo + 1) * DH)
                    if h == 1:
                        send_half_ref[hd, :, lanes] = piece
                        send_half_ref[heads + hd, :, lanes] = piece
                    else:
                        send_full_ref[hd + (h // 2) * heads, :, lanes] = piece
        whole = tn(dlow_ref[...], rows_ref[...]).astype(BF)
        blank = jnp.zeros((whole.shape[0], 2 * SIDE - 3 * DH), BF)
        for hd in range(heads):
            piece = jnp.concatenate([whole[:, hd * 3 * DH : (hd + 1) * 3 * DH], blank], 1)

            @pl.when(hc_ref[0] == hd % 2)
            def _():
                down_kept_ref[hd // 2, :, -SIDE:] = piece[:, :SIDE]
                up_kept_ref[hd // 2, :, -SIDE:] = piece[:, SIDE:]

            @pl.when(hc_ref[0] != hd % 2)
            def _():
                down_sent_ref[hd // 2, :, -SIDE:] = piece[:, :SIDE]
                up_sent_ref[hd // 2, :, -SIDE:] = piece[:, SIDE:]


def middle(hc, full, half, x_own, d_own, mask_col, wo, ff_all, bup_all, bias, gain, shift):
    heads, width, hid = ff_all.shape[0], ff_all.shape[2], bup_all.shape[2]
    pairs = heads // 2
    tokens = x_own.shape[0]

    def at(k, hc_ref):
        return jnp.where(k < pairs, 2 * k + 1 - hc_ref[0], 2 * (k - pairs) + hc_ref[0])

    once = lambda *shape: pl.BlockSpec(shape, lambda g, c: (0,) * len(shape))
    by_chunk = lambda part, *shape: pl.BlockSpec(shape, lambda g, c: (at(g % heads, c), part, 0))
    late = lambda *shape: pl.BlockSpec(shape, lambda g, c: (at(jnp.maximum(g - heads, 0), c), 0, 0))
    grads = pl.BlockSpec(
        (pairs, width, hid + SIDE), lambda g, c: (0, 0, 0), pipeline_mode=pl.Buffered(1)
    )
    big = jax.ShapeDtypeStruct((pairs, width, hid + SIDE), BF)
    table = jax.ShapeDtypeStruct((OWN * heads, 128, 256), BF)
    return pl.pallas_call(
        functools.partial(middle_body, heads),
        grid_spec=pltpu.PrefetchScalarGridSpec(
            num_scalar_prefetch=1,
            grid=(2 * heads,),
            in_specs=[
                once(OWN * heads, 128, 256),
                once(OWN * heads, 128, 256),
                once(tokens, width),
                once(tokens, width),
                once(tokens, 1),
                once(width, width),
                by_chunk(0, 1, width, hid),
                by_chunk(0, 1, 1, hid),
                by_chunk(1, 1, hid, width),
                once(2, width),
                once(2, width),
                once(2, width),
            ],
            out_specs=[
                once(tokens, width),
                once(OWN * heads, 128, 256),
                once(OWN * heads, 128, 256),
                once(tokens, width),
                grads,
                grads,
                grads,
                grads,
                once(8, width),
                late(1, 1, hid),
            ],
            scratch_shapes=[
                pltpu.VMEM((tokens, width), BF),
                pltpu.VMEM((tokens, width), F32),
                pltpu.VMEM((tokens, width), F32),
                pltpu.VMEM((tokens, 1), F32),
                pltpu.VMEM((tokens, width), BF),
                pltpu.VMEM((tokens, width), F32),
                pltpu.VMEM((heads, tokens, hid), BF),
                pltpu.VMEM((heads, tokens, hid), F32),
                pltpu.VMEM((tokens, width), BF),
            ],
        ),
        out_shape=[
            jax.ShapeDtypeStruct((tokens, width), BF),
            table,
            table,
            jax.ShapeDtypeStruct((tokens, width), F32),
            big,
            big,
            big,
            big,
            jax.ShapeDtypeStruct((8, width), F32),
            jax.ShapeDtypeStruct((heads, 1, hid), F32),
        ],
        compiler_params=pltpu.CompilerParams(vmem_limit_bytes=VMEM),
        name="middle",
        cost_estimate=cost(1),
    )(hc, full, half, x_own, d_own, mask_col, wo, ff_all, bup_all, ff_all, bias, gain, shift)


def swap(x, axis, bit=1):
    size = lax.axis_size(axis)
    return lax.ppermute(x, axis, [(i, i ^ bit) for i in range(size)])


def pick(x, index, axis=0):
    return lax.dynamic_index_in_dim(x, index, axis, keepdims=False)


def plus(a, b):
    return (a.astype(F32) + b.astype(F32)).astype(BF)


def fold(kept, came, index, axis):
    return tuple(plus(pick(kept, i, axis), pick(came, i, axis)) for i in (1 - index, index))


def total(pieces):
    return sum(p.astype(F32) for p in pieces)


barrier = lax.optimization_barrier


def per_device(
    inputs,
    w_qkv,
    b_qv,
    w_out,
    out_bias,
    w_up,
    b_up,
    w_down,
    norm_gain,
    norm_shift,
    d_out,
    q_perm,
    k_perm,
    masked,
):
    seqs, block_len, width = inputs.shape
    heads = lax.axis_size("hx") * lax.axis_size("hc")
    plane = OWN * heads
    share = block_len // heads
    tokens = seqs * share
    length = lax.axis_size("sq") * OWN
    sq = lax.axis_index("sq")
    own = lax.axis_index("own")
    hx = lax.axis_index("hx")
    hc = lax.axis_index("hc")
    head = hx * lax.axis_size("hc") + hc
    head_cols = q_perm.shape[1] * DH

    pad = jnp.zeros((15, width), BF)
    with_bias = jnp.concatenate([w_out, b_up[None], pad], 0)
    mine = lax.dynamic_slice_in_dim(inputs, head * share, share, 1)
    x_own = lax.all_to_all(mine, "sq", 0, 0, tiled=True).reshape(tokens, width)
    out_bias_all = lax.all_gather(with_bias, HEAD, axis=0, tiled=False)
    x_own, out_bias_all, d_out, q_perm, k_perm, w_qkv = barrier(
        (x_own, out_bias_all, d_out, q_perm, k_perm, w_qkv)
    )
    x_all = lax.all_gather(x_own, PLANE, axis=0, tiled=True)
    d_own = lax.all_to_all(d_out, "sq", 0, 0, tiled=True).reshape(tokens, width)

    def positions(perm):
        mine = pick(perm, sq)
        full = pick(mine, 2 * own).reshape(2, TOK_DEV)
        half = lax.dynamic_slice_in_dim(mine[1], own * TOK_DEV, TOK_DEV, 0)
        return jnp.concatenate([full, half[None]], 0).reshape(-1, 1, CHUNK)

    masked_row = pick(masked, sq)
    *places, mask_col = prepare(
        block_len,
        heads,
        jnp.stack([own, head]).astype(jnp.int32),
        positions(q_perm),
        positions(k_perm),
        masked_row[None],
        tokens,
    )

    def two_heads(x):
        full = lax.dynamic_slice_in_dim(x, own * 2 * DH, DH, x.ndim - 1)
        return full, x[..., DH : 2 * DH]

    w_full, w_half = two_heads(w_qkv)
    w_sel = jnp.concatenate(
        [w_full[0], w_half[0], w_full[1], w_full[2], w_half[1], w_half[2]], 1
    )
    b_full, b_half = two_heads(b_qv.astype(F32))
    none = jnp.zeros((DH,), F32)
    b_sel = jnp.concatenate([b_full[0], b_half[0], none, b_full[1], none, b_half[1]])[None]
    w_rows = jnp.concatenate(
        [w_qkv[0]]
        + [w_qkv[i, :, h * DH : (h + 1) * DH] for h in range(3) for i in (1, 2)],
        1,
    ).T
    ff = jnp.concatenate([w_up, w_down], 0)

    slots = lax.dynamic_slice_in_dim(pick(q_perm, sq), own * TOK_DEV, TOK_DEV, 1)
    slot_masked = jnp.any(slots[..., None] == masked_row[None, None, :], -1).astype(jnp.int32)
    occupancy = jnp.sum(slot_masked.reshape(slots.shape[0], TOK_DEV // CLUSTER, CLUSTER), -1)
    bias = out_bias.astype(F32)
    out_all = out_bias_all[:, : w_out.shape[0]].reshape(heads * head_cols, width)
    bup_all = out_bias_all[:, w_out.shape[0]].astype(F32)[:, None]

    (
        x_all,
        d_own,
        places,
        w_sel,
        b_sel,
        w_rows,
        mask_col,
        occupancy,
        bias,
        out_all,
        bup_all,
        ff,
    ) = barrier(
        (
            x_all,
            d_own,
            places,
            w_sel,
            b_sel,
            w_rows,
            mask_col,
            occupancy,
            bias,
            out_all,
            bup_all,
            ff,
        )
    )
    ff_all = lax.all_gather(ff, HEAD, axis=0, tiled=False)

    tq_full, tq_half, tkv_full, tkv_half = project(x_all, w_sel, b_sel)
    half_at = 2 * TOK_DEV // CHUNK
    *kept_full, ent_full, done_full = attend(places, 0, half_at, tq_full, tkv_full)
    done_full, tq_half = barrier((done_full, tq_half))
    got_full = lax.all_to_all(done_full, PLANE, 0, 0, tiled=True)
    *kept_half, ent_half, done_half = attend(places, half_at, half_at // 2, tq_half, tkv_half)
    done_half, got_full = barrier((done_half, got_full))
    got_half = lax.all_to_all(done_half, PLANE, 0, 0, tiled=True)
    ent_seg = jnp.concatenate([ent_full, ent_half], 0)[:, :GROUPS, 0].reshape(3, TOK_DEV // CLUSTER)
    ent_got = swap(jnp.where(own == 0, ent_seg[1], ent_seg[0]), "own")
    ff_all, w_rows, got_half = barrier((ff_all, w_rows, got_half))
    w_all = lax.all_gather(w_rows, HEAD, axis=0, tiled=False)
    (
        result_own,
        send_full,
        send_half,
        d_first_in,
        down_sent,
        down_kept,
        up_sent,
        up_kept,
        sums_own,
        grad_bup,
    ) = middle(
        hc[None],
        got_full,
        got_half,
        x_own,
        d_own,
        mask_col,
        out_all,
        ff_all,
        bup_all,
        bias,
        norm_gain,
        norm_shift,
    )
    rows = width // length
    near = seqs <= 4

    def shifted(pieces):
        return [pieces[0]] + [
            lax.ppermute(p, "sq", [(i, (i + s) % seqs) for i in range(seqs)])
            for s, p in enumerate(pieces)
            if s > 0
        ]

    def cut_z(x):
        return [pick(x, (sq + s) % seqs) for s in range(seqs)] if near else [x]

    def over_z(pieces):
        if near:
            return shifted(pieces)
        return list(lax.all_to_all(pieces[0], "sq", 0, 0, tiled=True))

    td_full = lax.all_to_all(send_full, PLANE, 0, 0, tiled=True)
    down_came, up_came = swap(down_sent, "hc"), swap(up_sent, "hc")
    result_own = cut_z(result_own.reshape(seqs, share, width))
    cut = lambda x: x.reshape(x.shape[0], length // OWN, OWN, rows, x.shape[-1])
    down_sent, down_kept = fold(cut(down_kept), cut(down_came), hx, 0)
    up_sent, up_kept = fold(cut(up_kept), cut(up_came), own, 2)
    (
        td_full,
        send_half,
        ent_got,
        w_all,
        down_sent,
        down_kept,
        up_sent,
        up_kept,
        result_own,
    ) = barrier(
        (
            td_full,
            send_half,
            ent_got,
            w_all,
            down_sent,
            down_kept,
            up_sent,
            up_kept,
            result_own,
        )
    )
    td_half = lax.all_to_all(send_half, PLANE, 0, 0, tiled=True)
    down_came, up_came = swap(down_sent, "hx"), swap(up_sent, "own")
    result_got = over_z(result_own)
    rows_full = attend_back(places, 0, td_full.reshape(plane * 128, 256), *kept_full)
    rows_full, td_half, down_came, up_came, result_got = barrier(
        (rows_full, td_half, down_came, up_came, result_got)
    )
    back_full = lax.all_to_all(rows_full, PLANE, 0, 0, tiled=True)
    down_sent, down_kept = fold(down_kept, down_came, own, 1)
    up_sent, up_kept = fold(up_kept, up_came, hx, 0)
    td_half, down_sent, down_kept, up_sent, up_kept = barrier(
        (td_half, down_sent, down_kept, up_sent, up_kept)
    )
    down_came, up_came = swap(down_sent, "own"), swap(up_sent, "hx")
    rows_half = attend_back(places, half_at, td_half.reshape(plane * 128, 256), *kept_half)
    rows_half, back_full, down_came, up_came = barrier((rows_half, back_full, down_came, up_came))
    back_half = lax.all_to_all(rows_half, PLANE, 0, 0, tiled=True)
    both = cut_z(jnp.concatenate([plus(down_kept, down_came), plus(up_kept, up_came)], 2))
    rows_full, rows_half, both = barrier((rows_full, rows_half, both))
    both_got = over_z(both)
    grad_sel, sum_sel = project_grad(x_all, rows_full, rows_half)

    sums = sum_sel.reshape(6, DH)
    at_full = (jnp.arange(3) == 2 * own)[:, None]
    at_half = (jnp.arange(3) == 1)[:, None]
    at_head = (jnp.arange(heads) == head)[None, :, None, None]
    pair = jnp.stack(
        [jnp.where(at_full, sums[a], 0.0) + jnp.where(at_half, sums[b], 0.0) for a, b in ((0, 1), (3, 5))]
    )
    bqv = jnp.where(at_head, pair[:, None], 0.0)
    small = jnp.concatenate([sums_own[:6].reshape(-1), grad_bup.reshape(-1), bqv.reshape(-1)])
    grad_sel = grad_sel.reshape(length // OWN, OWN, rows, 384)
    grad_sent, grad_kept = pick(grad_sel, 1 - own, 1), pick(grad_sel, own, 1)
    grad_came = swap(grad_sent, "own")
    for axis in ("hc", "hx", "own"):
        small = small + swap(small, axis)
    back_full, back_half, grad_came, small, both_got = barrier(
        (back_full, back_half, grad_came, small, both_got)
    )
    low = jnp.where(own == 0, grad_kept, grad_came)
    high = jnp.where(own == 0, grad_came, grad_kept)
    shared = plus(grad_kept, grad_came)
    order = [(low, 0), (shared, 1), (high, 0), (low, 2), (shared, 4), (high, 2), (low, 3), (shared, 5), (high, 3)]
    grad_all = cut_z(jnp.concatenate([a[..., c * DH : (c + 1) * DH] for a, c in order], -1))
    back_full, grad_all = barrier((back_full, grad_all))
    grad_got = over_z(grad_all)
    bit = 1
    while bit < seqs:
        small = small + swap(small, "sq", bit)
        bit *= 2
    d_in_own = project_back(back_full, back_half, w_all, d_first_in)
    d_inputs = lax.all_to_all(
        d_in_own.reshape(seqs, share, width), "sq", 0, 0, tiled=True
    ).astype(F32)
    both = total(both_got)
    wide = both.shape[1] // 2
    down_sum = both[:, : wide - SIDE]
    up_sum = both[:, wide : 2 * wide - SIDE]
    out_sum = jnp.concatenate([both[:, wide - SIDE : wide], both[:, 2 * wide - SIDE :]], 1)[:, :head_cols]
    qkv_sum = total(grad_got).reshape(rows, 3, head_cols).transpose(1, 0, 2)
    if near:
        parts = []
        for i in range(seqs):
            part = result_got[0]
            for s in range(1, seqs):
                part = jnp.where((i + s) % seqs == sq, result_got[s], part)
            parts.append(part)
        result = jnp.stack(parts)
    else:
        result = jnp.stack(result_got)

    obias_sum = small[: 2 * width].reshape(2, width)
    gain_sum = small[2 * width : 4 * width].reshape(2, width)
    shift_sum = small[4 * width : 6 * width].reshape(2, width)
    bup_sum = small[6 * width : -2 * width]
    bqv_sum = small[-2 * width :].reshape(2, width)

    entropy = jnp.stack(
        [
            jnp.where(own == 0, ent_seg[0], ent_got),
            ent_seg[2],
            jnp.where(own == 0, ent_got, ent_seg[1]),
        ]
    )
    return (
        result.astype(F32),
        d_inputs,
        qkv_sum,
        bqv_sum,
        out_sum.T,
        obias_sum,
        up_sum,
        bup_sum,
        down_sum.T,
        gain_sum,
        shift_sum,
        entropy,
        occupancy,
    )


def solution(mesh):
    seq, head = (mesh.shape["seq"], mesh.shape["head"])
    fine = Mesh(
        mesh.devices.reshape(seq // OWN, OWN, 2, head // 2), ("sq", "own", "hx", "hc")
    )
    both = SEQ + HEAD
    placed = (
        P(None, SEQ, None),
        P(None, None, HEAD),
        P(None, HEAD),
        P(HEAD, None),
        P(),
        P(None, HEAD),
        P(HEAD),
        P(HEAD, None),
        P(),
        P(),
        P(None, both, None),
        P(None, HEAD, None),
        P(None, HEAD, None),
        P(),
    )
    return jax.shard_map(
        per_device,
        mesh=fine,
        in_specs=placed,
        out_specs=(
            P(None, both, None),
            P(None, both, None),
            P(None, SEQ, HEAD),
            P(),
            P(HEAD, SEQ),
            P(),
            P(SEQ, HEAD),
            P(),
            P(HEAD, SEQ),
            P(),
            P(),
            P(HEAD, SEQ),
            P(HEAD, SEQ),
        ),
        check_vma=False,
    )
```

```python
import functools

import jax
import jax.numpy as jnp
from jax import lax
from jax.experimental import pallas as pl
from jax.experimental.pallas import tpu as pltpu
from jax.sharding import Mesh
from jax.sharding import PartitionSpec as P

DH = 64
FF = 3072
CLUSTER = 128
LENGTH = 4096
TOK_DEV = 2048
OWN = LENGTH // TOK_DEV
EPS = 1e-06
PLANE = ("own", "hx", "hc")
HEAD = ("hx", "hc")
SEQ = ("sq", "own")
CHUNK = 512
GROUPS = CHUNK // CLUSTER
BF = jnp.bfloat16
F32 = jnp.float32
VMEM = 56 * 1024 * 1024
SIDE = 128


def cost(micros):
    return pl.CostEstimate(flops=micros * 10**9, transcendentals=0, bytes_accessed=micros * 10**6)


def nn(a, b):
    return lax.dot_general(a, b, (((1,), (0,)), ((), ())), preferred_element_type=F32)


def nt(a, b):
    return lax.dot_general(a, b, (((1,), (1,)), ((), ())), preferred_element_type=F32)


def tn(a, b):
    return lax.dot_general(a, b, (((0,), (0,)), ((), ())), preferred_element_type=F32)


def log2(n):
    return n.bit_length() - 1


def prepare_body(
    block_len, heads, here_ref, q_ref, k_ref, masked_ref, pq_ref, pk_ref, pqr_ref, pkr_ref, mask_ref
):
    share = block_len // heads

    def place(pos, size):
        block = pos >> log2(block_len)
        rest = pos & (block_len - 1)
        device = (block & (OWN - 1)) * heads + (rest >> log2(share))
        token = (block >> log2(OWN)) * share + (rest & (share - 1))
        return ((token >> log2(size)) << log2(size * OWN * heads)) + device * size + (token & (size - 1))

    for pos_ref, col_ref, row_ref, size in (
        (q_ref, pq_ref, pqr_ref, 128),
        (k_ref, pk_ref, pkr_ref, 256),
    ):
        for c in range(pos_ref.shape[0]):
            row = place(pos_ref[c], size)
            row_ref[c] = row
            col_ref[c] = jnp.broadcast_to(row, (8, CHUNK)).T[:, :1]
    token = lax.broadcasted_iota(jnp.int32, mask_ref.shape, 0)
    own_pos = (
        (((token >> log2(share)) * OWN + here_ref[0]) << log2(block_len))
        + here_ref[1] * share
        + (token & (share - 1))
    )
    mask_ref[...] = jnp.max((own_pos == masked_ref[...]).astype(F32), 1, keepdims=True)


def prepare(block_len, heads, here, q_pos, k_pos, masked_row, tokens):
    steps = q_pos.shape[0]
    vmem = pl.BlockSpec(memory_space=pltpu.VMEM)
    col = jax.ShapeDtypeStruct((steps, CHUNK, 1), jnp.int32)
    row = jax.ShapeDtypeStruct((steps, 1, CHUNK), jnp.int32)
    return pl.pallas_call(
        functools.partial(prepare_body, block_len, heads),
        in_specs=[pl.BlockSpec(memory_space=pltpu.SMEM), vmem, vmem, vmem],
        out_specs=[vmem] * 5,
        out_shape=[col, col, row, row, jax.ShapeDtypeStruct((tokens, 1), F32)],
        compiler_params=pltpu.CompilerParams(vmem_limit_bytes=VMEM),
        name="prepare",
        cost_estimate=cost(1),
    )(here, q_pos, k_pos, masked_row)


def project_body(x_ref, w_ref, b_ref, tq0_ref, tq1_ref, tkv0_ref, tkv1_ref):
    y = (nn(x_ref[...], w_ref[...]) + b_ref[...]).astype(BF)
    for t, (tq_ref, tkv_ref) in enumerate(((tq0_ref, tkv0_ref), (tq1_ref, tkv1_ref))):
        for lo in range(4):
            tq_ref[:, lo * DH : (lo + 1) * DH] = y[
                lo * 128 : (lo + 1) * 128, t * DH : (t + 1) * DH
            ]
        for lo in range(2):
            tkv_ref[:, lo * 128 : (lo + 1) * 128] = y[
                lo * 256 : (lo + 1) * 256, (t + 1) * 128 : (t + 2) * 128
            ]


def project(x_all, w_sel, b_sel):
    blocks = x_all.shape[0] // 512
    width = x_all.shape[1]
    quarter = pl.BlockSpec((128, 256), lambda j: (j, 0))
    half = pl.BlockSpec((256, 256), lambda j: (j, 0))
    quarter_shape = jax.ShapeDtypeStruct((1024, 256), BF)
    half_shape = jax.ShapeDtypeStruct((2048, 256), BF)
    return pl.pallas_call(
        project_body,
        grid=(blocks,),
        in_specs=[
            pl.BlockSpec((512, width), lambda j: (j, 0)),
            pl.BlockSpec((width, 384), lambda j: (0, 0)),
            pl.BlockSpec((1, 384), lambda j: (0, 0)),
        ],
        out_specs=[quarter, quarter, half, half],
        out_shape=[quarter_shape, quarter_shape, half_shape, half_shape],
        compiler_params=pltpu.CompilerParams(vmem_limit_bytes=VMEM),
        name="project",
        cost_estimate=cost(1),
    )(x_all, w_sel, b_sel)


def hot_rows(col, count):
    return (lax.broadcasted_iota(jnp.int32, (col.shape[0], count), 1) == col).astype(BF)


def hot_cols(row, count):
    return (lax.broadcasted_iota(jnp.int32, (count, row.shape[1]), 0) == row).astype(BF)


def take_quarter(table, place):
    wide = nn(hot_rows(place & 1023, 1024), table)
    lane = lax.broadcasted_iota(jnp.int32, wide.shape, 1)
    wide = jnp.where((lane >> 6) == (place >> 10), wide, 0.0)
    half = wide[:, :128] + wide[:, 128:]
    return half + pltpu.roll(half, 64, 1)


def take_half(table, place):
    wide = nn(hot_rows(place & 2047, 2048), table)
    return jnp.where((place >> 11) == 1, wide[:, 128:], wide[:, :128])


def spread_quarter(twice, place):
    wide = jnp.concatenate([twice, twice], 1)
    lane = lax.broadcasted_iota(jnp.int32, wide.shape, 1)
    return jnp.where((lane >> 6) == (place >> 10), wide, 0.0).astype(BF)


def spread_half(rows, place):
    upper = (place >> 11) == 1
    return jnp.concatenate(
        [jnp.where(upper, 0.0, rows), jnp.where(upper, rows, 0.0)], 1
    ).astype(BF)


def low_lanes(shape):
    return lax.broadcasted_iota(jnp.int32, shape, 1) < DH


def attend_body(
    pq_ref, pk_ref, pqr_ref, tq_ref, tkv_ref, q_ref, kv_ref, lt_ref, ent_ref, out_ref, acc_ref
):
    step = pl.program_id(0)
    place_q = pq_ref[0]
    twice = take_quarter(tq_ref[...], place_q)
    q_all = jnp.where(low_lanes(twice.shape), twice, 0.0).astype(BF)
    kv_all = take_half(tkv_ref[...], pk_ref[0]).astype(BF)
    q_ref[0] = q_all
    kv_ref[0] = kv_all
    outs = []
    ents = []
    for c in range(GROUPS):
        rows = slice(c * CLUSTER, (c + 1) * CLUSTER)
        q = q_all[rows]
        kv = kv_all[rows]
        scores = nt(q, kv) * (DH**-0.5)
        top = jnp.max(scores, 1, keepdims=True)
        total = jnp.sum(jnp.exp(scores - top), 1, keepdims=True)
        log_total = top + jnp.log(total)
        soft = jnp.exp(scores - log_total)
        inner = jnp.sum(soft * scores, 1, keepdims=True)
        ents.append(
            jnp.broadcast_to(jnp.sum(log_total - inner, 0, keepdims=True) / CLUSTER, (1, 128))
        )
        lt_ref[0, rows, :] = log_total
        got = nn(soft.astype(BF), kv)
        outs.append(jnp.where(low_lanes(got.shape), pltpu.roll(got, 64, 1), got))
    ent_ref[0] = jnp.concatenate(ents + ents, 0)
    spread = spread_quarter(jnp.concatenate(outs, 0), place_q)
    part = nn(hot_cols(pqr_ref[0] & 1023, 1024), spread)

    @pl.when(step == 0)
    def _():
        acc_ref[...] = part

    @pl.when(step > 0)
    def _():
        acc_ref[...] += part

    @pl.when(step == pl.num_programs(0) - 1)
    def _():
        for j in range(out_ref.shape[0]):
            out_ref[j] = acc_ref[j * 128 : (j + 1) * 128, :].astype(BF)


def once(*shape):
    return pl.BlockSpec(shape, lambda g: (0,) * len(shape))


def attend(places, start, steps, tq, tkv):
    pq_col, pk_col, pq_row, _ = places
    chunk = lambda width: pl.BlockSpec((1, CHUNK, width), lambda g: (g, 0, 0))
    col = pl.BlockSpec((1, CHUNK, 1), lambda g: (g + start, 0, 0))
    return pl.pallas_call(
        attend_body,
        grid=(steps,),
        in_specs=[
            col,
            col,
            pl.BlockSpec((1, 1, CHUNK), lambda g: (g + start, 0, 0)),
            once(1024, 256),
            once(2048, 256),
        ],
        out_specs=[
            chunk(128),
            chunk(128),
            chunk(1),
            pl.BlockSpec((1, 8, 128), lambda g: (g, 0, 0)),
            once(8, 128, 256),
        ],
        out_shape=[
            jax.ShapeDtypeStruct((steps, CHUNK, 128), BF),
            jax.ShapeDtypeStruct((steps, CHUNK, 128), BF),
            jax.ShapeDtypeStruct((steps, CHUNK, 1), F32),
            jax.ShapeDtypeStruct((steps, 8, 128), F32),
            jax.ShapeDtypeStruct((8, 128, 256), BF),
        ],
        scratch_shapes=[pltpu.VMEM((1024, 256), F32)],
        compiler_params=pltpu.CompilerParams(vmem_limit_bytes=VMEM),
        name="attend",
        cost_estimate=cost(1),
    )(pq_col, pk_col, pq_row, tq, tkv)


def attend_back_body(
    pq_ref, pk_ref, pqr_ref, pkr_ref, td_ref, q_ref, kv_ref, lt_ref, out_ref, accq, acckv
):
    step = pl.program_id(0)
    place_q = pq_ref[0]
    twice = take_quarter(td_ref[...], place_q)
    d_all = jnp.where(low_lanes(twice.shape), 0.0, twice).astype(BF)
    gq = []
    gkv = []
    for c in range(GROUPS):
        rows = slice(c * CLUSTER, (c + 1) * CLUSTER)
        q = q_ref[0, rows, :]
        kv = kv_ref[0, rows, :]
        d = d_all[rows]
        scores = nt(q, kv) * (DH**-0.5)
        soft = jnp.exp(scores - lt_ref[0, rows, :])
        d_soft = nt(d, kv)
        d_scores = soft * (d_soft - jnp.sum(soft * d_soft, 1, keepdims=True))
        d_raw = (d_scores * (DH**-0.5)).astype(BF)
        got = nn(d_raw, kv)
        gq.append(jnp.where(low_lanes(got.shape), got, pltpu.roll(got, 64, 1)))
        gkv.append(tn(d_raw, q) + tn(soft.astype(BF), d))
    part_q = nn(
        hot_cols(pqr_ref[0] & 1023, 1024), spread_quarter(jnp.concatenate(gq, 0), place_q)
    )
    part_kv = nn(
        hot_cols(pkr_ref[0] & 2047, 2048), spread_half(jnp.concatenate(gkv, 0), pk_ref[0])
    )

    @pl.when(step == 0)
    def _():
        accq[...] = part_q
        acckv[...] = part_kv

    @pl.when(step > 0)
    def _():
        accq[...] += part_q
        acckv[...] += part_kv

    @pl.when(step == pl.num_programs(0) - 1)
    def _():
        for j in range(out_ref.shape[0]):
            out_ref[j, :128, :] = accq[j * 128 : (j + 1) * 128, :].astype(BF)
            out_ref[j, 128:, :] = acckv[j * 256 : (j + 1) * 256, :].astype(BF)


def attend_back(places, start, td, q_all, kv_all, log_total):
    pq_col, pk_col, pq_row, pk_row = places
    steps = q_all.shape[0]
    chunk = lambda width: pl.BlockSpec((1, CHUNK, width), lambda g: (g, 0, 0))
    col = pl.BlockSpec((1, CHUNK, 1), lambda g: (g + start, 0, 0))
    line = pl.BlockSpec((1, 1, CHUNK), lambda g: (g + start, 0, 0))
    return pl.pallas_call(
        attend_back_body,
        grid=(steps,),
        in_specs=[
            col,
            col,
            line,
            line,
            once(1024, 256),
            chunk(128),
            chunk(128),
            chunk(1),
        ],
        out_specs=once(8, 384, 256),
        out_shape=jax.ShapeDtypeStruct((8, 384, 256), BF),
        scratch_shapes=[pltpu.VMEM((1024, 256), F32), pltpu.VMEM((2048, 256), F32)],
        compiler_params=pltpu.CompilerParams(vmem_limit_bytes=VMEM),
        name="attend_back",
        cost_estimate=cost(1),
    )(pq_col, pk_col, pq_row, pk_row, td, q_all, kv_all, log_total)


def project_grad_body(x_ref, full_ref, half_ref, grad_ref, sum_ref, acc_ref):
    j = pl.program_id(0)
    quarters = []
    for lo in range(4):
        cols = slice(lo * DH, (lo + 1) * DH)
        quarters.append(jnp.concatenate([full_ref[0, :128, cols], half_ref[0, :128, cols]], 1))
    parts = [jnp.concatenate(quarters, 0)]
    for ref in (full_ref, half_ref):
        parts.append(jnp.concatenate([ref[0, 128:, :128], ref[0, 128:, 128:]], 0))
    rows = jnp.concatenate(parts, 1)
    part = tn(x_ref[...], rows)
    sums = jnp.sum(rows.astype(F32), 0, keepdims=True)

    @pl.when(j == 0)
    def _():
        acc_ref[...] = part
        sum_ref[...] = sums

    @pl.when(j > 0)
    def _():
        acc_ref[...] += part
        sum_ref[...] += sums

    @pl.when(j == pl.num_programs(0) - 1)
    def _():
        grad_ref[...] = acc_ref[...].astype(BF)


def project_grad(x_all, full, half):
    tokens, width = x_all.shape
    rows = pl.BlockSpec((1, 384, 256), lambda j: (j, 0, 0))
    return pl.pallas_call(
        project_grad_body,
        grid=(tokens // 512,),
        in_specs=[pl.BlockSpec((512, width), lambda j: (j, 0)), rows, rows],
        out_specs=[once(width, 384), once(1, 384)],
        out_shape=[
            jax.ShapeDtypeStruct((width, 384), BF),
            jax.ShapeDtypeStruct((1, 384), F32),
        ],
        scratch_shapes=[pltpu.VMEM((width, 384), F32)],
        compiler_params=pltpu.CompilerParams(vmem_limit_bytes=VMEM),
        name="project_grad",
        cost_estimate=cost(1),
    )(x_all, full, half)


def project_back_body(heads, full_ref, half_ref, w_ref, dfi_ref, dx_ref, q_ref, kv_ref):
    for hd in range(heads):
        for h in range(3):
            if h == 1:
                piece = (half_ref[hd].astype(F32) + half_ref[heads + hd].astype(F32)).astype(BF)
            else:
                piece = full_ref[(h // 2) * heads + hd]
            n = hd * 3 + h
            for lo in range(4):
                q_ref[lo * 128 : (lo + 1) * 128, hd * 256 + h * DH : hd * 256 + (h + 1) * DH] = piece[
                    :128, lo * DH : (lo + 1) * DH
                ]
            for lo in range(2):
                kv_ref[lo * 256 : (lo + 1) * 256, n * 128 : (n + 1) * 128] = piece[
                    128:, lo * 128 : (lo + 1) * 128
                ]
    for i in range(4):
        r = slice(i * 128, (i + 1) * 128)
        dx = dfi_ref[r, :]
        for hd in range(heads):
            dx += nn(q_ref[r, hd * 256 : hd * 256 + 3 * DH], w_ref[hd, : 3 * DH, :])
            dx += nn(kv_ref[r, hd * 384 : (hd + 1) * 384], w_ref[hd, 3 * DH :, :])
        dx_ref[r, :] = dx.astype(BF)


def project_back(full, half, w_all, d_first_in):
    tokens, width = d_first_in.shape
    heads = w_all.shape[0]
    return pl.pallas_call(
        functools.partial(project_back_body, heads),
        out_shape=jax.ShapeDtypeStruct((tokens, width), BF),
        scratch_shapes=[
            pltpu.VMEM((tokens, heads * 256), BF),
            pltpu.VMEM((tokens, heads * 384), BF),
        ],
        compiler_params=pltpu.CompilerParams(vmem_limit_bytes=VMEM),
        name="project_back",
        cost_estimate=cost(1),
    )(full, half, w_all, d_first_in)


def erf_parts(u):
    mag = jnp.abs(u) * (0.5**0.5)
    bell = jnp.exp(-(mag * mag))
    t = 1.0 / (1.0 + 0.3275911 * mag)
    poly = t * (
        0.254829592
        + t * (-0.284496736 + t * (1.421413741 + t * (-1.453152027 + t * 1.061405429)))
    )
    tail = 0.5 * poly * bell
    return jnp.where(u < 0, tail, 1.0 - tail), bell * ((2 * jnp.pi) ** -0.5)


def row_mean(x):
    return jnp.mean(x, 1, keepdims=True)


def column_sum(x):
    return jnp.sum(x, 0, keepdims=True)


def middle_body(
    heads,
    hc_ref,
    full_ref,
    half_ref,
    x_ref,
    dout_ref,
    mask_ref,
    wo_ref,
    up_ref,
    bup_ref,
    down_ref,
    bias_ref,
    gain_ref,
    shift_ref,
    res_ref,
    send_full_ref,
    send_half_ref,
    dfi_ref,
    down_sent_ref,
    down_kept_ref,
    up_sent_ref,
    up_kept_ref,
    sums_ref,
    gbup_ref,
    rows_ref,
    first_ref,
    n1_ref,
    inv1_ref,
    low_ref,
    acc_ref,
    hid_ref,
    slope_ref,
    dlow_ref,
):
    step = pl.program_id(0)
    tiles = 4
    tokens = x_ref.shape[0]
    size = tokens // tiles

    @pl.when(step == 0)
    def _():
        for hd in range(heads):
            for h in range(3):
                if h == 1:
                    piece = (half_ref[hd].astype(F32) + half_ref[heads + hd].astype(F32)).astype(BF)
                else:
                    piece = full_ref[hd + (h // 2) * heads]
                col = (hd * 3 + h) * DH
                for lo in range(4):
                    rows_ref[lo * 128 : (lo + 1) * 128, col : col + DH] = piece[
                        :, lo * DH : (lo + 1) * DH
                    ]
        for i in range(tiles):
            r = slice(i * size, (i + 1) * size)
            v = x_ref[r, :].astype(F32) + nn(rows_ref[r, :], wo_ref[...]) + bias_ref[0:1, :]
            centred = v - row_mean(v)
            inv = lax.rsqrt(row_mean(centred * centred) + EPS)
            normed = centred * inv
            first = normed * gain_ref[0:1, :] + shift_ref[0:1, :]
            n1_ref[r, :] = normed
            inv1_ref[r, :] = inv
            first_ref[r, :] = first
            low_ref[r, :] = first.astype(BF)
            acc_ref[r, :] = first + bias_ref[1:2, :]

    @pl.when(step < heads)
    def _():
        for i in range(tiles):
            r = slice(i * size, (i + 1) * size)
            u = nn(low_ref[r, :], up_ref[0]) + bup_ref[0]
            phi, bell = erf_parts(u)
            hid = (u * phi).astype(BF)
            hid_ref[step, r, :] = hid
            slope_ref[step, r, :] = phi + u * bell
            acc_ref[r, :] += nn(hid, down_ref[0])

    @pl.when(step == heads)
    def _():
        zero = jnp.zeros((1, x_ref.shape[1]), F32)
        g_sum, s_sum, b_sum = zero, zero, zero
        for i in range(tiles):
            r = slice(i * size, (i + 1) * size)
            v = acc_ref[r, :]
            centred = v - row_mean(v)
            inv = lax.rsqrt(row_mean(centred * centred) + EPS)
            normed = centred * inv
            res_ref[r, :] = (normed * gain_ref[1:2, :] + shift_ref[1:2, :]).astype(BF)
            seed = dout_ref[r, :].astype(F32) * mask_ref[r, :]
            g_sum += column_sum(seed * normed)
            s_sum += column_sum(seed)
            e = seed * gain_ref[1:2, :]
            d = inv * (e - row_mean(e) - normed * row_mean(e * normed))
            b_sum += column_sum(d)
            acc_ref[r, :] = d
            dlow_ref[r, :] = d.astype(BF)
        sums_ref[1:2, :] = b_sum
        sums_ref[3:4, :] = g_sum
        sums_ref[5:6, :] = s_sum

    @pl.when(step >= heads)
    def _():
        c = step - heads
        total = jnp.zeros((1, up_ref.shape[2]), F32)
        for i in range(tiles):
            r = slice(i * size, (i + 1) * size)
            d_up = nt(dlow_ref[r, :], down_ref[0]) * slope_ref[c, r, :]
            total += column_sum(d_up)
            d_low = d_up.astype(BF)
            slope_ref[c, r, :] = d_up
            acc_ref[r, :] += nt(d_low, up_ref[0])
        gbup_ref[0] = total
        gdown = tn(dlow_ref[...], hid_ref[c]).astype(BF)
        gup = tn(low_ref[...], slope_ref[c].astype(BF)).astype(BF)

        hid = gdown.shape[1]
        for there, k, down_to, up_to in (
            (c < heads // 2, c, down_sent_ref, up_sent_ref),
            (c >= heads // 2, c - heads // 2, down_kept_ref, up_kept_ref),
        ):

            @pl.when(there)
            def _():
                down_to[k, :, :hid] = gdown
                up_to[k, :, :hid] = gup

    @pl.when(step == 2 * heads - 1)
    def _():
        zero = jnp.zeros((1, x_ref.shape[1]), F32)
        g_sum, s_sum, b_sum = zero, zero, zero
        for i in range(tiles):
            r = slice(i * size, (i + 1) * size)
            d_first = acc_ref[r, :]
            normed = n1_ref[r, :]
            g_sum += column_sum(d_first * normed)
            s_sum += column_sum(d_first)
            e = d_first * gain_ref[0:1, :]
            d = inv1_ref[r, :] * (e - row_mean(e) - normed * row_mean(e * normed))
            b_sum += column_sum(d)
            dfi_ref[r, :] = d
            dlow_ref[r, :] = d.astype(BF)
        sums_ref[0:1, :] = b_sum
        sums_ref[2:3, :] = g_sum
        sums_ref[4:5, :] = s_sum
        for lo in range(4):
            r = slice(lo * 128, (lo + 1) * 128)
            back = nt(dlow_ref[r, :], wo_ref[...]).astype(BF)
            for hd in range(heads):
                for h in range(3):
                    piece = back[:, (hd * 3 + h) * DH : (hd * 3 + h + 1) * DH]
                    lanes = slice(lo * DH, (lo + 1) * DH)
                    if h == 1:
                        send_half_ref[hd, :, lanes] = piece
                        send_half_ref[heads + hd, :, lanes] = piece
                    else:
                        send_full_ref[hd + (h // 2) * heads, :, lanes] = piece
        whole = tn(dlow_ref[...], rows_ref[...]).astype(BF)
        blank = jnp.zeros((whole.shape[0], 2 * SIDE - 3 * DH), BF)
        for hd in range(heads):
            piece = jnp.concatenate([whole[:, hd * 3 * DH : (hd + 1) * 3 * DH], blank], 1)

            @pl.when(hc_ref[0] == hd % 2)
            def _():
                down_kept_ref[hd // 2, :, -SIDE:] = piece[:, :SIDE]
                up_kept_ref[hd // 2, :, -SIDE:] = piece[:, SIDE:]

            @pl.when(hc_ref[0] != hd % 2)
            def _():
                down_sent_ref[hd // 2, :, -SIDE:] = piece[:, :SIDE]
                up_sent_ref[hd // 2, :, -SIDE:] = piece[:, SIDE:]


def middle(hc, full, half, x_own, d_own, mask_col, wo, ff_all, bup_all, bias, gain, shift):
    heads, width, hid = ff_all.shape[0], ff_all.shape[2], bup_all.shape[2]
    pairs = heads // 2
    tokens = x_own.shape[0]

    def at(k, hc_ref):
        return jnp.where(k < pairs, 2 * k + 1 - hc_ref[0], 2 * (k - pairs) + hc_ref[0])

    once = lambda *shape: pl.BlockSpec(shape, lambda g, c: (0,) * len(shape))
    by_chunk = lambda part, *shape: pl.BlockSpec(shape, lambda g, c: (at(g % heads, c), part, 0))
    late = lambda *shape: pl.BlockSpec(shape, lambda g, c: (at(jnp.maximum(g - heads, 0), c), 0, 0))
    grads = pl.BlockSpec(
        (pairs, width, hid + SIDE), lambda g, c: (0, 0, 0), pipeline_mode=pl.Buffered(1)
    )
    big = jax.ShapeDtypeStruct((pairs, width, hid + SIDE), BF)
    table = jax.ShapeDtypeStruct((OWN * heads, 128, 256), BF)
    return pl.pallas_call(
        functools.partial(middle_body, heads),
        grid_spec=pltpu.PrefetchScalarGridSpec(
            num_scalar_prefetch=1,
            grid=(2 * heads,),
            in_specs=[
                once(OWN * heads, 128, 256),
                once(OWN * heads, 128, 256),
                once(tokens, width),
                once(tokens, width),
                once(tokens, 1),
                once(width, width),
                by_chunk(0, 1, width, hid),
                by_chunk(0, 1, 1, hid),
                by_chunk(1, 1, hid, width),
                once(2, width),
                once(2, width),
                once(2, width),
            ],
            out_specs=[
                once(tokens, width),
                once(OWN * heads, 128, 256),
                once(OWN * heads, 128, 256),
                once(tokens, width),
                grads,
                grads,
                grads,
                grads,
                once(8, width),
                late(1, 1, hid),
            ],
            scratch_shapes=[
                pltpu.VMEM((tokens, width), BF),
                pltpu.VMEM((tokens, width), F32),
                pltpu.VMEM((tokens, width), F32),
                pltpu.VMEM((tokens, 1), F32),
                pltpu.VMEM((tokens, width), BF),
                pltpu.VMEM((tokens, width), F32),
                pltpu.VMEM((heads, tokens, hid), BF),
                pltpu.VMEM((heads, tokens, hid), F32),
                pltpu.VMEM((tokens, width), BF),
            ],
        ),
        out_shape=[
            jax.ShapeDtypeStruct((tokens, width), BF),
            table,
            table,
            jax.ShapeDtypeStruct((tokens, width), F32),
            big,
            big,
            big,
            big,
            jax.ShapeDtypeStruct((8, width), F32),
            jax.ShapeDtypeStruct((heads, 1, hid), F32),
        ],
        compiler_params=pltpu.CompilerParams(vmem_limit_bytes=VMEM),
        name="middle",
        cost_estimate=cost(1),
    )(hc, full, half, x_own, d_own, mask_col, wo, ff_all, bup_all, ff_all, bias, gain, shift)


def swap(x, axis, bit=1):
    size = lax.axis_size(axis)
    return lax.ppermute(x, axis, [(i, i ^ bit) for i in range(size)])


def pick(x, index, axis=0):
    return lax.dynamic_index_in_dim(x, index, axis, keepdims=False)


def plus(a, b):
    return (a.astype(F32) + b.astype(F32)).astype(BF)


def fold(kept, came, index, axis):
    return tuple(plus(pick(kept, i, axis), pick(came, i, axis)) for i in (1 - index, index))


def total(pieces):
    return sum(p.astype(F32) for p in pieces)


barrier = lax.optimization_barrier


def per_device(
    inputs,
    w_qkv,
    b_qv,
    w_out,
    out_bias,
    w_up,
    b_up,
    w_down,
    norm_gain,
    norm_shift,
    d_out,
    q_perm,
    k_perm,
    masked,
):
    seqs, block_len, width = inputs.shape
    heads = lax.axis_size("hx") * lax.axis_size("hc")
    plane = OWN * heads
    share = block_len // heads
    tokens = seqs * share
    length = lax.axis_size("sq") * OWN
    sq = lax.axis_index("sq")
    own = lax.axis_index("own")
    hx = lax.axis_index("hx")
    hc = lax.axis_index("hc")
    head = hx * lax.axis_size("hc") + hc
    head_cols = q_perm.shape[1] * DH

    pad = jnp.zeros((15, width), BF)
    with_bias = jnp.concatenate([w_out, b_up[None], pad], 0)
    mine = lax.dynamic_slice_in_dim(inputs, head * share, share, 1)
    x_own = lax.all_to_all(mine, "sq", 0, 0, tiled=True).reshape(tokens, width)
    out_bias_all = lax.all_gather(with_bias, HEAD, axis=0, tiled=False)
    x_own, out_bias_all, d_out, q_perm, k_perm, w_qkv = barrier(
        (x_own, out_bias_all, d_out, q_perm, k_perm, w_qkv)
    )
    x_all = lax.all_gather(x_own, PLANE, axis=0, tiled=True)
    d_own = lax.all_to_all(d_out, "sq", 0, 0, tiled=True).reshape(tokens, width)

    def positions(perm):
        mine = pick(perm, sq)
        full = pick(mine, 2 * own).reshape(2, TOK_DEV)
        half = lax.dynamic_slice_in_dim(mine[1], own * TOK_DEV, TOK_DEV, 0)
        return jnp.concatenate([full, half[None]], 0).reshape(-1, 1, CHUNK)

    masked_row = pick(masked, sq)
    *places, mask_col = prepare(
        block_len,
        heads,
        jnp.stack([own, head]).astype(jnp.int32),
        positions(q_perm),
        positions(k_perm),
        masked_row[None],
        tokens,
    )

    def two_heads(x):
        full = lax.dynamic_slice_in_dim(x, own * 2 * DH, DH, x.ndim - 1)
        return full, x[..., DH : 2 * DH]

    w_full, w_half = two_heads(w_qkv)
    w_sel = jnp.concatenate(
        [w_full[0], w_half[0], w_full[1], w_full[2], w_half[1], w_half[2]], 1
    )
    b_full, b_half = two_heads(b_qv.astype(F32))
    none = jnp.zeros((DH,), F32)
    b_sel = jnp.concatenate([b_full[0], b_half[0], none, b_full[1], none, b_half[1]])[None]
    w_rows = jnp.concatenate(
        [w_qkv[0]]
        + [w_qkv[i, :, h * DH : (h + 1) * DH] for h in range(3) for i in (1, 2)],
        1,
    ).T
    ff = jnp.concatenate([w_up, w_down], 0)

    slots = lax.dynamic_slice_in_dim(pick(q_perm, sq), own * TOK_DEV, TOK_DEV, 1)
    slot_masked = jnp.any(slots[..., None] == masked_row[None, None, :], -1).astype(jnp.int32)
    occupancy = jnp.sum(slot_masked.reshape(slots.shape[0], TOK_DEV // CLUSTER, CLUSTER), -1)
    bias = out_bias.astype(F32)
    out_all = out_bias_all[:, : w_out.shape[0]].reshape(heads * head_cols, width)
    bup_all = out_bias_all[:, w_out.shape[0]].astype(F32)[:, None]

    (
        x_all,
        d_own,
        places,
        w_sel,
        b_sel,
        w_rows,
        mask_col,
        occupancy,
        bias,
        out_all,
        bup_all,
        ff,
    ) = barrier(
        (
            x_all,
            d_own,
            places,
            w_sel,
            b_sel,
            w_rows,
            mask_col,
            occupancy,
            bias,
            out_all,
            bup_all,
            ff,
        )
    )
    ff_all = lax.all_gather(ff, HEAD, axis=0, tiled=False)

    tq_full, tq_half, tkv_full, tkv_half = project(x_all, w_sel, b_sel)
    half_at = 2 * TOK_DEV // CHUNK
    *kept_full, ent_full, done_full = attend(places, 0, half_at, tq_full, tkv_full)
    done_full, tq_half = barrier((done_full, tq_half))
    got_full = lax.all_to_all(done_full, PLANE, 0, 0, tiled=True)
    *kept_half, ent_half, done_half = attend(places, half_at, half_at // 2, tq_half, tkv_half)
    done_half, got_full = barrier((done_half, got_full))
    got_half = lax.all_to_all(done_half, PLANE, 0, 0, tiled=True)
    ent_seg = jnp.concatenate([ent_full, ent_half], 0)[:, :GROUPS, 0].reshape(3, TOK_DEV // CLUSTER)
    ent_got = swap(jnp.where(own == 0, ent_seg[1], ent_seg[0]), "own")
    ff_all, w_rows, got_half = barrier((ff_all, w_rows, got_half))
    w_all = lax.all_gather(w_rows, HEAD, axis=0, tiled=False)
    (
        result_own,
        send_full,
        send_half,
        d_first_in,
        down_sent,
        down_kept,
        up_sent,
        up_kept,
        sums_own,
        grad_bup,
    ) = middle(
        hc[None],
        got_full,
        got_half,
        x_own,
        d_own,
        mask_col,
        out_all,
        ff_all,
        bup_all,
        bias,
        norm_gain,
        norm_shift,
    )
    rows = width // length
    near = seqs <= 4

    def shifted(pieces):
        return [pieces[0]] + [
            lax.ppermute(p, "sq", [(i, (i + s) % seqs) for i in range(seqs)])
            for s, p in enumerate(pieces)
            if s > 0
        ]

    def cut_z(x):
        return [pick(x, (sq + s) % seqs) for s in range(seqs)] if near else [x]

    def over_z(pieces):
        if near:
            return shifted(pieces)
        return list(lax.all_to_all(pieces[0], "sq", 0, 0, tiled=True))

    td_full = lax.all_to_all(send_full, PLANE, 0, 0, tiled=True)
    down_came, up_came = swap(down_sent, "hc"), swap(up_sent, "hc")
    result_own = cut_z(result_own.reshape(seqs, share, width))
    cut = lambda x: x.reshape(x.shape[0], length // OWN, OWN, rows, x.shape[-1])
    down_sent, down_kept = fold(cut(down_kept), cut(down_came), hx, 0)
    up_sent, up_kept = fold(cut(up_kept), cut(up_came), own, 2)
    (
        td_full,
        send_half,
        ent_got,
        w_all,
        down_sent,
        down_kept,
        up_sent,
        up_kept,
        result_own,
    ) = barrier(
        (
            td_full,
            send_half,
            ent_got,
            w_all,
            down_sent,
            down_kept,
            up_sent,
            up_kept,
            result_own,
        )
    )
    td_half = lax.all_to_all(send_half, PLANE, 0, 0, tiled=True)
    down_came, up_came = swap(down_sent, "hx"), swap(up_sent, "own")
    result_got = over_z(result_own)
    rows_full = attend_back(places, 0, td_full.reshape(plane * 128, 256), *kept_full)
    rows_full, td_half, down_came, up_came, result_got = barrier(
        (rows_full, td_half, down_came, up_came, result_got)
    )
    back_full = lax.all_to_all(rows_full, PLANE, 0, 0, tiled=True)
    down_sent, down_kept = fold(down_kept, down_came, own, 1)
    up_sent, up_kept = fold(up_kept, up_came, hx, 0)
    td_half, down_sent, down_kept, up_sent, up_kept = barrier(
        (td_half, down_sent, down_kept, up_sent, up_kept)
    )
    down_came, up_came = swap(down_sent, "own"), swap(up_sent, "hx")
    rows_half = attend_back(places, half_at, td_half.reshape(plane * 128, 256), *kept_half)
    rows_half, back_full = barrier((rows_half, back_full))
    back_half = lax.all_to_all(rows_half, PLANE, 0, 0, tiled=True)
    rows_half, down_came, up_came = barrier((rows_half, down_came, up_came))
    both = cut_z(jnp.concatenate([plus(down_kept, down_came), plus(up_kept, up_came)], 2))
    rows_full, rows_half, both = barrier((rows_full, rows_half, both))
    both_got = over_z(both)
    grad_sel, sum_sel = project_grad(x_all, rows_full, rows_half)

    sums = sum_sel.reshape(6, DH)
    at_full = (jnp.arange(3) == 2 * own)[:, None]
    at_half = (jnp.arange(3) == 1)[:, None]
    at_head = (jnp.arange(heads) == head)[None, :, None, None]
    pair = jnp.stack(
        [jnp.where(at_full, sums[a], 0.0) + jnp.where(at_half, sums[b], 0.0) for a, b in ((0, 1), (3, 5))]
    )
    bqv = jnp.where(at_head, pair[:, None], 0.0)
    small = jnp.concatenate([sums_own[:6].reshape(-1), grad_bup.reshape(-1), bqv.reshape(-1)])
    grad_sel = grad_sel.reshape(length // OWN, OWN, rows, 384)
    grad_sent, grad_kept = pick(grad_sel, 1 - own, 1), pick(grad_sel, own, 1)
    grad_came = swap(grad_sent, "own")
    back_half, grad_came = barrier((back_half, grad_came))
    low = jnp.where(own == 0, grad_kept, grad_came)
    high = jnp.where(own == 0, grad_came, grad_kept)
    shared = plus(grad_kept, grad_came)
    order = [(low, 0), (shared, 1), (high, 0), (low, 2), (shared, 4), (high, 2), (low, 3), (shared, 5), (high, 3)]
    grad_all = cut_z(jnp.concatenate([a[..., c * DH : (c + 1) * DH] for a, c in order], -1))
    back_full, grad_all = barrier((back_full, grad_all))
    grad_got = over_z(grad_all)
    d_in_own = project_back(back_full, back_half, w_all, d_first_in)
    d_in_own, small = barrier((d_in_own, small))
    for axis in ("hc", "hx", "own"):
        small = small + swap(small, axis)
    bit = 1
    while bit < seqs:
        small = small + swap(small, "sq", bit)
        bit *= 2
    d_inputs = lax.all_to_all(
        d_in_own.reshape(seqs, share, width), "sq", 0, 0, tiled=True
    ).astype(F32)
    both = total(both_got)
    wide = both.shape[1] // 2
    down_sum = both[:, : wide - SIDE]
    up_sum = both[:, wide : 2 * wide - SIDE]
    out_sum = jnp.concatenate([both[:, wide - SIDE : wide], both[:, 2 * wide - SIDE :]], 1)[:, :head_cols]
    qkv_sum = total(grad_got).reshape(rows, 3, head_cols).transpose(1, 0, 2)
    if near:
        parts = []
        for i in range(seqs):
            part = result_got[0]
            for s in range(1, seqs):
                part = jnp.where((i + s) % seqs == sq, result_got[s], part)
            parts.append(part)
        result = jnp.stack(parts)
    else:
        result = jnp.stack(result_got)

    obias_sum = small[: 2 * width].reshape(2, width)
    gain_sum = small[2 * width : 4 * width].reshape(2, width)
    shift_sum = small[4 * width : 6 * width].reshape(2, width)
    bup_sum = small[6 * width : -2 * width]
    bqv_sum = small[-2 * width :].reshape(2, width)

    entropy = jnp.stack(
        [
            jnp.where(own == 0, ent_seg[0], ent_got),
            ent_seg[2],
            jnp.where(own == 0, ent_got, ent_seg[1]),
        ]
    )
    return (
        result.astype(F32),
        d_inputs,
        qkv_sum,
        bqv_sum,
        out_sum.T,
        obias_sum,
        up_sum,
        bup_sum,
        down_sum.T,
        gain_sum,
        shift_sum,
        entropy,
        occupancy,
    )


def solution(mesh):
    seq, head = (mesh.shape["seq"], mesh.shape["head"])
    fine = Mesh(
        mesh.devices.reshape(seq // OWN, OWN, 2, head // 2), ("sq", "own", "hx", "hc")
    )
    both = SEQ + HEAD
    placed = (
        P(None, SEQ, None),
        P(None, None, HEAD),
        P(None, HEAD),
        P(HEAD, None),
        P(),
        P(None, HEAD),
        P(HEAD),
        P(HEAD, None),
        P(),
        P(),
        P(None, both, None),
        P(None, HEAD, None),
        P(None, HEAD, None),
        P(),
    )
    return jax.shard_map(
        per_device,
        mesh=fine,
        in_specs=placed,
        out_specs=(
            P(None, both, None),
            P(None, both, None),
            P(None, SEQ, HEAD),
            P(),
            P(HEAD, SEQ),
            P(),
            P(SEQ, HEAD),
            P(),
            P(HEAD, SEQ),
            P(),
            P(),
            P(HEAD, SEQ),
            P(HEAD, SEQ),
        ),
        check_vma=False,
    )
```

```python
import functools

import jax
import jax.numpy as jnp
from jax import lax
from jax.experimental import pallas as pl
from jax.experimental.pallas import tpu as pltpu
from jax.sharding import Mesh
from jax.sharding import PartitionSpec as P

DH = 64
FF = 3072
CLUSTER = 128
LENGTH = 4096
TOK_DEV = 2048
OWN = LENGTH // TOK_DEV
EPS = 1e-06
PLANE = ("own", "hx", "hc")
HEAD = ("hx", "hc")
SEQ = ("sq", "own")
CHUNK = 512
STEPS = 3 * TOK_DEV // CHUNK
FULL_STEPS = 2 * TOK_DEV // CHUNK
GROUPS = CHUNK // CLUSTER
BF = jnp.bfloat16
F32 = jnp.float32
VMEM = 56 * 1024 * 1024
SIDE = 128


def cost(micros):
    return pl.CostEstimate(flops=micros * 10**9, transcendentals=0, bytes_accessed=micros * 10**6)


def nn(a, b):
    return lax.dot_general(a, b, (((1,), (0,)), ((), ())), preferred_element_type=F32)


def nt(a, b):
    return lax.dot_general(a, b, (((1,), (1,)), ((), ())), preferred_element_type=F32)


def tn(a, b):
    return lax.dot_general(a, b, (((0,), (0,)), ((), ())), preferred_element_type=F32)


def columns(count, body):
    def at(n, carry):
        body(pl.ds(pl.multiple_of(n * 256, 256), 256))
        return carry

    lax.fori_loop(0, count // 256, at, 0)


def clusters(body):
    def at(pair, carry):
        for j in range(2):
            c = 2 * pair + j
            body(c, pl.ds(pl.multiple_of(c * CLUSTER, CLUSTER), CLUSTER))
        return carry

    lax.fori_loop(0, GROUPS // 2, at, 0)


def log2(n):
    return n.bit_length() - 1


def prepare_body(
    block_len,
    heads,
    here_ref,
    q_ref,
    k_ref,
    slots_ref,
    masked_ref,
    pq_ref,
    pk_ref,
    pqr_ref,
    pkr_ref,
    mask_ref,
    listed_ref,
):
    share = block_len // heads

    def place(pos, size):
        block = pos >> log2(block_len)
        rest = pos & (block_len - 1)
        device = (block & (OWN - 1)) * heads + (rest >> log2(share))
        token = (block >> log2(OWN)) * share + (rest & (share - 1))
        return ((token >> log2(size)) << log2(size * OWN * heads)) + device * size + (token & (size - 1))

    for pos_ref, col_ref, row_ref, size in (
        (q_ref, pq_ref, pqr_ref, 128),
        (k_ref, pk_ref, pkr_ref, 256),
    ):

        def chunk(c, carry):
            row = place(pos_ref[c], size)
            row_ref[c] = row
            col_ref[c] = jnp.broadcast_to(row, (8, CHUNK)).T[:, :1]
            return carry

        lax.fori_loop(0, pos_ref.shape[0], chunk, 0)
    token = lax.broadcasted_iota(jnp.int32, mask_ref.shape, 0)
    own_pos = (
        (((token >> log2(share)) * OWN + here_ref[0]) << log2(block_len))
        + here_ref[1] * share
        + (token & (share - 1))
    )
    mask_ref[...] = jnp.max((own_pos == masked_ref[...]).astype(F32), 1, keepdims=True)
    masked_col = jnp.broadcast_to(masked_ref[...], (8, masked_ref.shape[1])).T[:, :1]

    def count(c, carry):
        listed_ref[c] = jnp.sum((slots_ref[c] == masked_col).astype(jnp.int32), 0, keepdims=True)
        return carry

    lax.fori_loop(0, slots_ref.shape[0], count, 0)


def prepare(block_len, heads, here, q_pos, k_pos, slots, masked_row, tokens):
    steps = q_pos.shape[0]
    vmem = pl.BlockSpec(memory_space=pltpu.VMEM)
    col = jax.ShapeDtypeStruct((steps, CHUNK, 1), jnp.int32)
    row = jax.ShapeDtypeStruct((steps, 1, CHUNK), jnp.int32)
    return pl.pallas_call(
        functools.partial(prepare_body, block_len, heads),
        in_specs=[pl.BlockSpec(memory_space=pltpu.SMEM), vmem, vmem, vmem, vmem],
        out_specs=[vmem] * 6,
        out_shape=[
            col,
            col,
            row,
            row,
            jax.ShapeDtypeStruct((tokens, 1), F32),
            jax.ShapeDtypeStruct(slots.shape, jnp.int32),
        ],
        compiler_params=pltpu.CompilerParams(vmem_limit_bytes=VMEM),
        name="prepare",
        cost_estimate=cost(1),
    )(here, q_pos, k_pos, slots, masked_row)


def plus(a, b):
    return (a.astype(F32) + b.astype(F32)).astype(BF)


def project_body(x_ref, w_ref, b_ref, tq_ref, tkv_ref):
    y = (nn(x_ref[...], w_ref[...]) + b_ref[...]).astype(BF)
    for t in range(2):
        for lo in range(4):
            tq_ref[t, :, lo * DH : (lo + 1) * DH] = y[
                lo * 128 : (lo + 1) * 128, t * DH : (t + 1) * DH
            ]
        for lo in range(2):
            tkv_ref[t, :, lo * 128 : (lo + 1) * 128] = y[
                lo * 256 : (lo + 1) * 256, (t + 1) * 128 : (t + 2) * 128
            ]


def project(x_all, w_sel, b_sel):
    blocks = x_all.shape[0] // 512
    width = x_all.shape[1]
    return pl.pallas_call(
        project_body,
        grid=(blocks,),
        in_specs=[
            pl.BlockSpec((512, width), lambda j: (j, 0)),
            pl.BlockSpec((width, 384), lambda j: (0, 0)),
            pl.BlockSpec((1, 384), lambda j: (0, 0)),
        ],
        out_specs=[
            pl.BlockSpec((2, 128, 256), lambda j: (0, j, 0)),
            pl.BlockSpec((2, 256, 256), lambda j: (0, j, 0)),
        ],
        out_shape=[
            jax.ShapeDtypeStruct((2, 1024, 256), BF),
            jax.ShapeDtypeStruct((2, 2048, 256), BF),
        ],
        compiler_params=pltpu.CompilerParams(vmem_limit_bytes=VMEM),
        name="project",
        cost_estimate=cost(1),
    )(x_all, w_sel, b_sel)


def hot_rows(col, count):
    lane = lax.broadcasted_iota(jnp.int32, (1, count), 1).astype(jnp.int16)
    shape = (col.shape[0], count)
    same = jnp.broadcast_to(lane, shape) == jnp.broadcast_to(col.astype(jnp.int16), shape)
    return jnp.where(same, jnp.ones((), BF), jnp.zeros((), BF))


def hot_cols(row, count):
    place = lax.broadcasted_iota(jnp.int32, (count, 1), 0).astype(jnp.int16)
    shape = (count, row.shape[1])
    same = jnp.broadcast_to(place, shape) == jnp.broadcast_to(row.astype(jnp.int16), shape)
    return jnp.where(same, jnp.ones((), BF), jnp.zeros((), BF))


def take_quarter(table, place):
    wide = nn(hot_rows(place & 1023, 1024), table)
    lane = lax.broadcasted_iota(jnp.int32, wide.shape, 1)
    wide = jnp.where((lane >> 6) == (place >> 10), wide, 0.0)
    half = wide[:, :128] + wide[:, 128:]
    return half + pltpu.roll(half, 64, 1)


def take_half(table, place):
    wide = nn(hot_rows(place & 2047, 2048), table)
    return jnp.where((place >> 11) == 1, wide[:, 128:], wide[:, :128])


def spread_quarter(twice, place):
    wide = jnp.concatenate([twice, twice], 1)
    lane = lax.broadcasted_iota(jnp.int32, wide.shape, 1)
    return jnp.where((lane >> 6) == (place >> 10), wide, 0.0).astype(BF)


def spread_half(rows, place):
    upper = (place >> 11) == 1
    return jnp.concatenate(
        [jnp.where(upper, 0.0, rows), jnp.where(upper, rows, 0.0)], 1
    ).astype(BF)


def low_lanes(shape):
    return lax.broadcasted_iota(jnp.int32, shape, 1) < DH


def attend_body(
    pq_ref, pk_ref, pqr_ref, tq_ref, tkv_ref, q_ref, kv_ref, lt_ref, ent_ref, out_ref, acc_ref, got_ref
):
    step = pl.program_id(0)
    place_q = pq_ref[0]
    twice = take_quarter(tq_ref[0], place_q)
    q_all = jnp.where(low_lanes(twice.shape), twice, 0.0).astype(BF)
    kv_all = take_half(tkv_ref[0], pk_ref[0]).astype(BF)
    q_ref[0] = q_all
    kv_ref[0] = kv_all

    def cluster(c, rows):
        kv = kv_ref[0, rows, :]
        scores = nt(q_ref[0, rows, :], kv) * (DH**-0.5)
        top = jnp.max(scores, 1, keepdims=True)
        total = jnp.sum(jnp.exp(scores - top), 1, keepdims=True)
        log_total = top + jnp.log(total)
        soft = jnp.exp(scores - log_total)
        inner = jnp.sum(soft * scores, 1, keepdims=True)
        ent_ref[0, pl.ds(c, 1), :] = jnp.broadcast_to(
            jnp.sum(log_total - inner, 0, keepdims=True) / CLUSTER, (1, 128)
        )
        lt_ref[0, rows, :] = log_total
        got = nn(soft.astype(BF), kv)
        got_ref[rows, :] = jnp.where(low_lanes(got.shape), pltpu.roll(got, 64, 1), got)

    clusters(cluster)
    spread = spread_quarter(got_ref[...], place_q)

    @pl.when((step == 0) | (step == FULL_STEPS))
    def _():
        acc_ref[...] = jnp.zeros(acc_ref.shape, F32)

    acc_ref[...] += nn(hot_cols(pqr_ref[0] & 1023, 1024), spread)

    @pl.when((step == FULL_STEPS - 1) | (step == STEPS - 1))
    def _():
        rows = pl.ds(pl.multiple_of(128 * table_of(step), 128), 128)
        for j in range(out_ref.shape[0]):
            out_ref[j, rows, :] = acc_ref[j * 128 : (j + 1) * 128, :].astype(BF)


def table_of(g):
    return g // FULL_STEPS


def once(*shape):
    return pl.BlockSpec(shape, lambda g: (0,) * len(shape))


def attend(places, tq, tkv):
    pq_col, pk_col, pq_row, _ = places
    chunk = lambda width: pl.BlockSpec((1, CHUNK, width), lambda g: (g, 0, 0))
    table = lambda rows: pl.BlockSpec((1, rows, 256), lambda g: (table_of(g), 0, 0))
    return pl.pallas_call(
        attend_body,
        grid=(STEPS,),
        in_specs=[
            chunk(1),
            chunk(1),
            pl.BlockSpec((1, 1, CHUNK), lambda g: (g, 0, 0)),
            table(1024),
            table(2048),
        ],
        out_specs=[
            chunk(128),
            chunk(128),
            chunk(1),
            pl.BlockSpec((1, 8, 128), lambda g: (g, 0, 0)),
            once(8, 256, 256),
        ],
        out_shape=[
            jax.ShapeDtypeStruct((STEPS, CHUNK, 128), BF),
            jax.ShapeDtypeStruct((STEPS, CHUNK, 128), BF),
            jax.ShapeDtypeStruct((STEPS, CHUNK, 1), F32),
            jax.ShapeDtypeStruct((STEPS, 8, 128), F32),
            jax.ShapeDtypeStruct((8, 256, 256), BF),
        ],
        scratch_shapes=[pltpu.VMEM((1024, 256), F32), pltpu.VMEM((CHUNK, 128), F32)],
        compiler_params=pltpu.CompilerParams(vmem_limit_bytes=VMEM),
        name="attend",
        cost_estimate=cost(1),
    )(pq_col, pk_col, pq_row, tq, tkv)


def attend_back_body(
    pq_ref, pk_ref, pqr_ref, pkr_ref, td_ref, q_ref, kv_ref, lt_ref, out_ref, accq, acckv, d_ref, gq_ref, gkv_ref
):
    step = pl.program_id(0)
    place_q = pq_ref[0]
    twice = take_quarter(td_ref[...], place_q)
    d_ref[...] = jnp.where(low_lanes(twice.shape), 0.0, twice).astype(BF)

    def cluster(c, rows):
        q = q_ref[0, rows, :]
        kv = kv_ref[0, rows, :]
        d = d_ref[rows, :]
        scores = nt(q, kv) * (DH**-0.5)
        soft = jnp.exp(scores - lt_ref[0, rows, :])
        d_soft = nt(d, kv)
        d_scores = soft * (d_soft - jnp.sum(soft * d_soft, 1, keepdims=True))
        d_raw = (d_scores * (DH**-0.5)).astype(BF)
        got = nn(d_raw, kv)
        gq_ref[rows, :] = jnp.where(low_lanes(got.shape), got, pltpu.roll(got, 64, 1))
        gkv_ref[rows, :] = tn(d_raw, q) + tn(soft.astype(BF), d)

    clusters(cluster)

    @pl.when(step == 0)
    def _():
        accq[...] = jnp.zeros(accq.shape, F32)
        acckv[...] = jnp.zeros(acckv.shape, F32)

    accq[...] += nn(hot_cols(pqr_ref[0] & 1023, 1024), spread_quarter(gq_ref[...], place_q))
    acckv[...] += nn(hot_cols(pkr_ref[0] & 2047, 2048), spread_half(gkv_ref[...], pk_ref[0]))

    @pl.when(step == pl.num_programs(0) - 1)
    def _():
        for j in range(out_ref.shape[0]):
            out_ref[j, :128, :] = accq[j * 128 : (j + 1) * 128, :].astype(BF)
            out_ref[j, 128:, :] = acckv[j * 256 : (j + 1) * 256, :].astype(BF)


def attend_back(places, start, steps, td, q_all, kv_all, log_total):
    pq_col, pk_col, pq_row, pk_row = places
    chunk = lambda width: pl.BlockSpec((1, CHUNK, width), lambda g: (g + start, 0, 0))
    col = chunk(1)
    line = pl.BlockSpec((1, 1, CHUNK), lambda g: (g + start, 0, 0))
    return pl.pallas_call(
        attend_back_body,
        grid=(steps,),
        in_specs=[
            col,
            col,
            line,
            line,
            once(1024, 256),
            chunk(128),
            chunk(128),
            chunk(1),
        ],
        out_specs=once(8, 384, 256),
        out_shape=jax.ShapeDtypeStruct((8, 384, 256), BF),
        scratch_shapes=[
            pltpu.VMEM((1024, 256), F32),
            pltpu.VMEM((2048, 256), F32),
            pltpu.VMEM((CHUNK, 128), BF),
            pltpu.VMEM((CHUNK, 128), F32),
            pltpu.VMEM((CHUNK, 128), F32),
        ],
        compiler_params=pltpu.CompilerParams(vmem_limit_bytes=VMEM),
        name="attend_back",
        cost_estimate=cost(1),
    )(pq_col, pk_col, pq_row, pk_row, td, q_all, kv_all, log_total)


def project_grad_body(x_ref, full_ref, half_ref, grad_ref, sum_ref, acc_ref):
    j = pl.program_id(0)
    quarters = []
    for lo in range(4):
        cols = slice(lo * DH, (lo + 1) * DH)
        quarters.append(jnp.concatenate([full_ref[0, :128, cols], half_ref[0, :128, cols]], 1))
    parts = [jnp.concatenate(quarters, 0)]
    for ref in (full_ref, half_ref):
        parts.append(jnp.concatenate([ref[0, 128:, :128], ref[0, 128:, 128:]], 0))
    rows = jnp.concatenate(parts, 1)
    part = tn(x_ref[...], rows)
    sums = jnp.sum(rows.astype(F32), 0, keepdims=True)

    @pl.when(j == 0)
    def _():
        acc_ref[...] = part
        sum_ref[...] = sums

    @pl.when(j > 0)
    def _():
        acc_ref[...] += part
        sum_ref[...] += sums

    @pl.when(j == pl.num_programs(0) - 1)
    def _():
        grad_ref[...] = acc_ref[...].astype(BF)


def project_grad(x_all, full, half):
    tokens, width = x_all.shape
    rows = pl.BlockSpec((1, 384, 256), lambda j: (j, 0, 0))
    return pl.pallas_call(
        project_grad_body,
        grid=(tokens // 512,),
        in_specs=[pl.BlockSpec((512, width), lambda j: (j, 0)), rows, rows],
        out_specs=[once(width, 384), once(1, 384)],
        out_shape=[
            jax.ShapeDtypeStruct((width, 384), BF),
            jax.ShapeDtypeStruct((1, 384), F32),
        ],
        scratch_shapes=[pltpu.VMEM((width, 384), F32)],
        compiler_params=pltpu.CompilerParams(vmem_limit_bytes=VMEM),
        name="project_grad",
        cost_estimate=cost(1),
    )(x_all, full, half)


def project_back_body(heads, full_ref, half_ref, w_ref, dfi_ref, dx_ref, q_ref, kv_ref, wq_ref, wkv_ref):
    for hd in range(heads):
        wq_ref[hd * 3 * DH : (hd + 1) * 3 * DH, :] = w_ref[hd, : 3 * DH, :]
        wkv_ref[hd * 6 * DH : (hd + 1) * 6 * DH, :] = w_ref[hd, 3 * DH :, :]
        for h in range(3):
            if h == 1:
                piece = (half_ref[hd].astype(F32) + half_ref[heads + hd].astype(F32)).astype(BF)
            else:
                piece = full_ref[(h // 2) * heads + hd]
            n = hd * 3 + h
            for lo in range(4):
                q_ref[lo * 128 : (lo + 1) * 128, n * DH : (n + 1) * DH] = piece[
                    :128, lo * DH : (lo + 1) * DH
                ]
            for lo in range(2):
                kv_ref[lo * 256 : (lo + 1) * 256, n * 128 : (n + 1) * 128] = piece[
                    128:, lo * 128 : (lo + 1) * 128
                ]

    def back(cols):
        dx = dfi_ref[:, cols] + nn(q_ref[...], wq_ref[:, cols]) + nn(kv_ref[...], wkv_ref[:, cols])
        dx_ref[:, cols] = dx.astype(BF)

    columns(dx_ref.shape[1], back)


def project_back(full, half, w_all, d_first_in):
    tokens, width = d_first_in.shape
    heads = w_all.shape[0]
    return pl.pallas_call(
        functools.partial(project_back_body, heads),
        out_shape=jax.ShapeDtypeStruct((tokens, width), BF),
        scratch_shapes=[
            pltpu.VMEM((tokens, width), BF),
            pltpu.VMEM((tokens, 2 * width), BF),
            pltpu.VMEM((width, width), BF),
            pltpu.VMEM((2 * width, width), BF),
        ],
        compiler_params=pltpu.CompilerParams(vmem_limit_bytes=VMEM),
        name="project_back",
        cost_estimate=cost(1),
    )(full, half, w_all, d_first_in)


def erf_parts(u):
    mag = jnp.abs(u) * (0.5**0.5)
    bell = jnp.exp(-(mag * mag))
    t = 1.0 / (1.0 + 0.3275911 * mag)
    poly = t * (
        0.254829592
        + t * (-0.284496736 + t * (1.421413741 + t * (-1.453152027 + t * 1.061405429)))
    )
    tail = 0.5 * poly * bell
    return jnp.where(u < 0, tail, 1.0 - tail), bell * ((2 * jnp.pi) ** -0.5)


def row_mean(x):
    return jnp.mean(x, 1, keepdims=True)


def column_sum(x):
    return jnp.sum(x, 0, keepdims=True)


def middle_body(
    heads,
    hc_ref,
    got_ref,
    x_ref,
    dout_ref,
    mask_ref,
    wo_ref,
    up_ref,
    down_ref,
    bias_ref,
    gain_ref,
    shift_ref,
    res_ref,
    send_full_ref,
    send_half_ref,
    dfi_ref,
    down_sent_ref,
    down_kept_ref,
    up_sent_ref,
    up_kept_ref,
    sums_ref,
    gbup_ref,
    rows_ref,
    n1_ref,
    inv1_ref,
    low_ref,
    low_t_ref,
    acc_ref,
    hid_ref,
    slope_ref,
    dlow_ref,
    dlow_t_ref,
    dup_ref,
    rows_back_ref,
):
    step = pl.program_id(0)
    tokens, width = x_ref.shape
    hid = up_ref.shape[2]
    size = 64

    def tiles(body, carry):
        def at(i, carry):
            return body(pl.ds(pl.multiple_of(i * size, size), size), carry)

        return lax.fori_loop(0, tokens // size, at, carry)

    @pl.when(step == 0)
    def _():
        for hd in range(heads):
            rows_ref[:, hd * 256 + 3 * DH : (hd + 1) * 256] = jnp.zeros((tokens, DH), BF)
            for h in range(3):
                if h == 1:
                    piece = plus(got_ref[hd, 128:, :], got_ref[heads + hd, 128:, :])
                else:
                    piece = got_ref[hd + (h // 2) * heads, :128, :]
                col = hd * 256 + h * DH
                for lo in range(4):
                    rows_ref[lo * 128 : (lo + 1) * 128, col : col + DH] = piece[
                        :, lo * DH : (lo + 1) * DH
                    ]

        def project(cols):
            acc_ref[:, cols] = nn(rows_ref[...], wo_ref[:, cols])

        columns(width, project)

        def norm(r, carry):
            v = x_ref[r, :].astype(F32) + acc_ref[r, :] + bias_ref[0:1, :]
            centred = v - row_mean(v)
            inv = lax.rsqrt(row_mean(centred * centred) + EPS)
            normed = centred * inv
            first = normed * gain_ref[0:1, :] + shift_ref[0:1, :]
            n1_ref[r, :] = normed
            inv1_ref[r, :] = inv
            low_ref[r, :] = first.astype(BF)
            acc_ref[r, :] = first + bias_ref[1:2, :]
            return carry

        tiles(norm, 0)
        low_t_ref[...] = low_ref[...].T

    @pl.when(step < heads)
    def _():
        at_bias = pl.multiple_of(chunk_at(step, heads, hc_ref[0]) * 256 + 3 * DH, DH)

        def upper(cols):
            bup = wo_ref[pl.ds(at_bias, 16), cols][:1].astype(F32)
            u = nn(low_ref[...], up_ref[0, :, cols]) + bup
            phi, bell = erf_parts(u)
            hid_ref[step, :, cols] = (u * phi).astype(BF)
            slope_ref[step, :, cols] = phi + u * bell

        columns(hid, upper)
        acc_ref[...] += nn(hid_ref[step], down_ref[0])

    @pl.when(step == heads)
    def _():
        zero = jnp.zeros((1, width), F32)

        def norm(r, carry):
            g_sum, s_sum, b_sum = carry
            v = acc_ref[r, :]
            centred = v - row_mean(v)
            inv = lax.rsqrt(row_mean(centred * centred) + EPS)
            normed = centred * inv
            res_ref[r, :] = (normed * gain_ref[1:2, :] + shift_ref[1:2, :]).astype(BF)
            seed = dout_ref[r, :].astype(F32) * mask_ref[r, :]
            e = seed * gain_ref[1:2, :]
            d = inv * (e - row_mean(e) - normed * row_mean(e * normed))
            acc_ref[r, :] = d
            dlow_ref[r, :] = d.astype(BF)
            return g_sum + column_sum(seed * normed), s_sum + column_sum(seed), b_sum + column_sum(d)

        g_sum, s_sum, b_sum = tiles(norm, (zero, zero, zero))
        sums_ref[1:2, :] = b_sum
        sums_ref[3:4, :] = g_sum
        sums_ref[5:6, :] = s_sum
        dlow_t_ref[...] = dlow_ref[...].T

    @pl.when(step >= heads)
    def _():
        c = step - heads
        for n in range(0, hid, 256):
            cols = slice(n, n + 256)
            d_up = nt(dlow_ref[...], down_ref[0, cols, :]) * slope_ref[c, :, cols]
            gbup_ref[0, :, cols] = column_sum(d_up)
            dup_ref[:, cols] = d_up.astype(BF)

        acc_ref[...] += nt(dup_ref[...], up_ref[0])

        for there, k, down_to, up_to in (
            (c < heads // 2, c, down_sent_ref, up_sent_ref),
            (c >= heads // 2, c - heads // 2, down_kept_ref, up_kept_ref),
        ):

            @pl.when(there)
            def _():
                def products(cols):
                    down_to[k, :, cols] = nn(dlow_t_ref[...], hid_ref[c, :, cols]).astype(BF)
                    up_to[k, :, cols] = nn(low_t_ref[...], dup_ref[:, cols]).astype(BF)

                columns(hid, products)

    @pl.when(step == 2 * heads - 1)
    def _():
        zero = jnp.zeros((1, width), F32)

        def norm(r, carry):
            g_sum, s_sum, b_sum = carry
            d_first = acc_ref[r, :]
            normed = n1_ref[r, :]
            e = d_first * gain_ref[0:1, :]
            d = inv1_ref[r, :] * (e - row_mean(e) - normed * row_mean(e * normed))
            dfi_ref[r, :] = d
            dlow_ref[r, :] = d.astype(BF)
            return (
                g_sum + column_sum(d_first * normed),
                s_sum + column_sum(d_first),
                b_sum + column_sum(d),
            )

        g_sum, s_sum, b_sum = tiles(norm, (zero, zero, zero))
        sums_ref[0:1, :] = b_sum
        sums_ref[2:3, :] = g_sum
        sums_ref[4:5, :] = s_sum
        dlow_t_ref[...] = dlow_ref[...].T

        def back(cols):
            rows_back_ref[:, cols] = nt(dlow_ref[...], wo_ref[cols, :]).astype(BF)

        columns(heads * 256, back)
        for lo in range(4):
            for hd in range(heads):
                for h in range(3):
                    col = hd * 256 + h * DH
                    piece = rows_back_ref[lo * 128 : (lo + 1) * 128, col : col + DH]
                    lanes = slice(lo * DH, (lo + 1) * DH)
                    if h == 1:
                        send_half_ref[hd, :, lanes] = piece
                        send_half_ref[heads + hd, :, lanes] = piece
                    else:
                        send_full_ref[hd + (h // 2) * heads, :, lanes] = piece

        def grad(k, carry):
            at = pl.multiple_of(chunk_at(k, heads, hc_ref[0]) * 256, 256)
            whole = nn(dlow_t_ref[...], rows_ref[:, pl.ds(at, 256)]).astype(BF)

            @pl.when(k < heads // 2)
            def _():
                down_sent_ref[k, :, hid:] = whole[:, :SIDE]
                up_sent_ref[k, :, hid:] = whole[:, SIDE:]

            @pl.when(k >= heads // 2)
            def _():
                down_kept_ref[k - heads // 2, :, hid:] = whole[:, :SIDE]
                up_kept_ref[k - heads // 2, :, hid:] = whole[:, SIDE:]

            return carry

        lax.fori_loop(0, heads, grad, 0)


def chunk_at(k, heads, hc):
    pairs = heads // 2
    return jnp.where(k < pairs, 2 * k + 1 - hc, 2 * (k - pairs) + hc)


def middle(hc, got, x_own, d_own, mask_col, wo, ff_all, bias, gain, shift):
    heads, width, hid = ff_all.shape[0], ff_all.shape[2], ff_all.shape[1] - ff_all.shape[2]
    pairs = heads // 2
    tokens = x_own.shape[0]

    def at(k, hc_ref):
        return chunk_at(k, heads, hc_ref[0])

    once = lambda *shape: pl.BlockSpec(shape, lambda g, c: (0,) * len(shape))
    by_chunk = lambda part, *shape: pl.BlockSpec(shape, lambda g, c: (at(g % heads, c), part, 0))
    late = lambda *shape: pl.BlockSpec(shape, lambda g, c: (at(jnp.maximum(g - heads, 0), c), 0, 0))
    grads = pl.BlockSpec(
        (pairs, width, hid + SIDE), lambda g, c: (0, 0, 0), pipeline_mode=pl.Buffered(1)
    )
    big = jax.ShapeDtypeStruct((pairs, width, hid + SIDE), BF)
    table = jax.ShapeDtypeStruct((OWN * heads, 128, 256), BF)
    return pl.pallas_call(
        functools.partial(middle_body, heads),
        grid_spec=pltpu.PrefetchScalarGridSpec(
            num_scalar_prefetch=1,
            grid=(2 * heads,),
            in_specs=[
                once(OWN * heads, 256, 256),
                once(tokens, width),
                once(tokens, width),
                once(tokens, 1),
                once(heads * 256, width),
                by_chunk(0, 1, width, hid),
                by_chunk(1, 1, hid, width),
                once(2, width),
                once(2, width),
                once(2, width),
            ],
            out_specs=[
                once(tokens, width),
                once(OWN * heads, 128, 256),
                once(OWN * heads, 128, 256),
                once(tokens, width),
                grads,
                grads,
                grads,
                grads,
                once(8, width),
                late(1, 1, hid),
            ],
            scratch_shapes=[
                pltpu.VMEM((tokens, heads * 256), BF),
                pltpu.VMEM((tokens, width), F32),
                pltpu.VMEM((tokens, 1), F32),
                pltpu.VMEM((tokens, width), BF),
                pltpu.VMEM((width, tokens), BF),
                pltpu.VMEM((tokens, width), F32),
                pltpu.VMEM((heads, tokens, hid), BF),
                pltpu.VMEM((heads, tokens, hid), F32),
                pltpu.VMEM((tokens, width), BF),
                pltpu.VMEM((width, tokens), BF),
                pltpu.VMEM((tokens, hid), BF),
                pltpu.VMEM((tokens, heads * 256), BF),
            ],
        ),
        out_shape=[
            jax.ShapeDtypeStruct((tokens, width), BF),
            table,
            table,
            jax.ShapeDtypeStruct((tokens, width), F32),
            big,
            big,
            big,
            big,
            jax.ShapeDtypeStruct((8, width), F32),
            jax.ShapeDtypeStruct((heads, 1, hid), F32),
        ],
        compiler_params=pltpu.CompilerParams(vmem_limit_bytes=VMEM),
        name="middle",
        cost_estimate=cost(1),
    )(hc, got, x_own, d_own, mask_col, wo, ff_all, ff_all, bias, gain, shift)


def swap(x, axis, bit=1):
    size = lax.axis_size(axis)
    return lax.ppermute(x, axis, [(i, i ^ bit) for i in range(size)])


def pick(x, index, axis=0):
    return lax.dynamic_index_in_dim(x, index, axis, keepdims=False)


def fold(kept, came, index, axis):
    return tuple(plus(pick(kept, i, axis), pick(came, i, axis)) for i in (1 - index, index))


def total(pieces):
    return sum(p.astype(F32) for p in pieces)


barrier = lax.optimization_barrier


def per_device(
    inputs,
    w_qkv,
    b_qv,
    w_out,
    out_bias,
    w_up,
    b_up,
    w_down,
    norm_gain,
    norm_shift,
    d_out,
    q_perm,
    k_perm,
    masked,
):
    seqs, block_len, width = inputs.shape
    heads = lax.axis_size("hx") * lax.axis_size("hc")
    plane = OWN * heads
    share = block_len // heads
    tokens = seqs * share
    length = lax.axis_size("sq") * OWN
    sq = lax.axis_index("sq")
    own = lax.axis_index("own")
    hx = lax.axis_index("hx")
    hc = lax.axis_index("hc")
    head = hx * lax.axis_size("hc") + hc
    head_cols = q_perm.shape[1] * DH

    pad = jnp.zeros((256 - head_cols - 1, width), BF)
    with_bias = jnp.concatenate([w_out, b_up[None], pad], 0)
    mine = lax.dynamic_slice_in_dim(inputs, head * share, share, 1)
    x_own = lax.all_to_all(mine, "sq", 0, 0, tiled=True).reshape(tokens, width)
    out_bias_all = lax.all_gather(with_bias, HEAD, axis=0, tiled=False)
    x_own, out_bias_all, d_out, q_perm, k_perm, w_qkv = barrier(
        (x_own, out_bias_all, d_out, q_perm, k_perm, w_qkv)
    )
    x_all = lax.all_gather(x_own, PLANE, axis=0, tiled=True)
    d_own = lax.all_to_all(d_out, "sq", 0, 0, tiled=True).reshape(tokens, width)

    def positions(perm):
        mine = pick(perm, sq)
        full = pick(mine, 2 * own).reshape(2, TOK_DEV)
        half = lax.dynamic_slice_in_dim(mine[1], own * TOK_DEV, TOK_DEV, 0)
        return jnp.concatenate([full, half[None]], 0).reshape(-1, 1, CHUNK)

    masked_row = pick(masked, sq)
    *places, mask_col, listed = prepare(
        block_len,
        heads,
        jnp.stack([own, head]).astype(jnp.int32),
        positions(q_perm),
        positions(k_perm),
        lax.dynamic_slice_in_dim(pick(q_perm, sq), own * TOK_DEV, TOK_DEV, 1).reshape(-1, 1, CHUNK),
        masked_row[None],
        tokens,
    )

    def two_heads(x):
        full = lax.dynamic_slice_in_dim(x, own * 2 * DH, DH, x.ndim - 1)
        return full, x[..., DH : 2 * DH]

    w_full, w_half = two_heads(w_qkv)
    w_sel = jnp.concatenate(
        [w_full[0], w_half[0], w_full[1], w_full[2], w_half[1], w_half[2]], 1
    )
    b_full, b_half = two_heads(b_qv.astype(F32))
    none = jnp.zeros((DH,), F32)
    b_sel = jnp.concatenate([b_full[0], b_half[0], none, b_full[1], none, b_half[1]])[None]
    w_rows = jnp.concatenate(
        [w_qkv[0]]
        + [w_qkv[i, :, h * DH : (h + 1) * DH] for h in range(3) for i in (1, 2)],
        1,
    ).T
    ff = jnp.concatenate([w_up, w_down], 0)

    occupancy = jnp.sum(listed.reshape(q_perm.shape[1], TOK_DEV // CLUSTER, CLUSTER), -1)
    bias = out_bias.astype(F32)
    out_all = out_bias_all.reshape(heads * 256, width)

    (
        x_all,
        d_own,
        places,
        w_sel,
        b_sel,
        w_rows,
        mask_col,
        occupancy,
        bias,
        out_all,
        ff,
    ) = barrier(
        (
            x_all,
            d_own,
            places,
            w_sel,
            b_sel,
            w_rows,
            mask_col,
            occupancy,
            bias,
            out_all,
            ff,
        )
    )
    ff_all = lax.all_gather(ff, HEAD, axis=0, tiled=False)

    tq, tkv = project(x_all, w_sel, b_sel)
    *kept, ent, done = attend(places, tq, tkv)
    got = lax.all_to_all(done, PLANE, 0, 0, tiled=True)
    ent_seg = ent[:, :GROUPS, 0].reshape(3, TOK_DEV // CLUSTER)
    ent_got = swap(jnp.where(own == 0, ent_seg[1], ent_seg[0]), "own")
    ff_all, w_rows, got = barrier((ff_all, w_rows, got))
    w_all = lax.all_gather(w_rows, HEAD, axis=0, tiled=False)
    (
        result_own,
        send_full,
        send_half,
        d_first_in,
        down_sent,
        down_kept,
        up_sent,
        up_kept,
        sums_own,
        grad_bup,
    ) = middle(
        hc[None],
        got,
        x_own,
        d_own,
        mask_col,
        out_all,
        ff_all,
        bias,
        norm_gain,
        norm_shift,
    )
    rows = width // length
    near = seqs <= 4

    def shifted(pieces):
        return [pieces[0]] + [
            lax.ppermute(p, "sq", [(i, (i + s) % seqs) for i in range(seqs)])
            for s, p in enumerate(pieces)
            if s > 0
        ]

    def cut_z(x):
        return [pick(x, (sq + s) % seqs) for s in range(seqs)] if near else [x]

    def over_z(pieces):
        if near:
            return shifted(pieces)
        return list(lax.all_to_all(pieces[0], "sq", 0, 0, tiled=True))

    td_full = lax.all_to_all(send_full, PLANE, 0, 0, tiled=True)
    down_came, up_came = swap(down_sent, "hc"), swap(up_sent, "hc")
    result_own = cut_z(result_own.reshape(seqs, share, width))
    cut = lambda x: x.reshape(x.shape[0], length // OWN, OWN, rows, x.shape[-1])
    down_sent, down_kept = fold(cut(down_kept), cut(down_came), hx, 0)
    up_sent, up_kept = fold(cut(up_kept), cut(up_came), own, 2)
    (
        td_full,
        send_half,
        ent_got,
        w_all,
        down_sent,
        down_kept,
        up_sent,
        up_kept,
        result_own,
    ) = barrier(
        (
            td_full,
            send_half,
            ent_got,
            w_all,
            down_sent,
            down_kept,
            up_sent,
            up_kept,
            result_own,
        )
    )
    td_half = lax.all_to_all(send_half, PLANE, 0, 0, tiled=True)
    down_came, up_came = swap(down_sent, "hx"), swap(up_sent, "own")
    result_got = over_z(result_own)
    rows_full = attend_back(places, 0, FULL_STEPS, td_full.reshape(plane * 128, 256), *kept)
    rows_full, td_half, down_came, up_came, result_got = barrier(
        (rows_full, td_half, down_came, up_came, result_got)
    )
    back_full = lax.all_to_all(rows_full, PLANE, 0, 0, tiled=True)
    down_sent, down_kept = fold(down_kept, down_came, own, 1)
    up_sent, up_kept = fold(up_kept, up_came, hx, 0)
    td_half, down_sent, down_kept, up_sent, up_kept = barrier(
        (td_half, down_sent, down_kept, up_sent, up_kept)
    )
    down_came, up_came = swap(down_sent, "own"), swap(up_sent, "hx")
    rows_half = attend_back(
        places, FULL_STEPS, STEPS - FULL_STEPS, td_half.reshape(plane * 128, 256), *kept
    )
    rows_half, back_full = barrier((rows_half, back_full))
    back_half = lax.all_to_all(rows_half, PLANE, 0, 0, tiled=True)
    rows_half, down_came, up_came = barrier((rows_half, down_came, up_came))
    both = cut_z(jnp.concatenate([plus(down_kept, down_came), plus(up_kept, up_came)], 2))
    rows_full, rows_half, both = barrier((rows_full, rows_half, both))
    both_got = over_z(both)
    grad_sel, sum_sel = project_grad(x_all, rows_full, rows_half)

    sums = sum_sel.reshape(6, DH)
    at_full = (jnp.arange(3) == 2 * own)[:, None]
    at_half = (jnp.arange(3) == 1)[:, None]
    at_head = (jnp.arange(heads) == head)[None, :, None, None]
    pair = jnp.stack(
        [jnp.where(at_full, sums[a], 0.0) + jnp.where(at_half, sums[b], 0.0) for a, b in ((0, 1), (3, 5))]
    )
    bqv = jnp.where(at_head, pair[:, None], 0.0)
    small = jnp.concatenate([sums_own[:6].reshape(-1), grad_bup.reshape(-1), bqv.reshape(-1)])
    grad_sel = grad_sel.reshape(length // OWN, OWN, rows, 384)
    grad_sent, grad_kept = pick(grad_sel, 1 - own, 1), pick(grad_sel, own, 1)
    grad_came = swap(grad_sent, "own")
    back_half, grad_came = barrier((back_half, grad_came))
    low = jnp.where(own == 0, grad_kept, grad_came)
    high = jnp.where(own == 0, grad_came, grad_kept)
    shared = plus(grad_kept, grad_came)
    order = [(low, 0), (shared, 1), (high, 0), (low, 2), (shared, 4), (high, 2), (low, 3), (shared, 5), (high, 3)]
    grad_all = cut_z(jnp.concatenate([a[..., c * DH : (c + 1) * DH] for a, c in order], -1))
    back_full, grad_all = barrier((back_full, grad_all))
    grad_got = over_z(grad_all)
    d_in_own = project_back(back_full, back_half, w_all, d_first_in)
    d_in_own, small = barrier((d_in_own, small))
    for axis in ("hc", "hx", "own"):
        small = small + swap(small, axis)
    bit = 1
    while bit < seqs:
        small = small + swap(small, "sq", bit)
        bit *= 2
    d_inputs = lax.all_to_all(
        d_in_own.reshape(seqs, share, width), "sq", 0, 0, tiled=True
    ).astype(F32)
    both = total(both_got)
    wide = both.shape[1] // 2
    down_sum = both[:, : wide - SIDE]
    up_sum = both[:, wide : 2 * wide - SIDE]
    out_sum = jnp.concatenate([both[:, wide - SIDE : wide], both[:, 2 * wide - SIDE :]], 1)[:, :head_cols]
    qkv_sum = total(grad_got).reshape(rows, 3, head_cols).transpose(1, 0, 2)
    if near:
        parts = []
        for i in range(seqs):
            part = result_got[0]
            for s in range(1, seqs):
                part = jnp.where((i + s) % seqs == sq, result_got[s], part)
            parts.append(part)
        result = jnp.stack(parts)
    else:
        result = jnp.stack(result_got)

    obias_sum = small[: 2 * width].reshape(2, width)
    gain_sum = small[2 * width : 4 * width].reshape(2, width)
    shift_sum = small[4 * width : 6 * width].reshape(2, width)
    bup_sum = small[6 * width : -2 * width]
    bqv_sum = small[-2 * width :].reshape(2, width)

    entropy = jnp.stack(
        [
            jnp.where(own == 0, ent_seg[0], ent_got),
            ent_seg[2],
            jnp.where(own == 0, ent_got, ent_seg[1]),
        ]
    )
    return (
        result.astype(F32),
        d_inputs,
        qkv_sum,
        bqv_sum,
        out_sum.T,
        obias_sum,
        up_sum,
        bup_sum,
        down_sum.T,
        gain_sum,
        shift_sum,
        entropy,
        occupancy,
    )


def solution(mesh):
    seq, head = (mesh.shape["seq"], mesh.shape["head"])
    fine = Mesh(
        mesh.devices.reshape(seq // OWN, OWN, 2, head // 2), ("sq", "own", "hx", "hc")
    )
    both = SEQ + HEAD
    placed = (
        P(None, SEQ, None),
        P(None, None, HEAD),
        P(None, HEAD),
        P(HEAD, None),
        P(),
        P(None, HEAD),
        P(HEAD),
        P(HEAD, None),
        P(),
        P(),
        P(None, both, None),
        P(None, HEAD, None),
        P(None, HEAD, None),
        P(),
    )
    return jax.shard_map(
        per_device,
        mesh=fine,
        in_specs=placed,
        out_specs=(
            P(None, both, None),
            P(None, both, None),
            P(None, SEQ, HEAD),
            P(),
            P(HEAD, SEQ),
            P(),
            P(SEQ, HEAD),
            P(),
            P(HEAD, SEQ),
            P(),
            P(),
            P(HEAD, SEQ),
            P(HEAD, SEQ),
        ),
        check_vma=False,
    )
```

```python
import functools

import jax
import jax.numpy as jnp
from jax import lax
from jax.experimental import pallas as pl
from jax.experimental.pallas import tpu as pltpu
from jax.sharding import Mesh
from jax.sharding import PartitionSpec as P

DH = 64
FF = 3072
CLUSTER = 128
LENGTH = 4096
TOK_DEV = 2048
OWN = LENGTH // TOK_DEV
EPS = 1e-06
PLANE = ("own", "hx", "hc")
HEAD = ("hx", "hc")
SEQ = ("sq", "own")
CHUNK = 512
STEPS = 3 * TOK_DEV // CHUNK
FULL_STEPS = 2 * TOK_DEV // CHUNK
GROUPS = CHUNK // CLUSTER
BF = jnp.bfloat16
F32 = jnp.float32
VMEM = 56 * 1024 * 1024
SIDE = 128


def cost(micros):
    return pl.CostEstimate(flops=micros * 10**9, transcendentals=0, bytes_accessed=micros * 10**6)


def nn(a, b):
    return lax.dot_general(a, b, (((1,), (0,)), ((), ())), preferred_element_type=F32)


def nt(a, b):
    return lax.dot_general(a, b, (((1,), (1,)), ((), ())), preferred_element_type=F32)


def tn(a, b):
    return lax.dot_general(a, b, (((0,), (0,)), ((), ())), preferred_element_type=F32)


def columns(count, body):
    def at(n, carry):
        body(pl.ds(pl.multiple_of(n * 256, 256), 256))
        return carry

    lax.fori_loop(0, count // 256, at, 0)


def clusters(body):
    def at(pair, carry):
        for j in range(2):
            c = 2 * pair + j
            body(c, pl.ds(pl.multiple_of(c * CLUSTER, CLUSTER), CLUSTER))
        return carry

    lax.fori_loop(0, GROUPS // 2, at, 0)


def log2(n):
    return n.bit_length() - 1


def prepare_body(
    block_len,
    heads,
    here_ref,
    q_ref,
    k_ref,
    slots_ref,
    masked_ref,
    pq_ref,
    pk_ref,
    pqr_ref,
    pkr_ref,
    mask_ref,
    listed_ref,
):
    share = block_len // heads

    def place(pos, size):
        block = pos >> log2(block_len)
        rest = pos & (block_len - 1)
        device = (block & (OWN - 1)) * heads + (rest >> log2(share))
        token = (block >> log2(OWN)) * share + (rest & (share - 1))
        return ((token >> log2(size)) << log2(size * OWN * heads)) + device * size + (token & (size - 1))

    for pos_ref, col_ref, row_ref, size in (
        (q_ref, pq_ref, pqr_ref, 128),
        (k_ref, pk_ref, pkr_ref, 256),
    ):

        def chunk(c, carry):
            row = place(pos_ref[c], size)
            row_ref[c] = row
            col_ref[c] = jnp.broadcast_to(row, (8, CHUNK)).T[:, :1]
            return carry

        lax.fori_loop(0, pos_ref.shape[0], chunk, 0)
    token = lax.broadcasted_iota(jnp.int32, mask_ref.shape, 0)
    own_pos = (
        (((token >> log2(share)) * OWN + here_ref[0]) << log2(block_len))
        + here_ref[1] * share
        + (token & (share - 1))
    )
    mask_ref[...] = jnp.max((own_pos == masked_ref[...]).astype(F32), 1, keepdims=True)
    masked_col = jnp.broadcast_to(masked_ref[...], (8, masked_ref.shape[1])).T[:, :1]

    def count(c, carry):
        listed_ref[c] = jnp.sum((slots_ref[c] == masked_col).astype(jnp.int32), 0, keepdims=True)
        return carry

    lax.fori_loop(0, slots_ref.shape[0], count, 0)


def prepare(block_len, heads, here, q_pos, k_pos, slots, masked_row, tokens):
    steps = q_pos.shape[0]
    vmem = pl.BlockSpec(memory_space=pltpu.VMEM)
    col = jax.ShapeDtypeStruct((steps, CHUNK, 1), jnp.int32)
    row = jax.ShapeDtypeStruct((steps, 1, CHUNK), jnp.int32)
    return pl.pallas_call(
        functools.partial(prepare_body, block_len, heads),
        in_specs=[pl.BlockSpec(memory_space=pltpu.SMEM), vmem, vmem, vmem, vmem],
        out_specs=[vmem] * 6,
        out_shape=[
            col,
            col,
            row,
            row,
            jax.ShapeDtypeStruct((tokens, 1), F32),
            jax.ShapeDtypeStruct(slots.shape, jnp.int32),
        ],
        compiler_params=pltpu.CompilerParams(vmem_limit_bytes=VMEM),
        name="prepare",
        cost_estimate=cost(1),
    )(here, q_pos, k_pos, slots, masked_row)


def plus(a, b):
    return (a.astype(F32) + b.astype(F32)).astype(BF)


def project_body(x_ref, w_ref, b_ref, tq_ref, tkv_ref):
    y = (nn(x_ref[...], w_ref[...]) + b_ref[...]).astype(BF)
    for t in range(2):
        for lo in range(4):
            tq_ref[t, :, lo * DH : (lo + 1) * DH] = y[
                lo * 128 : (lo + 1) * 128, t * DH : (t + 1) * DH
            ]
        for lo in range(2):
            tkv_ref[t, :, lo * 128 : (lo + 1) * 128] = y[
                lo * 256 : (lo + 1) * 256, (t + 1) * 128 : (t + 2) * 128
            ]


def project(x_all, w_sel, b_sel):
    blocks = x_all.shape[0] // 512
    width = x_all.shape[1]
    return pl.pallas_call(
        project_body,
        grid=(blocks,),
        in_specs=[
            pl.BlockSpec((512, width), lambda j: (j, 0)),
            pl.BlockSpec((width, 384), lambda j: (0, 0)),
            pl.BlockSpec((1, 384), lambda j: (0, 0)),
        ],
        out_specs=[
            pl.BlockSpec((2, 128, 256), lambda j: (0, j, 0)),
            pl.BlockSpec((2, 256, 256), lambda j: (0, j, 0)),
        ],
        out_shape=[
            jax.ShapeDtypeStruct((2, 1024, 256), BF),
            jax.ShapeDtypeStruct((2, 2048, 256), BF),
        ],
        compiler_params=pltpu.CompilerParams(vmem_limit_bytes=VMEM),
        name="project",
        cost_estimate=cost(1),
    )(x_all, w_sel, b_sel)


def hot_rows(col, count):
    lane = lax.broadcasted_iota(jnp.int32, (1, count), 1).astype(jnp.int16)
    shape = (col.shape[0], count)
    same = jnp.broadcast_to(lane, shape) == jnp.broadcast_to(col.astype(jnp.int16), shape)
    return jnp.where(same, jnp.ones((), BF), jnp.zeros((), BF))


def hot_cols(row, count):
    place = lax.broadcasted_iota(jnp.int32, (count, 1), 0).astype(jnp.int16)
    shape = (count, row.shape[1])
    same = jnp.broadcast_to(place, shape) == jnp.broadcast_to(row.astype(jnp.int16), shape)
    return jnp.where(same, jnp.ones((), BF), jnp.zeros((), BF))


def take_quarter(table, place):
    wide = nn(hot_rows(place & 1023, 1024), table)
    lane = lax.broadcasted_iota(jnp.int32, wide.shape, 1)
    wide = jnp.where((lane >> 6) == (place >> 10), wide, 0.0)
    half = wide[:, :128] + wide[:, 128:]
    return half + pltpu.roll(half, 64, 1)


def take_half(table, place):
    wide = nn(hot_rows(place & 2047, 2048), table)
    return jnp.where((place >> 11) == 1, wide[:, 128:], wide[:, :128])


def spread_quarter(twice, place):
    wide = jnp.concatenate([twice, twice], 1)
    lane = lax.broadcasted_iota(jnp.int32, wide.shape, 1)
    return jnp.where((lane >> 6) == (place >> 10), wide, 0.0).astype(BF)


def spread_half(rows, place):
    upper = (place >> 11) == 1
    return jnp.concatenate(
        [jnp.where(upper, 0.0, rows), jnp.where(upper, rows, 0.0)], 1
    ).astype(BF)


def low_lanes(shape):
    return lax.broadcasted_iota(jnp.int32, shape, 1) < DH


def attend_body(
    pq_ref, pk_ref, pqr_ref, tq_ref, tkv_ref, q_ref, kv_ref, lt_ref, ent_ref, out_ref, acc_ref, got_ref
):
    step = pl.program_id(0)
    place_q = pq_ref[0]
    twice = take_quarter(tq_ref[0], place_q)
    q_all = jnp.where(low_lanes(twice.shape), twice, 0.0).astype(BF)
    kv_all = take_half(tkv_ref[0], pk_ref[0]).astype(BF)
    q_ref[0] = q_all
    kv_ref[0] = kv_all

    def cluster(c, rows):
        kv = kv_ref[0, rows, :]
        scores = nt(q_ref[0, rows, :], kv) * (DH**-0.5)
        top = jnp.max(scores, 1, keepdims=True)
        total = jnp.sum(jnp.exp(scores - top), 1, keepdims=True)
        log_total = top + jnp.log(total)
        soft = jnp.exp(scores - log_total)
        inner = jnp.sum(soft * scores, 1, keepdims=True)
        ent_ref[0, pl.ds(c, 1), :] = jnp.broadcast_to(
            jnp.sum(log_total - inner, 0, keepdims=True) / CLUSTER, (1, 128)
        )
        lt_ref[0, rows, :] = log_total
        got = nn(soft.astype(BF), kv)
        got_ref[rows, :] = jnp.where(low_lanes(got.shape), pltpu.roll(got, 64, 1), got)

    clusters(cluster)
    spread = spread_quarter(got_ref[...], place_q)

    @pl.when((step == 0) | (step == FULL_STEPS))
    def _():
        acc_ref[...] = jnp.zeros(acc_ref.shape, F32)

    acc_ref[...] += nn(hot_cols(pqr_ref[0] & 1023, 1024), spread)

    @pl.when((step == FULL_STEPS - 1) | (step == STEPS - 1))
    def _():
        rows = pl.ds(pl.multiple_of(128 * table_of(step), 128), 128)
        for j in range(out_ref.shape[0]):
            out_ref[j, rows, :] = acc_ref[j * 128 : (j + 1) * 128, :].astype(BF)


def table_of(g):
    return g // FULL_STEPS


def once(*shape):
    return pl.BlockSpec(shape, lambda g: (0,) * len(shape))


def attend(places, tq, tkv):
    pq_col, pk_col, pq_row, _ = places
    chunk = lambda width: pl.BlockSpec((1, CHUNK, width), lambda g: (g, 0, 0))
    table = lambda rows: pl.BlockSpec((1, rows, 256), lambda g: (table_of(g), 0, 0))
    return pl.pallas_call(
        attend_body,
        grid=(STEPS,),
        in_specs=[
            chunk(1),
            chunk(1),
            pl.BlockSpec((1, 1, CHUNK), lambda g: (g, 0, 0)),
            table(1024),
            table(2048),
        ],
        out_specs=[
            chunk(128),
            chunk(128),
            chunk(1),
            pl.BlockSpec((1, 8, 128), lambda g: (g, 0, 0)),
            once(8, 256, 256),
        ],
        out_shape=[
            jax.ShapeDtypeStruct((STEPS, CHUNK, 128), BF),
            jax.ShapeDtypeStruct((STEPS, CHUNK, 128), BF),
            jax.ShapeDtypeStruct((STEPS, CHUNK, 1), F32),
            jax.ShapeDtypeStruct((STEPS, 8, 128), F32),
            jax.ShapeDtypeStruct((8, 256, 256), BF),
        ],
        scratch_shapes=[pltpu.VMEM((1024, 256), F32), pltpu.VMEM((CHUNK, 128), F32)],
        compiler_params=pltpu.CompilerParams(vmem_limit_bytes=VMEM),
        name="attend",
        cost_estimate=cost(1),
    )(pq_col, pk_col, pq_row, tq, tkv)


def attend_back_body(
    pq_ref, pk_ref, pqr_ref, pkr_ref, td_ref, q_ref, kv_ref, lt_ref, out_ref, accq, acckv, d_ref, gq_ref, gkv_ref
):
    step = pl.program_id(0)
    place_q = pq_ref[0]
    twice = take_quarter(td_ref[...], place_q)
    d_ref[...] = jnp.where(low_lanes(twice.shape), 0.0, twice).astype(BF)

    def cluster(c, rows):
        q = q_ref[0, rows, :]
        kv = kv_ref[0, rows, :]
        d = d_ref[rows, :]
        scores = nt(q, kv) * (DH**-0.5)
        soft = jnp.exp(scores - lt_ref[0, rows, :])
        d_soft = nt(d, kv)
        d_scores = soft * (d_soft - jnp.sum(soft * d_soft, 1, keepdims=True))
        d_raw = (d_scores * (DH**-0.5)).astype(BF)
        got = nn(d_raw, kv)
        gq_ref[rows, :] = jnp.where(low_lanes(got.shape), got, pltpu.roll(got, 64, 1))
        gkv_ref[rows, :] = tn(d_raw, q) + tn(soft.astype(BF), d)

    clusters(cluster)

    @pl.when(step == 0)
    def _():
        accq[...] = jnp.zeros(accq.shape, F32)
        acckv[...] = jnp.zeros(acckv.shape, F32)

    accq[...] += nn(hot_cols(pqr_ref[0] & 1023, 1024), spread_quarter(gq_ref[...], place_q))
    acckv[...] += nn(hot_cols(pkr_ref[0] & 2047, 2048), spread_half(gkv_ref[...], pk_ref[0]))

    @pl.when(step == pl.num_programs(0) - 1)
    def _():
        for j in range(out_ref.shape[0]):
            out_ref[j, :128, :] = accq[j * 128 : (j + 1) * 128, :].astype(BF)
            out_ref[j, 128:, :] = acckv[j * 256 : (j + 1) * 256, :].astype(BF)


def attend_back(places, start, steps, td, q_all, kv_all, log_total):
    pq_col, pk_col, pq_row, pk_row = places
    chunk = lambda width: pl.BlockSpec((1, CHUNK, width), lambda g: (g + start, 0, 0))
    col = chunk(1)
    line = pl.BlockSpec((1, 1, CHUNK), lambda g: (g + start, 0, 0))
    return pl.pallas_call(
        attend_back_body,
        grid=(steps,),
        in_specs=[
            col,
            col,
            line,
            line,
            once(1024, 256),
            chunk(128),
            chunk(128),
            chunk(1),
        ],
        out_specs=once(8, 384, 256),
        out_shape=jax.ShapeDtypeStruct((8, 384, 256), BF),
        scratch_shapes=[
            pltpu.VMEM((1024, 256), F32),
            pltpu.VMEM((2048, 256), F32),
            pltpu.VMEM((CHUNK, 128), BF),
            pltpu.VMEM((CHUNK, 128), F32),
            pltpu.VMEM((CHUNK, 128), F32),
        ],
        compiler_params=pltpu.CompilerParams(vmem_limit_bytes=VMEM),
        name="attend_back",
        cost_estimate=cost(1),
    )(pq_col, pk_col, pq_row, pk_row, td, q_all, kv_all, log_total)


def project_grad_body(x_ref, full_ref, half_ref, grad_ref, sum_ref, acc_ref):
    j = pl.program_id(0)
    quarters = []
    for lo in range(4):
        cols = slice(lo * DH, (lo + 1) * DH)
        quarters.append(jnp.concatenate([full_ref[0, :128, cols], half_ref[0, :128, cols]], 1))
    parts = [jnp.concatenate(quarters, 0)]
    for ref in (full_ref, half_ref):
        parts.append(jnp.concatenate([ref[0, 128:, :128], ref[0, 128:, 128:]], 0))
    rows = jnp.concatenate(parts, 1)
    part = tn(x_ref[...], rows)
    sums = jnp.sum(rows.astype(F32), 0, keepdims=True)

    @pl.when(j == 0)
    def _():
        acc_ref[...] = part
        sum_ref[...] = sums

    @pl.when(j > 0)
    def _():
        acc_ref[...] += part
        sum_ref[...] += sums

    @pl.when(j == pl.num_programs(0) - 1)
    def _():
        grad_ref[...] = acc_ref[...].astype(BF)


def project_grad(x_all, full, half):
    tokens, width = x_all.shape
    rows = pl.BlockSpec((1, 384, 256), lambda j: (j, 0, 0))
    return pl.pallas_call(
        project_grad_body,
        grid=(tokens // 512,),
        in_specs=[pl.BlockSpec((512, width), lambda j: (j, 0)), rows, rows],
        out_specs=[once(width, 384), once(1, 384)],
        out_shape=[
            jax.ShapeDtypeStruct((width, 384), BF),
            jax.ShapeDtypeStruct((1, 384), F32),
        ],
        scratch_shapes=[pltpu.VMEM((width, 384), F32)],
        compiler_params=pltpu.CompilerParams(vmem_limit_bytes=VMEM),
        name="project_grad",
        cost_estimate=cost(1),
    )(x_all, full, half)


def project_back_body(heads, full_ref, half_ref, w_ref, dfi_ref, dx_ref, q_ref, kv_ref, wq_ref, wkv_ref):
    for hd in range(heads):
        wq_ref[hd * 3 * DH : (hd + 1) * 3 * DH, :] = w_ref[hd, : 3 * DH, :]
        wkv_ref[hd * 6 * DH : (hd + 1) * 6 * DH, :] = w_ref[hd, 3 * DH :, :]
        for h in range(3):
            if h == 1:
                piece = (half_ref[hd].astype(F32) + half_ref[heads + hd].astype(F32)).astype(BF)
            else:
                piece = full_ref[(h // 2) * heads + hd]
            n = hd * 3 + h
            for lo in range(4):
                q_ref[lo * 128 : (lo + 1) * 128, n * DH : (n + 1) * DH] = piece[
                    :128, lo * DH : (lo + 1) * DH
                ]
            for lo in range(2):
                kv_ref[lo * 256 : (lo + 1) * 256, n * 128 : (n + 1) * 128] = piece[
                    128:, lo * 128 : (lo + 1) * 128
                ]

    def back(cols):
        dx = dfi_ref[:, cols] + nn(q_ref[...], wq_ref[:, cols]) + nn(kv_ref[...], wkv_ref[:, cols])
        dx_ref[:, cols] = dx.astype(BF)

    columns(dx_ref.shape[1], back)


def project_back(full, half, w_all, d_first_in):
    tokens, width = d_first_in.shape
    heads = w_all.shape[0]
    return pl.pallas_call(
        functools.partial(project_back_body, heads),
        out_shape=jax.ShapeDtypeStruct((tokens, width), BF),
        scratch_shapes=[
            pltpu.VMEM((tokens, width), BF),
            pltpu.VMEM((tokens, 2 * width), BF),
            pltpu.VMEM((width, width), BF),
            pltpu.VMEM((2 * width, width), BF),
        ],
        compiler_params=pltpu.CompilerParams(vmem_limit_bytes=VMEM),
        name="project_back",
        cost_estimate=cost(1),
    )(full, half, w_all, d_first_in)


def erf_parts(u):
    bell = jnp.exp2(u * u * (-0.5 * 1.4426950408889634))
    t = 1.0 / (1.0 + (0.3275911 * 0.5**0.5) * jnp.abs(u))
    poly = t * (
        0.127414796
        + t * (-0.142248368 + t * (0.7107068705 + t * (-0.7265760135 + t * 0.5307027145)))
    )
    tail = poly * bell
    return jnp.where(u < 0, tail, 1.0 - tail), bell * ((2 * jnp.pi) ** -0.5)


def row_mean(x):
    return jnp.mean(x, 1, keepdims=True)


def column_sum(x):
    return jnp.sum(x, 0, keepdims=True)


def middle_body(
    heads,
    hc_ref,
    got_ref,
    x_ref,
    dout_ref,
    mask_ref,
    wo_ref,
    up_ref,
    down_ref,
    bias_ref,
    gain_ref,
    shift_ref,
    res_ref,
    send_full_ref,
    send_half_ref,
    dfi_ref,
    down_sent_ref,
    down_kept_ref,
    up_sent_ref,
    up_kept_ref,
    sums_ref,
    gbup_ref,
    rows_ref,
    n1_ref,
    inv1_ref,
    low_ref,
    low_t_ref,
    acc_ref,
    hid_ref,
    slope_ref,
    dlow_ref,
    dlow_t_ref,
    dup_ref,
    rows_back_ref,
    down_buf,
    up_buf,
    side_buf,
    main_sems,
    side_sems,
):
    step = pl.program_id(0)
    tokens, width = x_ref.shape
    hid = up_ref.shape[2]
    size = 64

    def main_copies(c, k, down_to, up_to):
        return [
            pltpu.make_async_copy(buf.at[c], to.at[k, :, pl.ds(0, hid)], main_sems.at[c, i])
            for i, (buf, to) in enumerate(((down_buf, down_to), (up_buf, up_to)))
        ]

    def tiles(body, carry):
        def at(i, carry):
            return body(pl.ds(pl.multiple_of(i * size, size), size), carry)

        return lax.fori_loop(0, tokens // size, at, carry)

    @pl.when(step == 0)
    def _():
        for hd in range(heads):
            rows_ref[:, hd * 256 + 3 * DH : (hd + 1) * 256] = jnp.zeros((tokens, DH), BF)
            for h in range(3):
                if h == 1:
                    piece = plus(got_ref[hd, 128:, :], got_ref[heads + hd, 128:, :])
                else:
                    piece = got_ref[hd + (h // 2) * heads, :128, :]
                col = hd * 256 + h * DH
                for lo in range(4):
                    rows_ref[lo * 128 : (lo + 1) * 128, col : col + DH] = piece[
                        :, lo * DH : (lo + 1) * DH
                    ]

        def project(cols):
            acc_ref[:, cols] = nn(rows_ref[...], wo_ref[:, cols])

        columns(width, project)

        def norm(r, carry):
            v = x_ref[r, :].astype(F32) + acc_ref[r, :] + bias_ref[0:1, :]
            centred = v - row_mean(v)
            inv = lax.rsqrt(row_mean(centred * centred) + EPS)
            normed = centred * inv
            first = normed * gain_ref[0:1, :] + shift_ref[0:1, :]
            n1_ref[r, :] = normed
            inv1_ref[r, :] = inv
            low_ref[r, :] = first.astype(BF)
            acc_ref[r, :] = first + bias_ref[1:2, :]
            return carry

        tiles(norm, 0)
        low_t_ref[...] = low_ref[...].T

    @pl.when(step < heads)
    def _():
        at_bias = pl.multiple_of(chunk_at(step, heads, hc_ref[0]) * 256 + 3 * DH, DH)

        def upper(cols):
            bup = wo_ref[pl.ds(at_bias, 16), cols][:1].astype(F32)
            u = nn(low_ref[...], up_ref[0, :, cols]) + bup
            phi, bell = erf_parts(u)
            hid_ref[step, :, cols] = (u * phi).astype(BF)
            slope_ref[step, :, cols] = phi + u * bell

        for n in range(0, hid, 256):
            upper(slice(n, n + 256))
        acc_ref[...] += nn(hid_ref[step], down_ref[0])

    @pl.when(step == heads)
    def _():
        zero = jnp.zeros((1, width), F32)

        def norm(r, carry):
            g_sum, s_sum, b_sum = carry
            v = acc_ref[r, :]
            centred = v - row_mean(v)
            inv = lax.rsqrt(row_mean(centred * centred) + EPS)
            normed = centred * inv
            res_ref[r, :] = (normed * gain_ref[1:2, :] + shift_ref[1:2, :]).astype(BF)
            seed = dout_ref[r, :].astype(F32) * mask_ref[r, :]
            e = seed * gain_ref[1:2, :]
            d = inv * (e - row_mean(e) - normed * row_mean(e * normed))
            acc_ref[r, :] = d
            dlow_ref[r, :] = d.astype(BF)
            return g_sum + column_sum(seed * normed), s_sum + column_sum(seed), b_sum + column_sum(d)

        g_sum, s_sum, b_sum = tiles(norm, (zero, zero, zero))
        sums_ref[1:2, :] = b_sum
        sums_ref[3:4, :] = g_sum
        sums_ref[5:6, :] = s_sum
        dlow_t_ref[...] = dlow_ref[...].T

    @pl.when(step >= heads)
    def _():
        c = step - heads
        for n in range(0, hid, 256):
            cols = slice(n, n + 256)
            d_up = nt(dlow_ref[...], down_ref[0, cols, :]) * slope_ref[c, :, cols]
            gbup_ref[0, :, cols] = column_sum(d_up)
            dup_ref[:, cols] = d_up.astype(BF)

        acc_ref[...] += nt(dup_ref[...], up_ref[0])

        def products(cols):
            down_buf[c, :, cols] = nn(dlow_t_ref[...], hid_ref[c, :, cols]).astype(BF)
            up_buf[c, :, cols] = nn(low_t_ref[...], dup_ref[:, cols]).astype(BF)

        columns(hid, products)

        @pl.when(c < heads // 2)
        def _():
            for copy in main_copies(c, c, down_sent_ref, up_sent_ref):
                copy.start()

        @pl.when(c >= heads // 2)
        def _():
            for copy in main_copies(c, c - heads // 2, down_kept_ref, up_kept_ref):
                copy.start()

    @pl.when(step == 2 * heads - 1)
    def _():
        zero = jnp.zeros((1, width), F32)

        def norm(r, carry):
            g_sum, s_sum, b_sum = carry
            d_first = acc_ref[r, :]
            normed = n1_ref[r, :]
            e = d_first * gain_ref[0:1, :]
            d = inv1_ref[r, :] * (e - row_mean(e) - normed * row_mean(e * normed))
            dfi_ref[r, :] = d
            dlow_ref[r, :] = d.astype(BF)
            return (
                g_sum + column_sum(d_first * normed),
                s_sum + column_sum(d_first),
                b_sum + column_sum(d),
            )

        g_sum, s_sum, b_sum = tiles(norm, (zero, zero, zero))
        sums_ref[0:1, :] = b_sum
        sums_ref[2:3, :] = g_sum
        sums_ref[4:5, :] = s_sum
        dlow_t_ref[...] = dlow_ref[...].T

        def back(cols):
            rows_back_ref[:, cols] = nt(dlow_ref[...], wo_ref[cols, :]).astype(BF)

        columns(heads * 256, back)
        for lo in range(4):
            for hd in range(heads):
                for h in range(3):
                    col = hd * 256 + h * DH
                    piece = rows_back_ref[lo * 128 : (lo + 1) * 128, col : col + DH]
                    lanes = slice(lo * DH, (lo + 1) * DH)
                    if h == 1:
                        send_half_ref[hd, :, lanes] = piece
                        send_half_ref[heads + hd, :, lanes] = piece
                    else:
                        send_full_ref[hd + (h // 2) * heads, :, lanes] = piece

        def grad(k, carry):
            at = pl.multiple_of(chunk_at(k, heads, hc_ref[0]) * 256, 256)
            whole = nn(dlow_t_ref[...], rows_ref[:, pl.ds(at, 256)]).astype(BF)

            side_buf[k, 0] = whole[:, :SIDE]
            side_buf[k, 1] = whole[:, SIDE:]
            return carry

        lax.fori_loop(0, heads, grad, 0)
        copies = []
        for k in range(heads):
            pairs = heads // 2
            to = (down_sent_ref, up_sent_ref) if k < pairs else (down_kept_ref, up_kept_ref)
            copies += main_copies(k, k % pairs, *to)
            for i in range(2):
                side = pltpu.make_async_copy(
                    side_buf.at[k, i], to[i].at[k % pairs, :, pl.ds(hid, SIDE)], side_sems.at[k, i]
                )
                side.start()
                copies.append(side)
        for copy in copies:
            copy.wait()


def chunk_at(k, heads, hc):
    pairs = heads // 2
    return jnp.where(k < pairs, 2 * k + 1 - hc, 2 * (k - pairs) + hc)


def middle(hc, got, x_own, d_own, mask_col, wo, ff_all, bias, gain, shift):
    heads, width, hid = ff_all.shape[0], ff_all.shape[2], ff_all.shape[1] - ff_all.shape[2]
    pairs = heads // 2
    tokens = x_own.shape[0]

    def at(k, hc_ref):
        return chunk_at(k, heads, hc_ref[0])

    once = lambda *shape: pl.BlockSpec(shape, lambda g, c: (0,) * len(shape))
    by_chunk = lambda part, *shape: pl.BlockSpec(shape, lambda g, c: (at(g % heads, c), part, 0))
    late = lambda *shape: pl.BlockSpec(shape, lambda g, c: (at(jnp.maximum(g - heads, 0), c), 0, 0))
    grads = pl.BlockSpec(memory_space=pl.ANY)
    big = jax.ShapeDtypeStruct((pairs, width, hid + SIDE), BF)
    table = jax.ShapeDtypeStruct((OWN * heads, 128, 256), BF)
    return pl.pallas_call(
        functools.partial(middle_body, heads),
        grid_spec=pltpu.PrefetchScalarGridSpec(
            num_scalar_prefetch=1,
            grid=(2 * heads,),
            in_specs=[
                once(OWN * heads, 256, 256),
                once(tokens, width),
                once(tokens, width),
                once(tokens, 1),
                once(heads * 256, width),
                by_chunk(0, 1, width, hid),
                by_chunk(1, 1, hid, width),
                once(2, width),
                once(2, width),
                once(2, width),
            ],
            out_specs=[
                once(tokens, width),
                once(OWN * heads, 128, 256),
                once(OWN * heads, 128, 256),
                once(tokens, width),
                grads,
                grads,
                grads,
                grads,
                once(8, width),
                late(1, 1, hid),
            ],
            scratch_shapes=[
                pltpu.VMEM((tokens, heads * 256), BF),
                pltpu.VMEM((tokens, width), F32),
                pltpu.VMEM((tokens, 1), F32),
                pltpu.VMEM((tokens, width), BF),
                pltpu.VMEM((width, tokens), BF),
                pltpu.VMEM((tokens, width), F32),
                pltpu.VMEM((heads, tokens, hid), BF),
                pltpu.VMEM((heads, tokens, hid), F32),
                pltpu.VMEM((tokens, width), BF),
                pltpu.VMEM((width, tokens), BF),
                pltpu.VMEM((tokens, hid), BF),
                pltpu.VMEM((tokens, heads * 256), BF),
                pltpu.VMEM((heads, width, hid), BF),
                pltpu.VMEM((heads, width, hid), BF),
                pltpu.VMEM((heads, 2, width, SIDE), BF),
                pltpu.SemaphoreType.DMA((heads, 2)),
                pltpu.SemaphoreType.DMA((heads, 2)),
            ],
        ),
        out_shape=[
            jax.ShapeDtypeStruct((tokens, width), BF),
            table,
            table,
            jax.ShapeDtypeStruct((tokens, width), F32),
            big,
            big,
            big,
            big,
            jax.ShapeDtypeStruct((8, width), F32),
            jax.ShapeDtypeStruct((heads, 1, hid), F32),
        ],
        compiler_params=pltpu.CompilerParams(vmem_limit_bytes=VMEM),
        name="middle",
        cost_estimate=cost(1),
    )(hc, got, x_own, d_own, mask_col, wo, ff_all, ff_all, bias, gain, shift)


def swap(x, axis, bit=1):
    size = lax.axis_size(axis)
    return lax.ppermute(x, axis, [(i, i ^ bit) for i in range(size)])


def pick(x, index, axis=0):
    return lax.dynamic_index_in_dim(x, index, axis, keepdims=False)


def fold(kept, came, index, axis):
    return tuple(plus(pick(kept, i, axis), pick(came, i, axis)) for i in (1 - index, index))


def total(pieces):
    return sum(p.astype(F32) for p in pieces)


barrier = lax.optimization_barrier


def per_device(
    inputs,
    w_qkv,
    b_qv,
    w_out,
    out_bias,
    w_up,
    b_up,
    w_down,
    norm_gain,
    norm_shift,
    d_out,
    q_perm,
    k_perm,
    masked,
):
    seqs, block_len, width = inputs.shape
    heads = lax.axis_size("hx") * lax.axis_size("hc")
    plane = OWN * heads
    share = block_len // heads
    tokens = seqs * share
    length = lax.axis_size("sq") * OWN
    sq = lax.axis_index("sq")
    own = lax.axis_index("own")
    hx = lax.axis_index("hx")
    hc = lax.axis_index("hc")
    head = hx * lax.axis_size("hc") + hc
    head_cols = q_perm.shape[1] * DH

    pad = jnp.zeros((256 - head_cols - 1, width), BF)
    with_bias = jnp.concatenate([w_out, b_up[None], pad], 0)
    mine = lax.dynamic_slice_in_dim(inputs, head * share, share, 1)
    x_own = lax.all_to_all(mine, "sq", 0, 0, tiled=True).reshape(tokens, width)
    out_bias_all = lax.all_gather(with_bias, HEAD, axis=0, tiled=False)
    x_own, out_bias_all, d_out, q_perm, k_perm, w_qkv = barrier(
        (x_own, out_bias_all, d_out, q_perm, k_perm, w_qkv)
    )
    x_all = lax.all_gather(x_own, PLANE, axis=0, tiled=True)
    d_own = lax.all_to_all(d_out, "sq", 0, 0, tiled=True).reshape(tokens, width)

    def positions(perm):
        mine = pick(perm, sq)
        full = pick(mine, 2 * own).reshape(2, TOK_DEV)
        half = lax.dynamic_slice_in_dim(mine[1], own * TOK_DEV, TOK_DEV, 0)
        return jnp.concatenate([full, half[None]], 0).reshape(-1, 1, CHUNK)

    masked_row = pick(masked, sq)
    *places, mask_col, listed = prepare(
        block_len,
        heads,
        jnp.stack([own, head]).astype(jnp.int32),
        positions(q_perm),
        positions(k_perm),
        lax.dynamic_slice_in_dim(pick(q_perm, sq), own * TOK_DEV, TOK_DEV, 1).reshape(-1, 1, CHUNK),
        masked_row[None],
        tokens,
    )

    def two_heads(x):
        full = lax.dynamic_slice_in_dim(x, own * 2 * DH, DH, x.ndim - 1)
        return full, x[..., DH : 2 * DH]

    w_full, w_half = two_heads(w_qkv)
    w_sel = jnp.concatenate(
        [w_full[0], w_half[0], w_full[1], w_full[2], w_half[1], w_half[2]], 1
    )
    b_full, b_half = two_heads(b_qv.astype(F32))
    none = jnp.zeros((DH,), F32)
    b_sel = jnp.concatenate([b_full[0], b_half[0], none, b_full[1], none, b_half[1]])[None]
    w_rows = jnp.concatenate(
        [w_qkv[0]]
        + [w_qkv[i, :, h * DH : (h + 1) * DH] for h in range(3) for i in (1, 2)],
        1,
    ).T
    ff = jnp.concatenate([w_up, w_down], 0)

    occupancy = jnp.sum(listed.reshape(q_perm.shape[1], TOK_DEV // CLUSTER, CLUSTER), -1)
    bias = out_bias.astype(F32)
    out_all = out_bias_all.reshape(heads * 256, width)

    (
        x_all,
        d_own,
        places,
        w_sel,
        b_sel,
        w_rows,
        mask_col,
        occupancy,
        bias,
        out_all,
        ff,
    ) = barrier(
        (
            x_all,
            d_own,
            places,
            w_sel,
            b_sel,
            w_rows,
            mask_col,
            occupancy,
            bias,
            out_all,
            ff,
        )
    )
    ff_all = lax.all_gather(ff, HEAD, axis=0, tiled=False)

    tq, tkv = project(x_all, w_sel, b_sel)
    *kept, ent, done = attend(places, tq, tkv)
    got = lax.all_to_all(done, PLANE, 0, 0, tiled=True)
    ent_seg = ent[:, :GROUPS, 0].reshape(3, TOK_DEV // CLUSTER)
    ent_got = swap(jnp.where(own == 0, ent_seg[1], ent_seg[0]), "own")
    ff_all, w_rows, got = barrier((ff_all, w_rows, got))
    w_all = lax.all_gather(w_rows, HEAD, axis=0, tiled=False)
    (
        result_own,
        send_full,
        send_half,
        d_first_in,
        down_sent,
        down_kept,
        up_sent,
        up_kept,
        sums_own,
        grad_bup,
    ) = middle(
        hc[None],
        got,
        x_own,
        d_own,
        mask_col,
        out_all,
        ff_all,
        bias,
        norm_gain,
        norm_shift,
    )
    rows = width // length
    near = seqs <= 4

    def shifted(pieces):
        return [pieces[0]] + [
            lax.ppermute(p, "sq", [(i, (i + s) % seqs) for i in range(seqs)])
            for s, p in enumerate(pieces)
            if s > 0
        ]

    def cut_z(x):
        return [pick(x, (sq + s) % seqs) for s in range(seqs)] if near else [x]

    def over_z(pieces):
        if near:
            return shifted(pieces)
        return list(lax.all_to_all(pieces[0], "sq", 0, 0, tiled=True))

    td_full = lax.all_to_all(send_full, PLANE, 0, 0, tiled=True)
    down_came, up_came = swap(down_sent, "hc"), swap(up_sent, "hc")
    result_own = cut_z(result_own.reshape(seqs, share, width))
    cut = lambda x: x.reshape(x.shape[0], length // OWN, OWN, rows, x.shape[-1])
    down_sent, down_kept = fold(cut(down_kept), cut(down_came), hx, 0)
    up_sent, up_kept = fold(cut(up_kept), cut(up_came), own, 2)
    (
        td_full,
        send_half,
        ent_got,
        w_all,
        down_sent,
        down_kept,
        up_sent,
        up_kept,
        result_own,
    ) = barrier(
        (
            td_full,
            send_half,
            ent_got,
            w_all,
            down_sent,
            down_kept,
            up_sent,
            up_kept,
            result_own,
        )
    )
    td_half = lax.all_to_all(send_half, PLANE, 0, 0, tiled=True)
    down_came, up_came = swap(down_sent, "hx"), swap(up_sent, "own")
    result_got = over_z(result_own)
    rows_full = attend_back(places, 0, FULL_STEPS, td_full.reshape(plane * 128, 256), *kept)
    rows_full, td_half, down_came, up_came, result_got = barrier(
        (rows_full, td_half, down_came, up_came, result_got)
    )
    back_full = lax.all_to_all(rows_full, PLANE, 0, 0, tiled=True)
    down_sent, down_kept = fold(down_kept, down_came, own, 1)
    up_sent, up_kept = fold(up_kept, up_came, hx, 0)
    td_half, down_sent, down_kept, up_sent, up_kept = barrier(
        (td_half, down_sent, down_kept, up_sent, up_kept)
    )
    down_came, up_came = swap(down_sent, "own"), swap(up_sent, "hx")
    rows_half = attend_back(
        places, FULL_STEPS, STEPS - FULL_STEPS, td_half.reshape(plane * 128, 256), *kept
    )
    rows_half, back_full = barrier((rows_half, back_full))
    back_half = lax.all_to_all(rows_half, PLANE, 0, 0, tiled=True)
    rows_half, down_came, up_came = barrier((rows_half, down_came, up_came))
    both = cut_z(jnp.concatenate([plus(down_kept, down_came), plus(up_kept, up_came)], 2))
    rows_full, rows_half, both = barrier((rows_full, rows_half, both))
    both_got = over_z(both)
    grad_sel, sum_sel = project_grad(x_all, rows_full, rows_half)

    sums = sum_sel.reshape(6, DH)
    at_full = (jnp.arange(3) == 2 * own)[:, None]
    at_half = (jnp.arange(3) == 1)[:, None]
    at_head = (jnp.arange(heads) == head)[None, :, None, None]
    pair = jnp.stack(
        [jnp.where(at_full, sums[a], 0.0) + jnp.where(at_half, sums[b], 0.0) for a, b in ((0, 1), (3, 5))]
    )
    bqv = jnp.where(at_head, pair[:, None], 0.0)
    small = jnp.concatenate([sums_own[:6].reshape(-1), grad_bup.reshape(-1), bqv.reshape(-1)])
    grad_sel = grad_sel.reshape(length // OWN, OWN, rows, 384)
    grad_sent, grad_kept = pick(grad_sel, 1 - own, 1), pick(grad_sel, own, 1)
    grad_came = swap(grad_sent, "own")
    back_half, grad_came = barrier((back_half, grad_came))
    low = jnp.where(own == 0, grad_kept, grad_came)
    high = jnp.where(own == 0, grad_came, grad_kept)
    shared = plus(grad_kept, grad_came)
    order = [(low, 0), (shared, 1), (high, 0), (low, 2), (shared, 4), (high, 2), (low, 3), (shared, 5), (high, 3)]
    grad_all = cut_z(jnp.concatenate([a[..., c * DH : (c + 1) * DH] for a, c in order], -1))
    back_full, grad_all = barrier((back_full, grad_all))
    grad_got = over_z(grad_all)
    d_in_own = project_back(back_full, back_half, w_all, d_first_in)
    d_in_own, small = barrier((d_in_own, small))
    for axis in ("hc", "hx", "own"):
        small = small + swap(small, axis)
    bit = 1
    while bit < seqs:
        small = small + swap(small, "sq", bit)
        bit *= 2
    d_inputs = lax.all_to_all(
        d_in_own.reshape(seqs, share, width), "sq", 0, 0, tiled=True
    ).astype(F32)
    both = total(both_got)
    wide = both.shape[1] // 2
    down_sum = both[:, : wide - SIDE]
    up_sum = both[:, wide : 2 * wide - SIDE]
    out_sum = jnp.concatenate([both[:, wide - SIDE : wide], both[:, 2 * wide - SIDE :]], 1)[:, :head_cols]
    qkv_sum = total(grad_got).reshape(rows, 3, head_cols).transpose(1, 0, 2)
    if near:
        parts = []
        for i in range(seqs):
            part = result_got[0]
            for s in range(1, seqs):
                part = jnp.where((i + s) % seqs == sq, result_got[s], part)
            parts.append(part)
        result = jnp.stack(parts)
    else:
        result = jnp.stack(result_got)

    obias_sum = small[: 2 * width].reshape(2, width)
    gain_sum = small[2 * width : 4 * width].reshape(2, width)
    shift_sum = small[4 * width : 6 * width].reshape(2, width)
    bup_sum = small[6 * width : -2 * width]
    bqv_sum = small[-2 * width :].reshape(2, width)

    entropy = jnp.stack(
        [
            jnp.where(own == 0, ent_seg[0], ent_got),
            ent_seg[2],
            jnp.where(own == 0, ent_got, ent_seg[1]),
        ]
    )
    return (
        result.astype(F32),
        d_inputs,
        qkv_sum,
        bqv_sum,
        out_sum.T,
        obias_sum,
        up_sum,
        bup_sum,
        down_sum.T,
        gain_sum,
        shift_sum,
        entropy,
        occupancy,
    )


def solution(mesh):
    seq, head = (mesh.shape["seq"], mesh.shape["head"])
    fine = Mesh(
        mesh.devices.reshape(seq // OWN, OWN, 2, head // 2), ("sq", "own", "hx", "hc")
    )
    both = SEQ + HEAD
    placed = (
        P(None, SEQ, None),
        P(None, None, HEAD),
        P(None, HEAD),
        P(HEAD, None),
        P(),
        P(None, HEAD),
        P(HEAD),
        P(HEAD, None),
        P(),
        P(),
        P(None, both, None),
        P(None, HEAD, None),
        P(None, HEAD, None),
        P(),
    )
    return jax.shard_map(
        per_device,
        mesh=fine,
        in_specs=placed,
        out_specs=(
            P(None, both, None),
            P(None, both, None),
            P(None, SEQ, HEAD),
            P(),
            P(HEAD, SEQ),
            P(),
            P(SEQ, HEAD),
            P(),
            P(HEAD, SEQ),
            P(),
            P(),
            P(HEAD, SEQ),
            P(HEAD, SEQ),
        ),
        check_vma=False,
    )
```

```python
import functools

import jax
import jax.numpy as jnp
from jax import lax
from jax.experimental import pallas as pl
from jax.experimental.pallas import tpu as pltpu
from jax.sharding import Mesh
from jax.sharding import PartitionSpec as P

DH = 64
FF = 3072
CLUSTER = 128
LENGTH = 4096
TOK_DEV = 2048
OWN = LENGTH // TOK_DEV
EPS = 1e-06
PLANE = ("own", "hx", "hc")
HEAD = ("hx", "hc")
SEQ = ("sq", "own")
CHUNK = 512
STEPS = 3 * TOK_DEV // CHUNK
FULL_STEPS = 2 * TOK_DEV // CHUNK
GROUPS = CHUNK // CLUSTER
BF = jnp.bfloat16
F32 = jnp.float32
VMEM = 56 * 1024 * 1024
SIDE = 128


def cost(micros):
    return pl.CostEstimate(flops=micros * 10**9, transcendentals=0, bytes_accessed=micros * 10**6)


def nn(a, b):
    return lax.dot_general(a, b, (((1,), (0,)), ((), ())), preferred_element_type=F32)


def nt(a, b):
    return lax.dot_general(a, b, (((1,), (1,)), ((), ())), preferred_element_type=F32)


def tn(a, b):
    return lax.dot_general(a, b, (((0,), (0,)), ((), ())), preferred_element_type=F32)


def columns(count, body):
    def at(n, carry):
        body(pl.ds(pl.multiple_of(n * 256, 256), 256))
        return carry

    lax.fori_loop(0, count // 256, at, 0)


def clusters(body):
    def at(pair, carry):
        for j in range(2):
            c = 2 * pair + j
            body(c, pl.ds(pl.multiple_of(c * CLUSTER, CLUSTER), CLUSTER))
        return carry

    lax.fori_loop(0, GROUPS // 2, at, 0)


def log2(n):
    return n.bit_length() - 1


def prepare_body(
    block_len,
    heads,
    here_ref,
    q_ref,
    k_ref,
    slots_ref,
    masked_ref,
    pq_ref,
    pk_ref,
    pqr_ref,
    pkr_ref,
    mask_ref,
    listed_ref,
):
    share = block_len // heads

    def place(pos, size):
        block = pos >> log2(block_len)
        rest = pos & (block_len - 1)
        device = (block & (OWN - 1)) * heads + (rest >> log2(share))
        token = (block >> log2(OWN)) * share + (rest & (share - 1))
        return ((token >> log2(size)) << log2(size * OWN * heads)) + device * size + (token & (size - 1))

    for pos_ref, col_ref, row_ref, size in (
        (q_ref, pq_ref, pqr_ref, 128),
        (k_ref, pk_ref, pkr_ref, 256),
    ):

        def chunk(c, carry):
            row = place(pos_ref[c], size)
            row_ref[c] = row
            col_ref[c] = jnp.broadcast_to(row, (8, CHUNK)).T[:, :1]
            return carry

        lax.fori_loop(0, pos_ref.shape[0], chunk, 0)
    token = lax.broadcasted_iota(jnp.int32, mask_ref.shape, 0)
    own_pos = (
        (((token >> log2(share)) * OWN + here_ref[0]) << log2(block_len))
        + here_ref[1] * share
        + (token & (share - 1))
    )
    mask_ref[...] = jnp.max((own_pos == masked_ref[...]).astype(F32), 1, keepdims=True)
    masked_col = jnp.broadcast_to(masked_ref[...], (8, masked_ref.shape[1])).T[:, :1]

    def count(c, carry):
        listed_ref[c] = jnp.sum((slots_ref[c] == masked_col).astype(jnp.int32), 0, keepdims=True)
        return carry

    lax.fori_loop(0, slots_ref.shape[0], count, 0)


def prepare(block_len, heads, here, q_pos, k_pos, slots, masked_row, tokens):
    steps = q_pos.shape[0]
    vmem = pl.BlockSpec(memory_space=pltpu.VMEM)
    col = jax.ShapeDtypeStruct((steps, CHUNK, 1), jnp.int32)
    row = jax.ShapeDtypeStruct((steps, 1, CHUNK), jnp.int32)
    return pl.pallas_call(
        functools.partial(prepare_body, block_len, heads),
        in_specs=[pl.BlockSpec(memory_space=pltpu.SMEM), vmem, vmem, vmem, vmem],
        out_specs=[vmem] * 6,
        out_shape=[
            col,
            col,
            row,
            row,
            jax.ShapeDtypeStruct((tokens, 1), F32),
            jax.ShapeDtypeStruct(slots.shape, jnp.int32),
        ],
        compiler_params=pltpu.CompilerParams(vmem_limit_bytes=VMEM),
        name="prepare",
        cost_estimate=cost(1),
    )(here, q_pos, k_pos, slots, masked_row)


def plus(a, b):
    return (a.astype(F32) + b.astype(F32)).astype(BF)


def project_body(x_ref, w_ref, b_ref, tq_ref, tkv_ref):
    y = (nn(x_ref[...], w_ref[...]) + b_ref[...]).astype(BF)
    for t in range(2):
        for lo in range(4):
            tq_ref[t, :, lo * DH : (lo + 1) * DH] = y[
                lo * 128 : (lo + 1) * 128, t * DH : (t + 1) * DH
            ]
        for lo in range(2):
            tkv_ref[t, :, lo * 128 : (lo + 1) * 128] = y[
                lo * 256 : (lo + 1) * 256, (t + 1) * 128 : (t + 2) * 128
            ]


def project(x_all, w_sel, b_sel):
    blocks = x_all.shape[0] // 512
    width = x_all.shape[1]
    return pl.pallas_call(
        project_body,
        grid=(blocks,),
        in_specs=[
            pl.BlockSpec((512, width), lambda j: (j, 0)),
            pl.BlockSpec((width, 384), lambda j: (0, 0)),
            pl.BlockSpec((1, 384), lambda j: (0, 0)),
        ],
        out_specs=[
            pl.BlockSpec((2, 128, 256), lambda j: (0, j, 0)),
            pl.BlockSpec((2, 256, 256), lambda j: (0, j, 0)),
        ],
        out_shape=[
            jax.ShapeDtypeStruct((2, 1024, 256), BF),
            jax.ShapeDtypeStruct((2, 2048, 256), BF),
        ],
        compiler_params=pltpu.CompilerParams(vmem_limit_bytes=VMEM),
        name="project",
        cost_estimate=cost(1),
    )(x_all, w_sel, b_sel)


def hot_rows(col, count):
    lane = lax.broadcasted_iota(jnp.int32, (1, count), 1).astype(jnp.int16)
    shape = (col.shape[0], count)
    same = jnp.broadcast_to(lane, shape) == jnp.broadcast_to(col.astype(jnp.int16), shape)
    return jnp.where(same, jnp.ones((), BF), jnp.zeros((), BF))


def hot_cols(row, count):
    place = lax.broadcasted_iota(jnp.int32, (count, 1), 0).astype(jnp.int16)
    shape = (count, row.shape[1])
    same = jnp.broadcast_to(place, shape) == jnp.broadcast_to(row.astype(jnp.int16), shape)
    return jnp.where(same, jnp.ones((), BF), jnp.zeros((), BF))


def take_quarter(table, place):
    wide = nn(hot_rows(place & 1023, 1024), table)
    lane = lax.broadcasted_iota(jnp.int32, wide.shape, 1)
    wide = jnp.where((lane >> 6) == (place >> 10), wide, 0.0)
    half = wide[:, :128] + wide[:, 128:]
    return half + pltpu.roll(half, 64, 1)


def take_half(table, place):
    wide = nn(hot_rows(place & 2047, 2048), table)
    return jnp.where((place >> 11) == 1, wide[:, 128:], wide[:, :128])


def spread_quarter(twice, place):
    wide = jnp.concatenate([twice, twice], 1)
    lane = lax.broadcasted_iota(jnp.int32, wide.shape, 1)
    return jnp.where((lane >> 6) == (place >> 10), wide, 0.0).astype(BF)


def spread_half(rows, place):
    upper = (place >> 11) == 1
    return jnp.concatenate(
        [jnp.where(upper, 0.0, rows), jnp.where(upper, rows, 0.0)], 1
    ).astype(BF)


def low_lanes(shape):
    return lax.broadcasted_iota(jnp.int32, shape, 1) < DH


def attend_body(
    pq_ref, pk_ref, pqr_ref, tq_ref, tkv_ref, q_ref, kv_ref, lt_ref, ent_ref, out_ref, acc_ref, got_ref
):
    step = pl.program_id(0)
    place_q = pq_ref[0]
    twice = take_quarter(tq_ref[0], place_q)
    q_all = jnp.where(low_lanes(twice.shape), twice, 0.0).astype(BF)
    kv_all = take_half(tkv_ref[0], pk_ref[0]).astype(BF)
    q_ref[0] = q_all
    kv_ref[0] = kv_all

    def cluster(c, rows):
        kv = kv_ref[0, rows, :]
        scores = nt(q_ref[0, rows, :], kv) * (DH**-0.5)
        top = jnp.max(scores, 1, keepdims=True)
        total = jnp.sum(jnp.exp(scores - top), 1, keepdims=True)
        log_total = top + jnp.log(total)
        soft = jnp.exp(scores - log_total)
        inner = jnp.sum(soft * scores, 1, keepdims=True)
        ent_ref[0, pl.ds(c, 1), :] = jnp.broadcast_to(
            jnp.sum(log_total - inner, 0, keepdims=True) / CLUSTER, (1, 128)
        )
        lt_ref[0, rows, :] = log_total
        got = nn(soft.astype(BF), kv)
        got_ref[rows, :] = jnp.where(low_lanes(got.shape), pltpu.roll(got, 64, 1), got)

    clusters(cluster)
    spread = spread_quarter(got_ref[...], place_q)

    @pl.when((step == 0) | (step == FULL_STEPS))
    def _():
        acc_ref[...] = jnp.zeros(acc_ref.shape, F32)

    acc_ref[...] += nn(hot_cols(pqr_ref[0] & 1023, 1024), spread)

    @pl.when((step == FULL_STEPS - 1) | (step == STEPS - 1))
    def _():
        rows = pl.ds(pl.multiple_of(128 * table_of(step), 128), 128)
        for j in range(out_ref.shape[0]):
            out_ref[j, rows, :] = acc_ref[j * 128 : (j + 1) * 128, :].astype(BF)


def table_of(g):
    return g // FULL_STEPS


def once(*shape):
    return pl.BlockSpec(shape, lambda g: (0,) * len(shape))


def attend(places, tq, tkv):
    pq_col, pk_col, pq_row, _ = places
    chunk = lambda width: pl.BlockSpec((1, CHUNK, width), lambda g: (g, 0, 0))
    table = lambda rows: pl.BlockSpec((1, rows, 256), lambda g: (table_of(g), 0, 0))
    return pl.pallas_call(
        attend_body,
        grid=(STEPS,),
        in_specs=[
            chunk(1),
            chunk(1),
            pl.BlockSpec((1, 1, CHUNK), lambda g: (g, 0, 0)),
            table(1024),
            table(2048),
        ],
        out_specs=[
            chunk(128),
            chunk(128),
            chunk(1),
            pl.BlockSpec((1, 8, 128), lambda g: (g, 0, 0)),
            once(8, 256, 256),
        ],
        out_shape=[
            jax.ShapeDtypeStruct((STEPS, CHUNK, 128), BF),
            jax.ShapeDtypeStruct((STEPS, CHUNK, 128), BF),
            jax.ShapeDtypeStruct((STEPS, CHUNK, 1), F32),
            jax.ShapeDtypeStruct((STEPS, 8, 128), F32),
            jax.ShapeDtypeStruct((8, 256, 256), BF),
        ],
        scratch_shapes=[pltpu.VMEM((1024, 256), F32), pltpu.VMEM((CHUNK, 128), F32)],
        compiler_params=pltpu.CompilerParams(vmem_limit_bytes=VMEM),
        name="attend",
        cost_estimate=cost(1),
    )(pq_col, pk_col, pq_row, tq, tkv)


def attend_back_body(
    pq_ref, pk_ref, pqr_ref, pkr_ref, td_ref, q_ref, kv_ref, lt_ref, out_ref, accq, acckv, d_ref, gq_ref, gkv_ref
):
    step = pl.program_id(0)
    place_q = pq_ref[0]
    twice = take_quarter(td_ref[...], place_q)
    d_ref[...] = jnp.where(low_lanes(twice.shape), 0.0, twice).astype(BF)

    def cluster(c, rows):
        q = q_ref[0, rows, :]
        kv = kv_ref[0, rows, :]
        d = d_ref[rows, :]
        scores = nt(q, kv) * (DH**-0.5)
        soft = jnp.exp(scores - lt_ref[0, rows, :])
        d_soft = nt(d, kv)
        d_scores = soft * (d_soft - jnp.sum(soft * d_soft, 1, keepdims=True))
        d_raw = (d_scores * (DH**-0.5)).astype(BF)
        got = nn(d_raw, kv)
        gq_ref[rows, :] = jnp.where(low_lanes(got.shape), got, pltpu.roll(got, 64, 1))
        gkv_ref[rows, :] = tn(d_raw, q) + tn(soft.astype(BF), d)

    clusters(cluster)

    @pl.when(step == 0)
    def _():
        accq[...] = jnp.zeros(accq.shape, F32)
        acckv[...] = jnp.zeros(acckv.shape, F32)

    accq[...] += nn(hot_cols(pqr_ref[0] & 1023, 1024), spread_quarter(gq_ref[...], place_q))
    acckv[...] += nn(hot_cols(pkr_ref[0] & 2047, 2048), spread_half(gkv_ref[...], pk_ref[0]))

    @pl.when(step == pl.num_programs(0) - 1)
    def _():
        for j in range(out_ref.shape[0]):
            out_ref[j, :128, :] = accq[j * 128 : (j + 1) * 128, :].astype(BF)
            out_ref[j, 128:, :] = acckv[j * 256 : (j + 1) * 256, :].astype(BF)


def attend_back(places, start, steps, td, q_all, kv_all, log_total):
    pq_col, pk_col, pq_row, pk_row = places
    chunk = lambda width: pl.BlockSpec((1, CHUNK, width), lambda g: (g + start, 0, 0))
    col = chunk(1)
    line = pl.BlockSpec((1, 1, CHUNK), lambda g: (g + start, 0, 0))
    return pl.pallas_call(
        attend_back_body,
        grid=(steps,),
        in_specs=[
            col,
            col,
            line,
            line,
            once(1024, 256),
            chunk(128),
            chunk(128),
            chunk(1),
        ],
        out_specs=once(8, 384, 256),
        out_shape=jax.ShapeDtypeStruct((8, 384, 256), BF),
        scratch_shapes=[
            pltpu.VMEM((1024, 256), F32),
            pltpu.VMEM((2048, 256), F32),
            pltpu.VMEM((CHUNK, 128), BF),
            pltpu.VMEM((CHUNK, 128), F32),
            pltpu.VMEM((CHUNK, 128), F32),
        ],
        compiler_params=pltpu.CompilerParams(vmem_limit_bytes=VMEM),
        name="attend_back",
        cost_estimate=cost(1),
    )(pq_col, pk_col, pq_row, pk_row, td, q_all, kv_all, log_total)


def project_grad_body(x_ref, full_ref, half_ref, grad_ref, sum_ref, acc_ref):
    j = pl.program_id(0)
    quarters = []
    for lo in range(4):
        cols = slice(lo * DH, (lo + 1) * DH)
        quarters.append(jnp.concatenate([full_ref[0, :128, cols], half_ref[0, :128, cols]], 1))
    parts = [jnp.concatenate(quarters, 0)]
    for ref in (full_ref, half_ref):
        parts.append(jnp.concatenate([ref[0, 128:, :128], ref[0, 128:, 128:]], 0))
    rows = jnp.concatenate(parts, 1)
    part = tn(x_ref[...], rows)
    sums = jnp.sum(rows.astype(F32), 0, keepdims=True)

    @pl.when(j == 0)
    def _():
        acc_ref[...] = part
        sum_ref[...] = sums

    @pl.when(j > 0)
    def _():
        acc_ref[...] += part
        sum_ref[...] += sums

    @pl.when(j == pl.num_programs(0) - 1)
    def _():
        grad_ref[...] = acc_ref[...].astype(BF)


def project_grad(x_all, full, half):
    tokens, width = x_all.shape
    rows = pl.BlockSpec((1, 384, 256), lambda j: (j, 0, 0))
    return pl.pallas_call(
        project_grad_body,
        grid=(tokens // 512,),
        in_specs=[pl.BlockSpec((512, width), lambda j: (j, 0)), rows, rows],
        out_specs=[once(width, 384), once(1, 384)],
        out_shape=[
            jax.ShapeDtypeStruct((width, 384), BF),
            jax.ShapeDtypeStruct((1, 384), F32),
        ],
        scratch_shapes=[pltpu.VMEM((width, 384), F32)],
        compiler_params=pltpu.CompilerParams(vmem_limit_bytes=VMEM),
        name="project_grad",
        cost_estimate=cost(1),
    )(x_all, full, half)


def project_back_body(heads, full_ref, half_ref, w_ref, dfi_ref, dx_ref, q_ref, kv_ref, wq_ref, wkv_ref):
    for hd in range(heads):
        wq_ref[hd * 3 * DH : (hd + 1) * 3 * DH, :] = w_ref[hd, : 3 * DH, :]
        wkv_ref[hd * 6 * DH : (hd + 1) * 6 * DH, :] = w_ref[hd, 3 * DH :, :]
        for h in range(3):
            if h == 1:
                piece = (half_ref[hd].astype(F32) + half_ref[heads + hd].astype(F32)).astype(BF)
            else:
                piece = full_ref[(h // 2) * heads + hd]
            n = hd * 3 + h
            for lo in range(4):
                q_ref[lo * 128 : (lo + 1) * 128, n * DH : (n + 1) * DH] = piece[
                    :128, lo * DH : (lo + 1) * DH
                ]
            for lo in range(2):
                kv_ref[lo * 256 : (lo + 1) * 256, n * 128 : (n + 1) * 128] = piece[
                    128:, lo * 128 : (lo + 1) * 128
                ]

    def back(cols):
        dx = dfi_ref[:, cols] + nn(q_ref[...], wq_ref[:, cols]) + nn(kv_ref[...], wkv_ref[:, cols])
        dx_ref[:, cols] = dx.astype(BF)

    for n in range(0, dx_ref.shape[1], 256):
        back(slice(n, n + 256))


def project_back(full, half, w_all, d_first_in):
    tokens, width = d_first_in.shape
    heads = w_all.shape[0]
    return pl.pallas_call(
        functools.partial(project_back_body, heads),
        out_shape=jax.ShapeDtypeStruct((tokens, width), BF),
        scratch_shapes=[
            pltpu.VMEM((tokens, width), BF),
            pltpu.VMEM((tokens, 2 * width), BF),
            pltpu.VMEM((width, width), BF),
            pltpu.VMEM((2 * width, width), BF),
        ],
        compiler_params=pltpu.CompilerParams(vmem_limit_bytes=VMEM),
        name="project_back",
        cost_estimate=cost(1),
    )(full, half, w_all, d_first_in)


def erf_parts(u):
    bell = jnp.exp2(u * u * (-0.5 * 1.4426950408889634))
    t = 1.0 / (1.0 + (0.3275911 * 0.5**0.5) * jnp.abs(u))
    poly = t * (
        0.127414796
        + t * (-0.142248368 + t * (0.7107068705 + t * (-0.7265760135 + t * 0.5307027145)))
    )
    tail = poly * bell
    return jnp.where(u < 0, tail, 1.0 - tail), bell * ((2 * jnp.pi) ** -0.5)


def row_mean(x):
    return jnp.mean(x, 1, keepdims=True)


def column_sum(x):
    return jnp.sum(x, 0, keepdims=True)


def middle_body(
    heads,
    hc_ref,
    got_ref,
    x_ref,
    dout_ref,
    mask_ref,
    wo_ref,
    up_ref,
    down_ref,
    bias_ref,
    gain_ref,
    shift_ref,
    res_ref,
    send_full_ref,
    send_half_ref,
    dfi_ref,
    down_sent_ref,
    down_kept_ref,
    up_sent_ref,
    up_kept_ref,
    sums_ref,
    gbup_ref,
    rows_ref,
    n1_ref,
    inv1_ref,
    low_ref,
    low_t_ref,
    acc_ref,
    hid_ref,
    slope_ref,
    dlow_ref,
    dlow_t_ref,
    dup_ref,
    rows_back_ref,
    down_buf,
    up_buf,
    side_buf,
    main_sems,
    side_sems,
):
    step = pl.program_id(0)
    tokens, width = x_ref.shape
    hid = up_ref.shape[2]
    size = 64

    def main_copies(c, k, down_to, up_to):
        return [
            pltpu.make_async_copy(buf.at[c], to.at[k, :, pl.ds(0, hid)], main_sems.at[c, i])
            for i, (buf, to) in enumerate(((down_buf, down_to), (up_buf, up_to)))
        ]

    def tiles(body, carry):
        def at(i, carry):
            return body(pl.ds(pl.multiple_of(i * size, size), size), carry)

        return lax.fori_loop(0, tokens // size, at, carry)

    @pl.when(step == 0)
    def _():
        for hd in range(heads):
            rows_ref[:, hd * 256 + 3 * DH : (hd + 1) * 256] = jnp.zeros((tokens, DH), BF)
            for h in range(3):
                if h == 1:
                    piece = plus(got_ref[hd, 128:, :], got_ref[heads + hd, 128:, :])
                else:
                    piece = got_ref[hd + (h // 2) * heads, :128, :]
                col = hd * 256 + h * DH
                for lo in range(4):
                    rows_ref[lo * 128 : (lo + 1) * 128, col : col + DH] = piece[
                        :, lo * DH : (lo + 1) * DH
                    ]

        def project(cols):
            acc_ref[:, cols] = nn(rows_ref[...], wo_ref[:, cols])

        columns(width, project)

        def norm(r, carry):
            v = x_ref[r, :].astype(F32) + acc_ref[r, :] + bias_ref[0:1, :]
            centred = v - row_mean(v)
            inv = lax.rsqrt(row_mean(centred * centred) + EPS)
            normed = centred * inv
            first = normed * gain_ref[0:1, :] + shift_ref[0:1, :]
            n1_ref[r, :] = normed
            inv1_ref[r, :] = inv
            low_ref[r, :] = first.astype(BF)
            acc_ref[r, :] = first + bias_ref[1:2, :]
            return carry

        tiles(norm, 0)
        low_t_ref[...] = low_ref[...].T

    @pl.when(step < heads)
    def _():
        at_bias = pl.multiple_of(chunk_at(step, heads, hc_ref[0]) * 256 + 3 * DH, DH)

        def upper(cols):
            bup = wo_ref[pl.ds(at_bias, 16), cols][:1].astype(F32)
            u = nn(low_ref[...], up_ref[0, :, cols]) + bup
            phi, bell = erf_parts(u)
            hid_ref[step, :, cols] = (u * phi).astype(BF)
            slope_ref[step, :, cols] = phi + u * bell

        for n in range(0, hid, 256):
            upper(slice(n, n + 256))
        acc_ref[...] += nn(hid_ref[step], down_ref[0])

    @pl.when(step == heads)
    def _():
        zero = jnp.zeros((1, width), F32)

        def norm(r, carry):
            g_sum, s_sum, b_sum = carry
            v = acc_ref[r, :]
            centred = v - row_mean(v)
            inv = lax.rsqrt(row_mean(centred * centred) + EPS)
            normed = centred * inv
            res_ref[r, :] = (normed * gain_ref[1:2, :] + shift_ref[1:2, :]).astype(BF)
            seed = dout_ref[r, :].astype(F32) * mask_ref[r, :]
            e = seed * gain_ref[1:2, :]
            d = inv * (e - row_mean(e) - normed * row_mean(e * normed))
            acc_ref[r, :] = d
            dlow_ref[r, :] = d.astype(BF)
            return g_sum + column_sum(seed * normed), s_sum + column_sum(seed), b_sum + column_sum(d)

        g_sum, s_sum, b_sum = tiles(norm, (zero, zero, zero))
        sums_ref[1:2, :] = b_sum
        sums_ref[3:4, :] = g_sum
        sums_ref[5:6, :] = s_sum
        dlow_t_ref[...] = dlow_ref[...].T

    @pl.when(step >= heads)
    def _():
        c = step - heads
        for n in range(0, hid, 256):
            cols = slice(n, n + 256)
            d_up = nt(dlow_ref[...], down_ref[0, cols, :]) * slope_ref[c, :, cols]
            gbup_ref[0, :, cols] = column_sum(d_up)
            dup_ref[:, cols] = d_up.astype(BF)

        acc_ref[...] += nt(dup_ref[...], up_ref[0])

        def products(cols):
            down_buf[c, :, cols] = nn(dlow_t_ref[...], hid_ref[c, :, cols]).astype(BF)
            up_buf[c, :, cols] = nn(low_t_ref[...], dup_ref[:, cols]).astype(BF)

        columns(hid, products)

        @pl.when(c < heads // 2)
        def _():
            for copy in main_copies(c, c, down_sent_ref, up_sent_ref):
                copy.start()

        @pl.when(c >= heads // 2)
        def _():
            for copy in main_copies(c, c - heads // 2, down_kept_ref, up_kept_ref):
                copy.start()

    @pl.when(step == 2 * heads - 1)
    def _():
        zero = jnp.zeros((1, width), F32)

        def norm(r, carry):
            g_sum, s_sum, b_sum = carry
            d_first = acc_ref[r, :]
            normed = n1_ref[r, :]
            e = d_first * gain_ref[0:1, :]
            d = inv1_ref[r, :] * (e - row_mean(e) - normed * row_mean(e * normed))
            dfi_ref[r, :] = d
            dlow_ref[r, :] = d.astype(BF)
            return (
                g_sum + column_sum(d_first * normed),
                s_sum + column_sum(d_first),
                b_sum + column_sum(d),
            )

        g_sum, s_sum, b_sum = tiles(norm, (zero, zero, zero))
        sums_ref[0:1, :] = b_sum
        sums_ref[2:3, :] = g_sum
        sums_ref[4:5, :] = s_sum
        dlow_t_ref[...] = dlow_ref[...].T

        def back(cols):
            rows_back_ref[:, cols] = nt(dlow_ref[...], wo_ref[cols, :]).astype(BF)

        columns(heads * 256, back)
        for lo in range(4):
            for hd in range(heads):
                for h in range(3):
                    col = hd * 256 + h * DH
                    piece = rows_back_ref[lo * 128 : (lo + 1) * 128, col : col + DH]
                    lanes = slice(lo * DH, (lo + 1) * DH)
                    if h == 1:
                        send_half_ref[hd, :, lanes] = piece
                        send_half_ref[heads + hd, :, lanes] = piece
                    else:
                        send_full_ref[hd + (h // 2) * heads, :, lanes] = piece

        def grad(k, carry):
            at = pl.multiple_of(chunk_at(k, heads, hc_ref[0]) * 256, 256)
            whole = nn(dlow_t_ref[...], rows_ref[:, pl.ds(at, 256)]).astype(BF)

            side_buf[k, 0] = whole[:, :SIDE]
            side_buf[k, 1] = whole[:, SIDE:]
            return carry

        lax.fori_loop(0, heads, grad, 0)
        copies = []
        for k in range(heads):
            pairs = heads // 2
            to = (down_sent_ref, up_sent_ref) if k < pairs else (down_kept_ref, up_kept_ref)
            copies += main_copies(k, k % pairs, *to)
            for i in range(2):
                side = pltpu.make_async_copy(
                    side_buf.at[k, i], to[i].at[k % pairs, :, pl.ds(hid, SIDE)], side_sems.at[k, i]
                )
                side.start()
                copies.append(side)
        for copy in copies:
            copy.wait()


def chunk_at(k, heads, hc):
    pairs = heads // 2
    return jnp.where(k < pairs, 2 * k + 1 - hc, 2 * (k - pairs) + hc)


def middle(hc, got, x_own, d_own, mask_col, wo, ff_all, bias, gain, shift):
    heads, width, hid = ff_all.shape[0], ff_all.shape[2], ff_all.shape[1] - ff_all.shape[2]
    pairs = heads // 2
    tokens = x_own.shape[0]

    def at(k, hc_ref):
        return chunk_at(k, heads, hc_ref[0])

    once = lambda *shape: pl.BlockSpec(shape, lambda g, c: (0,) * len(shape))
    by_chunk = lambda part, *shape: pl.BlockSpec(shape, lambda g, c: (at(g % heads, c), part, 0))
    late = lambda *shape: pl.BlockSpec(shape, lambda g, c: (at(jnp.maximum(g - heads, 0), c), 0, 0))
    grads = pl.BlockSpec(memory_space=pl.ANY)
    big = jax.ShapeDtypeStruct((pairs, width, hid + SIDE), BF)
    table = jax.ShapeDtypeStruct((OWN * heads, 128, 256), BF)
    return pl.pallas_call(
        functools.partial(middle_body, heads),
        grid_spec=pltpu.PrefetchScalarGridSpec(
            num_scalar_prefetch=1,
            grid=(2 * heads,),
            in_specs=[
                once(OWN * heads, 256, 256),
                once(tokens, width),
                once(tokens, width),
                once(tokens, 1),
                once(heads * 256, width),
                by_chunk(0, 1, width, hid),
                by_chunk(1, 1, hid, width),
                once(2, width),
                once(2, width),
                once(2, width),
            ],
            out_specs=[
                once(tokens, width),
                once(OWN * heads, 128, 256),
                once(OWN * heads, 128, 256),
                once(tokens, width),
                grads,
                grads,
                grads,
                grads,
                once(8, width),
                late(1, 1, hid),
            ],
            scratch_shapes=[
                pltpu.VMEM((tokens, heads * 256), BF),
                pltpu.VMEM((tokens, width), F32),
                pltpu.VMEM((tokens, 1), F32),
                pltpu.VMEM((tokens, width), BF),
                pltpu.VMEM((width, tokens), BF),
                pltpu.VMEM((tokens, width), F32),
                pltpu.VMEM((heads, tokens, hid), BF),
                pltpu.VMEM((heads, tokens, hid), F32),
                pltpu.VMEM((tokens, width), BF),
                pltpu.VMEM((width, tokens), BF),
                pltpu.VMEM((tokens, hid), BF),
                pltpu.VMEM((tokens, heads * 256), BF),
                pltpu.VMEM((heads, width, hid), BF),
                pltpu.VMEM((heads, width, hid), BF),
                pltpu.VMEM((heads, 2, width, SIDE), BF),
                pltpu.SemaphoreType.DMA((heads, 2)),
                pltpu.SemaphoreType.DMA((heads, 2)),
            ],
        ),
        out_shape=[
            jax.ShapeDtypeStruct((tokens, width), BF),
            table,
            table,
            jax.ShapeDtypeStruct((tokens, width), F32),
            big,
            big,
            big,
            big,
            jax.ShapeDtypeStruct((8, width), F32),
            jax.ShapeDtypeStruct((heads, 1, hid), F32),
        ],
        compiler_params=pltpu.CompilerParams(vmem_limit_bytes=VMEM),
        name="middle",
        cost_estimate=cost(1),
    )(hc, got, x_own, d_own, mask_col, wo, ff_all, ff_all, bias, gain, shift)


def swap(x, axis, bit=1):
    size = lax.axis_size(axis)
    return lax.ppermute(x, axis, [(i, i ^ bit) for i in range(size)])


def pick(x, index, axis=0):
    return lax.dynamic_index_in_dim(x, index, axis, keepdims=False)


def fold(kept, came, index, axis):
    return tuple(plus(pick(kept, i, axis), pick(came, i, axis)) for i in (1 - index, index))


def total(pieces):
    return sum(p.astype(F32) for p in pieces)


barrier = lax.optimization_barrier


def per_device(
    inputs,
    w_qkv,
    b_qv,
    w_out,
    out_bias,
    w_up,
    b_up,
    w_down,
    norm_gain,
    norm_shift,
    d_out,
    q_perm,
    k_perm,
    masked,
):
    seqs, block_len, width = inputs.shape
    heads = lax.axis_size("hx") * lax.axis_size("hc")
    plane = OWN * heads
    share = block_len // heads
    tokens = seqs * share
    length = lax.axis_size("sq") * OWN
    sq = lax.axis_index("sq")
    own = lax.axis_index("own")
    hx = lax.axis_index("hx")
    hc = lax.axis_index("hc")
    head = hx * lax.axis_size("hc") + hc
    head_cols = q_perm.shape[1] * DH

    pad = jnp.zeros((256 - head_cols - 1, width), BF)
    with_bias = jnp.concatenate([w_out, b_up[None], pad], 0)
    mine = lax.dynamic_slice_in_dim(inputs, head * share, share, 1)
    x_own = lax.all_to_all(mine, "sq", 0, 0, tiled=True).reshape(tokens, width)
    out_bias_all = lax.all_gather(with_bias, HEAD, axis=0, tiled=False)
    x_own, out_bias_all, d_out, q_perm, k_perm, w_qkv = barrier(
        (x_own, out_bias_all, d_out, q_perm, k_perm, w_qkv)
    )
    x_all = lax.all_gather(x_own, PLANE, axis=0, tiled=True)
    d_own = lax.all_to_all(d_out, "sq", 0, 0, tiled=True).reshape(tokens, width)

    def positions(perm):
        mine = pick(perm, sq)
        full = pick(mine, 2 * own).reshape(2, TOK_DEV)
        half = lax.dynamic_slice_in_dim(mine[1], own * TOK_DEV, TOK_DEV, 0)
        return jnp.concatenate([full, half[None]], 0).reshape(-1, 1, CHUNK)

    masked_row = pick(masked, sq)
    *places, mask_col, listed = prepare(
        block_len,
        heads,
        jnp.stack([own, head]).astype(jnp.int32),
        positions(q_perm),
        positions(k_perm),
        lax.dynamic_slice_in_dim(pick(q_perm, sq), own * TOK_DEV, TOK_DEV, 1).reshape(-1, 1, CHUNK),
        masked_row[None],
        tokens,
    )

    def two_heads(x):
        full = lax.dynamic_slice_in_dim(x, own * 2 * DH, DH, x.ndim - 1)
        return full, x[..., DH : 2 * DH]

    w_full, w_half = two_heads(w_qkv)
    w_sel = jnp.concatenate(
        [w_full[0], w_half[0], w_full[1], w_full[2], w_half[1], w_half[2]], 1
    )
    b_full, b_half = two_heads(b_qv.astype(F32))
    none = jnp.zeros((DH,), F32)
    b_sel = jnp.concatenate([b_full[0], b_half[0], none, b_full[1], none, b_half[1]])[None]
    w_rows = jnp.concatenate(
        [w_qkv[0]]
        + [w_qkv[i, :, h * DH : (h + 1) * DH] for h in range(3) for i in (1, 2)],
        1,
    ).T
    ff = jnp.concatenate([w_up, w_down], 0)

    occupancy = jnp.sum(listed.reshape(q_perm.shape[1], TOK_DEV // CLUSTER, CLUSTER), -1)
    bias = out_bias.astype(F32)
    out_all = out_bias_all.reshape(heads * 256, width)

    (
        x_all,
        d_own,
        places,
        w_sel,
        b_sel,
        w_rows,
        mask_col,
        occupancy,
        bias,
        out_all,
        ff,
    ) = barrier(
        (
            x_all,
            d_own,
            places,
            w_sel,
            b_sel,
            w_rows,
            mask_col,
            occupancy,
            bias,
            out_all,
            ff,
        )
    )
    ff_all = lax.all_gather(ff, HEAD, axis=0, tiled=False)

    tq, tkv = project(x_all, w_sel, b_sel)
    *kept, ent, done = attend(places, tq, tkv)
    got = lax.all_to_all(done, PLANE, 0, 0, tiled=True)
    ent_seg = ent[:, :GROUPS, 0].reshape(3, TOK_DEV // CLUSTER)
    ent_got = swap(jnp.where(own == 0, ent_seg[1], ent_seg[0]), "own")
    ff_all, w_rows, got = barrier((ff_all, w_rows, got))
    w_all = lax.all_gather(w_rows, HEAD, axis=0, tiled=False)
    (
        result_own,
        send_full,
        send_half,
        d_first_in,
        down_sent,
        down_kept,
        up_sent,
        up_kept,
        sums_own,
        grad_bup,
    ) = middle(
        hc[None],
        got,
        x_own,
        d_own,
        mask_col,
        out_all,
        ff_all,
        bias,
        norm_gain,
        norm_shift,
    )
    rows = width // length
    near = seqs <= 4

    def shifted(pieces):
        return [pieces[0]] + [
            lax.ppermute(p, "sq", [(i, (i + s) % seqs) for i in range(seqs)])
            for s, p in enumerate(pieces)
            if s > 0
        ]

    def cut_z(x):
        return [pick(x, (sq + s) % seqs) for s in range(seqs)] if near else [x]

    def over_z(pieces):
        if near:
            return shifted(pieces)
        return list(lax.all_to_all(pieces[0], "sq", 0, 0, tiled=True))

    td_full = lax.all_to_all(send_full, PLANE, 0, 0, tiled=True)
    down_came, up_came = swap(down_sent, "hc"), swap(up_sent, "hc")
    result_own = cut_z(result_own.reshape(seqs, share, width))
    cut = lambda x: x.reshape(x.shape[0], length // OWN, OWN, rows, x.shape[-1])
    down_sent, down_kept = fold(cut(down_kept), cut(down_came), hx, 0)
    up_sent, up_kept = fold(cut(up_kept), cut(up_came), own, 2)
    (
        td_full,
        send_half,
        ent_got,
        w_all,
        down_sent,
        down_kept,
        up_sent,
        up_kept,
        result_own,
    ) = barrier(
        (
            td_full,
            send_half,
            ent_got,
            w_all,
            down_sent,
            down_kept,
            up_sent,
            up_kept,
            result_own,
        )
    )
    td_half = lax.all_to_all(send_half, PLANE, 0, 0, tiled=True)
    down_came, up_came = swap(down_sent, "hx"), swap(up_sent, "own")
    result_got = over_z(result_own)
    rows_full = attend_back(places, 0, FULL_STEPS, td_full.reshape(plane * 128, 256), *kept)
    rows_full, td_half, down_came, up_came, result_got = barrier(
        (rows_full, td_half, down_came, up_came, result_got)
    )
    back_full = lax.all_to_all(rows_full, PLANE, 0, 0, tiled=True)
    down_sent, down_kept = fold(down_kept, down_came, own, 1)
    up_sent, up_kept = fold(up_kept, up_came, hx, 0)
    td_half, down_sent, down_kept, up_sent, up_kept = barrier(
        (td_half, down_sent, down_kept, up_sent, up_kept)
    )
    down_came, up_came = swap(down_sent, "own"), swap(up_sent, "hx")
    rows_half = attend_back(
        places, FULL_STEPS, STEPS - FULL_STEPS, td_half.reshape(plane * 128, 256), *kept
    )
    rows_half, back_full = barrier((rows_half, back_full))
    back_half = lax.all_to_all(rows_half, PLANE, 0, 0, tiled=True)
    rows_half, down_came, up_came = barrier((rows_half, down_came, up_came))
    both = cut_z(jnp.concatenate([plus(down_kept, down_came), plus(up_kept, up_came)], 2))
    rows_full, rows_half, both = barrier((rows_full, rows_half, both))
    both_got = over_z(both)
    grad_sel, sum_sel = project_grad(x_all, rows_full, rows_half)

    sums = sum_sel.reshape(6, DH)
    at_full = (jnp.arange(3) == 2 * own)[:, None]
    at_half = (jnp.arange(3) == 1)[:, None]
    at_head = (jnp.arange(heads) == head)[None, :, None, None]
    pair = jnp.stack(
        [jnp.where(at_full, sums[a], 0.0) + jnp.where(at_half, sums[b], 0.0) for a, b in ((0, 1), (3, 5))]
    )
    bqv = jnp.where(at_head, pair[:, None], 0.0)
    small = jnp.concatenate([sums_own[:6].reshape(-1), grad_bup.reshape(-1), bqv.reshape(-1)])
    grad_sel = grad_sel.reshape(length // OWN, OWN, rows, 384)
    grad_sent, grad_kept = pick(grad_sel, 1 - own, 1), pick(grad_sel, own, 1)
    grad_came = swap(grad_sent, "own")
    back_half, grad_came = barrier((back_half, grad_came))
    low = jnp.where(own == 0, grad_kept, grad_came)
    high = jnp.where(own == 0, grad_came, grad_kept)
    shared = plus(grad_kept, grad_came)
    order = [(low, 0), (shared, 1), (high, 0), (low, 2), (shared, 4), (high, 2), (low, 3), (shared, 5), (high, 3)]
    grad_all = cut_z(jnp.concatenate([a[..., c * DH : (c + 1) * DH] for a, c in order], -1))
    back_full, grad_all = barrier((back_full, grad_all))
    grad_got = over_z(grad_all)
    d_in_own = project_back(back_full, back_half, w_all, d_first_in)
    d_in_own, small = barrier((d_in_own, small))
    for axis in ("hc", "hx", "own"):
        small = small + swap(small, axis)
    bit = 1
    while bit < seqs:
        small = small + swap(small, "sq", bit)
        bit *= 2
    d_inputs = lax.all_to_all(
        d_in_own.reshape(seqs, share, width), "sq", 0, 0, tiled=True
    ).astype(F32)
    both = total(both_got)
    wide = both.shape[1] // 2
    down_sum = both[:, : wide - SIDE]
    up_sum = both[:, wide : 2 * wide - SIDE]
    out_sum = jnp.concatenate([both[:, wide - SIDE : wide], both[:, 2 * wide - SIDE :]], 1)[:, :head_cols]
    qkv_sum = total(grad_got).reshape(rows, 3, head_cols).transpose(1, 0, 2)
    if near:
        parts = []
        for i in range(seqs):
            part = result_got[0]
            for s in range(1, seqs):
                part = jnp.where((i + s) % seqs == sq, result_got[s], part)
            parts.append(part)
        result = jnp.stack(parts)
    else:
        result = jnp.stack(result_got)

    obias_sum = small[: 2 * width].reshape(2, width)
    gain_sum = small[2 * width : 4 * width].reshape(2, width)
    shift_sum = small[4 * width : 6 * width].reshape(2, width)
    bup_sum = small[6 * width : -2 * width]
    bqv_sum = small[-2 * width :].reshape(2, width)

    entropy = jnp.stack(
        [
            jnp.where(own == 0, ent_seg[0], ent_got),
            ent_seg[2],
            jnp.where(own == 0, ent_got, ent_seg[1]),
        ]
    )
    return (
        result.astype(F32),
        d_inputs,
        qkv_sum,
        bqv_sum,
        out_sum.T,
        obias_sum,
        up_sum,
        bup_sum,
        down_sum.T,
        gain_sum,
        shift_sum,
        entropy,
        occupancy,
    )


def solution(mesh):
    seq, head = (mesh.shape["seq"], mesh.shape["head"])
    fine = Mesh(
        mesh.devices.reshape(seq // OWN, OWN, 2, head // 2), ("sq", "own", "hx", "hc")
    )
    both = SEQ + HEAD
    placed = (
        P(None, SEQ, None),
        P(None, None, HEAD),
        P(None, HEAD),
        P(HEAD, None),
        P(),
        P(None, HEAD),
        P(HEAD),
        P(HEAD, None),
        P(),
        P(),
        P(None, both, None),
        P(None, HEAD, None),
        P(None, HEAD, None),
        P(),
    )
    return jax.shard_map(
        per_device,
        mesh=fine,
        in_specs=placed,
        out_specs=(
            P(None, both, None),
            P(None, both, None),
            P(None, SEQ, HEAD),
            P(),
            P(HEAD, SEQ),
            P(),
            P(SEQ, HEAD),
            P(),
            P(HEAD, SEQ),
            P(),
            P(),
            P(HEAD, SEQ),
            P(HEAD, SEQ),
        ),
        check_vma=False,
    )
```
